32 devices in a mesh: ctx: 8 (over y, x, core), grp: 4 (over z).
Axes of the slice: x: 2, y: 2, z: 4, core: 2. Of those that a mesh axis runs over, the one named last changes fastest.
Arguments:
- query_in: bfloat16 [8192, 4096], P('ctx', 'grp'), may hold values from -6 to 6
- key_in: bfloat16 [8192, 4096], P('ctx', 'grp'), may hold values from -6 to 6
- value_in: bfloat16 [8192, 4096], P('ctx', 'grp'), may hold values from -6 to 6
- residues: float32 [256, 16], P('grp'), may hold values from -1.5 to 1.5
- decay_time: float32 [256, 16], P('grp'), may hold values from 20 to 32768
- skip_gain: float32 [4096], P('grp'), may hold values from 0.5 to 1.5
- out_proj: bfloat16 [4096, 4096], P('ctx', 'grp'), may hold values from -0.09375 to 0.09375
- doc_lengths: int32 [4], replicated, may hold values from 1 to 4096, 8192 in all
- grad_out: bfloat16 [8192, 4096], P('ctx', 'grp'), may hold values from -6 to 6
Outputs:
- mixed_out: bfloat16 [8192, 4096], P('ctx', 'grp')
- grad_query: bfloat16 [8192, 4096], P('ctx', 'grp')
- grad_key: bfloat16 [8192, 4096], P('ctx', 'grp')
- grad_value: bfloat16 [8192, 4096], P('ctx', 'grp')
- grad_proj: float32 [4096, 4096], P('ctx', 'grp')
The draws below stay inside these ranges and needn't reach their ends.
Inputs may be any that keep to these rules, and one draw needn't show every extreme that they name: `doc_lengths`: document lengths in window order, summing to 8192; the longest is exactly 4096.
All inputs are finite; a program needn't handle non-finite values.
Results may differ from the reference program's by a relative error of at most 0.013.
Values may be sent and summed in bfloat16 or wider, within the bound.
A program may use at most 192 MiB of HBM per device.

```python
import math
import jax
import jax.numpy as jnp
import numpy as np
from jax import lax

D = 4096
GROUP = 16
ORDER = 16
NDOCS = 4
GROUPS = 256
TOKENS = 8192
N_GRP = 4


def level_of(rng, dims, split, low, top_value):
    loudness = 1.0
    for position, parts in split:
        draws = jax.random.uniform(jax.random.fold_in(jax.random.fold_in(rng, 6), position), (parts,), jnp.float32, low / len(split), top_value / len(split))
        loudness = loudness * jnp.repeat(jnp.exp(draws), dims[position] // parts).reshape((-1,) + (1,) * (len(dims) - 1 - position))
    return loudness


def profile(count, total, limit, lean):
    portions = [(1 << 20) // math.isqrt(rank ** lean) + 1 for rank in range(2, count + 1)]
    rest, given = total - limit - (count - 1), [1] * (count - 1)
    while rest > 0:
        free = [i for i in range(count - 1) if given[i] < limit]
        mass, left = sum([portions[i] for i in free]), rest
        for i in free:
            more = min(limit - given[i], max(1, left * portions[i] // mass), rest)
            given[i] = given[i] + more
            rest = rest - more
    return np.array([limit] + given)


def uneven_parts(own_key, number_of, total, bound, skew):
    if number_of == 2:
        one = jax.random.randint(own_key, (), max(1, total - bound), min(bound, total - 1) + 1)
        return jnp.stack([one, total - one])
    lengths = jnp.asarray(profile(number_of, total, bound, skew), jnp.int32)
    couples = (number_of - 1) // 2
    giver, sink = lengths[1:1 + 2 * couples:2], lengths[2:2 + 2 * couples:2]
    margin = jnp.minimum(giver - 1, bound - sink)
    moved = jax.random.randint(jax.random.fold_in(own_key, 1), (couples,), 0, 1 << 20) % (margin + 1)
    lengths = lengths.at[1:1 + 2 * couples:2].set(giver - moved).at[2:2 + 2 * couples:2].set(sink + moved)
    return lengths[jax.random.permutation(jax.random.fold_in(own_key, 2), number_of)]


def gaussian(rng, shape, scale, bound, cuts=(), kind=jnp.bfloat16):
    factor_of = level_of(rng, shape, cuts, -0.22, 0.18) if cuts else 1.0
    values = jax.random.normal(rng, shape, jnp.float32) * scale * factor_of
    return jnp.minimum(jnp.maximum(values, -bound), bound).astype(kind)


def setup_inputs(seed: int = 0) -> dict:
    splits = jax.random.split(jax.random.key(seed), 10)
    query_in = gaussian(splits[0], (TOKENS, D), 1.0, 6.0, ((0, 8), (1, 4)))
    key_in = gaussian(splits[1], (TOKENS, D), 1.0, 6.0, ((0, 8), (1, 4)))
    value_in = gaussian(splits[2], (TOKENS, D), 1.0, 6.0, ((0, 8), (1, 4)))
    residues = gaussian(splits[3], (GROUPS, ORDER), ORDER ** -0.5, 1.5, ((0, 4),), jnp.float32)
    decay_time = jnp.clip(jnp.exp(math.log(32768.0) - 7.4014754 * jax.random.uniform(splits[4], (GROUPS, ORDER), jnp.float32) ** level_of(splits[4], (GROUPS, ORDER), ((0, 4),), -0.2, 0.2)), 20.0, 32768.0)
    skip_gain = jnp.clip(0.5 + 1.0 * jax.random.uniform(splits[5], (D,), jnp.float32) ** level_of(splits[5], (D,), ((0, 4),), -0.2, 0.2), 0.5, 1.5)
    out_proj = gaussian(splits[6], (D, D), D ** -0.5, 0.09375, ((0, 8), (1, 4)))
    doc_lengths = uneven_parts(splits[7], NDOCS, TOKENS, TOKENS // 2, 2).astype(jnp.int32)
    grad_out = gaussian(splits[8], (TOKENS, D), 1.0, 6.0, ((0, 8), (1, 4)))
    return {"query_in": query_in, "key_in": key_in, "value_in": value_in, "residues": residues, "decay_time": decay_time, "skip_gain": skip_gain, "out_proj": out_proj, "doc_lengths": doc_lengths, "grad_out": grad_out}


def doc_index(doc_lengths, amount):
    starts = jnp.cumsum(doc_lengths) - doc_lengths
    where_now = jnp.arange(amount, dtype=jnp.int32)
    return lax.optimization_barrier(jnp.sum((starts[None, :] <= where_now[:, None]).astype(jnp.int32), axis=1)) - 1

def reference(query_in, key_in, value_in, residues, decay_time, skip_gain, out_proj, doc_lengths, grad_out):
    decay_factor = jnp.exp(-1.0 / decay_time)
    residue_scaled = residues * jnp.sqrt(-jnp.expm1(-2.0 / decay_time))
    factor_chan = jnp.repeat(decay_factor, GROUP, axis=0)
    scaled_chan = jnp.repeat(residue_scaled, GROUP, axis=0)
    doc_ids = doc_index(doc_lengths, TOKENS)
    prior_ids = jnp.concatenate([jnp.array([-1], jnp.int32), doc_ids[:-1]])
    resets = doc_ids != prior_ids
    query_f = query_in.astype(jnp.float32)
    key_f = key_in.astype(jnp.float32)
    value_f = value_in.astype(jnp.float32)
    product = (key_f * value_f).astype(jnp.bfloat16)
    product_f = product.astype(jnp.float32)

    def forward_step(state, item):
        line, fresh = item
        state = jnp.where(fresh, 0.0, factor_chan * state) + line[:, None]
        return (state, lax.optimization_barrier(jnp.sum(scaled_chan * state, axis=1)))
    _, convolved = lax.scan(forward_step, jnp.zeros((D, ORDER), jnp.float32), (product_f, resets))
    filtered = convolved + skip_gain * product_f
    gated = (query_f * filtered).astype(jnp.bfloat16)
    width = D // N_GRP
    running = jnp.zeros((TOKENS, D), jnp.float32)
    for number in range(N_GRP):
        partial_value = jnp.dot(gated[:, number * width:(number + 1) * width], out_proj[:, number * width:(number + 1) * width].T, preferred_element_type=jnp.float32)
        running = running + lax.optimization_barrier(partial_value.astype(jnp.bfloat16)).astype(jnp.float32)
    mixed_out = running.astype(jnp.bfloat16)
    grad_gated = jnp.dot(grad_out, out_proj, preferred_element_type=jnp.float32)
    grad_query = (grad_gated * filtered).astype(jnp.bfloat16)
    grad_filtered = grad_gated * query_f
    resets_next = jnp.concatenate([resets[1:], jnp.array([True])])

    def backward_step(carry, item):
        line, cut = item
        carry = scaled_chan * line[:, None] + jnp.where(cut, 0.0, factor_chan * carry)
        return (carry, lax.optimization_barrier(jnp.sum(carry, axis=1)))
    _, returned = lax.scan(backward_step, jnp.zeros((D, ORDER), jnp.float32), (grad_filtered, resets_next), reverse=True)
    grad_product = returned + skip_gain * grad_filtered
    grad_key = (grad_product * value_f).astype(jnp.bfloat16)
    grad_value = (grad_product * key_f).astype(jnp.bfloat16)
    grad_proj = jnp.dot(grad_out.T, gated, preferred_element_type=jnp.float32)
    return (mixed_out, grad_query, grad_key, grad_value, grad_proj)
```

```python
import functools

import jax
import jax.numpy as jnp
from jax import lax
from jax.experimental import pallas as pl
from jax.experimental.pallas import tpu as pltpu
from jax.sharding import PartitionSpec as P

LANES = 128
BLOCK = 128
F32 = jnp.float32
BF16 = jnp.bfloat16


def doc_index(starts, where_now):
    return jnp.sum((starts[None, :] <= where_now[:, None]).astype(jnp.int32), axis=1) - 1


def pick(stacked, count, rows, members):
    lane_filter = lax.broadcasted_iota(jnp.int32, (rows, LANES), 1) // members
    out = stacked[:rows]
    for g in range(1, count):
        out = jnp.where(lane_filter == g, stacked[g * rows:(g + 1) * rows], out)
    return out


def summary_kernel(count, poles, members, a_ref, b_ref, leave_ref, out_ref):
    line = (a_ref[...].astype(F32) * b_ref[...].astype(F32)).astype(BF16)
    stacked = jnp.dot(leave_ref[...], line, preferred_element_type=F32)
    out_ref[...] = pick(stacked, count, poles, members).astype(out_ref.dtype)


def summarize(a, b, leave, poles, members):
    rows, channels = a.shape
    count = LANES // members
    return pl.pallas_call(
        functools.partial(summary_kernel, count, poles, members),
        grid=(channels // LANES,),
        in_specs=[
            pl.BlockSpec((rows, LANES), lambda j: (0, j)),
            pl.BlockSpec((rows, LANES), lambda j: (0, j)),
            pl.BlockSpec((count * poles, rows), lambda j: (j, 0)),
        ],
        out_specs=pl.BlockSpec((poles, LANES), lambda j: (0, j)),
        out_shape=jax.ShapeDtypeStruct((poles, channels), BF16),
        cost_estimate=pl.CostEstimate(
            flops=2 * rows * channels * poles * count,
            bytes_accessed=rows * channels * 8,
            transcendentals=0,
        ),
    )(a, b, leave)


def convolve(reverse, count, poles, members, blocks, line_of, emit, lag_ref, gain_ref, mask_ref,
             leave_ref, alive_ref, across_ref, alive_across_ref, enter_ref, base):
    for g in range(count):
        row = jnp.broadcast_to(lag_ref[g:g + 1, :], (BLOCK, LANES))
        matrix = pltpu.roll(row, 0, 1, stride=1, stride_axis=0)
        base[g * BLOCK:(g + 1) * BLOCK, :LANES] = matrix.astype(BF16)
    base[:, LANES:] = gain_ref[...]
    state = enter_ref[...]
    for step in range(blocks):
        b = blocks - 1 - step if reverse else step
        line = line_of(b)
        low = line.astype(BF16)
        mask = mask_ref[b]
        left = (base[...].reshape(count, BLOCK, LANES + poles) * mask[None]).reshape(
            count * BLOCK, LANES + poles
        )
        right = jnp.concatenate([low, state.astype(BF16)], axis=0)
        result = pick(
            jnp.dot(left, right, preferred_element_type=F32), count, BLOCK, members
        )
        emit(b, line, result)
        if step < blocks - 1:
            gone = leave_ref[...] * alive_ref[b:b + 1, :]
            fresh = pick(
                jnp.dot(gone.astype(BF16), low, preferred_element_type=F32), count, poles, members
            )
            state = across_ref[...] * alive_across_ref[b:b + 1, :] * state + fresh


def forward_kernel(count, poles, members, blocks, query, key, value, skip, lag, gain, mask, leave,
                   alive, across, alive_across, enter, filtered, gated, base):
    def rows(b):
        return pl.ds(b * BLOCK, BLOCK)

    def line_of(b):
        return (key[rows(b), :].astype(F32) * value[rows(b), :].astype(F32)).astype(BF16).astype(F32)

    def emit(b, line, result):
        result = result + skip[...] * line
        filtered[rows(b), :] = result
        gated[rows(b), :] = (query[rows(b), :].astype(F32) * result).astype(BF16)

    convolve(False, count, poles, members, blocks, line_of, emit, lag, gain, mask, leave, alive,
             across, alive_across, enter, base)


def backward_kernel(count, poles, members, blocks, query, key, value, grad_gated, filtered, skip,
                    lag, gain, mask, leave, alive, across, alive_across, enter, grad_query,
                    grad_key, grad_value, base):
    def rows(b):
        return pl.ds(b * BLOCK, BLOCK)

    def line_of(b):
        grad = grad_gated[rows(b), :]
        grad_query[rows(b), :] = (grad * filtered[rows(b), :]).astype(BF16)
        return grad * query[rows(b), :].astype(F32)

    def emit(b, line, result):
        result = result + skip[...] * line
        grad_key[rows(b), :] = (result * value[rows(b), :].astype(F32)).astype(BF16)
        grad_value[rows(b), :] = (result * key[rows(b), :].astype(F32)).astype(BF16)

    convolve(True, count, poles, members, blocks, line_of, emit, lag, gain, mask, leave, alive,
             across, alive_across, enter, base)


def run_conv(kernel, wide, skip, tables, enter, out_types, poles, members):
    rows, channels = wide[0].shape
    count = LANES // members
    blocks = rows // BLOCK
    column = pl.BlockSpec((rows, LANES), lambda j: (0, j))
    lag, gain, mask, leave, alive, across, alive_across = tables
    return pl.pallas_call(
        functools.partial(kernel, count, poles, members, blocks),
        grid=(channels // LANES,),
        in_specs=[column] * len(wide) + [
            pl.BlockSpec((1, LANES), lambda j: (0, j)),
            pl.BlockSpec((count, BLOCK), lambda j: (j, 0)),
            pl.BlockSpec((count * BLOCK, poles), lambda j: (j, 0)),
            pl.BlockSpec((blocks, BLOCK, BLOCK + poles), lambda j: (0, 0, 0)),
            pl.BlockSpec((count * poles, BLOCK), lambda j: (j, 0)),
            pl.BlockSpec((blocks, BLOCK), lambda j: (0, 0)),
            pl.BlockSpec((poles, LANES), lambda j: (0, j)),
            pl.BlockSpec((blocks, LANES), lambda j: (0, 0)),
            pl.BlockSpec((poles, LANES), lambda j: (0, j)),
        ],
        out_specs=[column] * len(out_types),
        out_shape=[jax.ShapeDtypeStruct((rows, channels), kind) for kind in out_types],
        scratch_shapes=[pltpu.VMEM((count * BLOCK, BLOCK + poles), BF16)],
        cost_estimate=pl.CostEstimate(
            flops=16 * rows * channels * BLOCK * 2, bytes_accessed=rows * channels * 14, transcendentals=0
        ),
    )(*wide, skip, lag, gain, mask, leave, alive, across, alive_across, enter)


def swap(value, flip, size):
    return lax.ppermute(value, "ctx", [(i, i ^ flip) for i in range(size)])


def gather_rows(own, size, me):
    if size != 8:
        return lax.all_gather(own, "ctx", axis=0, tiled=True)
    half = own.shape[0] // 2
    by_x, by_y = swap(own, 2, size), swap(own, 4, size)
    first, second = swap(by_x[:half], 4, size), swap(by_y[half:], 2, size)
    parts = {0: [own], 2: [by_x], 4: [by_y], 6: [first, second]}
    for flip in (0, 2, 4, 6):
        parts[flip ^ 1] = [swap(part, 1, size) for part in parts[flip]]
    rows, columns = own.shape
    whole = jnp.zeros((rows * size, columns), own.dtype)
    for flip, pieces in parts.items():
        at = (me ^ flip) * rows
        for piece in pieces:
            whole = lax.dynamic_update_slice(whole, piece, (at, 0))
            at = at + piece.shape[0]
    return whole


def scatter_terms(grad_full, gated, size, me):
    contract = (((0,), (0,)), ((), ()))
    if size != 8:
        term = lax.dot_general(grad_full, gated, contract, preferred_element_type=F32).astype(BF16)
        return term, lambda term: lax.psum_scatter(term, "ctx", scatter_dimension=0, tiled=True).astype(F32)
    width = grad_full.shape[1] // size

    def chunk(flip):
        part = lax.dynamic_slice_in_dim(grad_full, (me ^ flip) * width, width, axis=1)
        return lax.dot_general(part, gated, contract, preferred_element_type=F32).astype(BF16)

    terms = {flip: chunk(flip) for flip in (7, 3, 5, 1, 6, 2, 4, 0)}

    def finish(terms):
        half = gated.shape[1] // 2
        sums = {}
        for flip in (6, 2, 4, 0):
            sums[flip] = terms[flip].astype(F32) + swap(terms[flip ^ 1], 1, size).astype(F32)

        def route(columns, near, far):
            far_sum = sums[far][:, columns] + swap(sums[6][:, columns].astype(BF16), near, size).astype(F32)
            own_sum = sums[0][:, columns] + swap(sums[near][:, columns].astype(BF16), near, size).astype(F32)
            return own_sum + swap(far_sum.astype(BF16), far, size).astype(F32)

        return jnp.concatenate([route(slice(0, half), 2, 4), route(slice(half, None), 4, 2)], axis=1)

    return terms, finish


def local(
    query_in, key_in, value_in, residues, decay_time, skip_gain, out_proj, doc_lengths, grad_out
):
    rows, channels = query_in.shape
    filters, poles = residues.shape
    members = channels // filters
    blocks = rows // BLOCK
    size, me = lax.axis_size("ctx"), lax.axis_index("ctx")
    gathered = gather_rows(out_proj, size, me)
    grad_full = lax.all_gather(grad_out, "grp", axis=1, tiled=True)

    docs = jnp.arange(doc_lengths.shape[0])
    starts = jnp.sum(jnp.where(docs[None, :] < docs[:, None], doc_lengths[None, :], 0), axis=1)
    flat_ids = doc_index(starts, me * rows + jnp.arange(rows, dtype=jnp.int32))
    ids = flat_ids.reshape(blocks, BLOCK)
    firsts, lasts = ids[:, 0], ids[:, -1]
    before = doc_index(starts, me * rows - 1 + BLOCK * jnp.arange(blocks + 1, dtype=jnp.int32))
    after = doc_index(starts, me * rows + BLOCK * jnp.arange(1, blocks + 1, dtype=jnp.int32))
    ends = doc_index(starts, rows * jnp.arange(1, size + 1, dtype=jnp.int32) - 1)
    opens = doc_index(starts, rows * jnp.arange(size, dtype=jnp.int32))
    rate = 1.0 / decay_time
    beta = residues * jnp.sqrt(-jnp.expm1(-2.0 * rate))
    lags = jnp.arange(BLOCK, dtype=F32)
    rate_chan = jnp.repeat(rate.T, members, axis=1)
    response = jnp.sum(beta[:, :, None] * jnp.exp(-lags[None, None, :] * rate[:, :, None]), axis=1)
    mirrored = jnp.concatenate([response[:, :1], response[:, :0:-1]], axis=1)
    gain = beta[:, None, :] * jnp.exp(-(lags + 1.0)[None, :, None] * rate[:, None, :])
    gain_rev = gain[:, ::-1, :]
    leave_rev = jnp.exp(-lags[None, :] * rate.reshape(-1, 1))
    leave = jnp.exp(-(BLOCK - 1.0 - lags)[None, :] * rate.reshape(-1, 1))
    across = jnp.exp(-BLOCK * rate_chan)
    same = ids[:, :, None] == ids[:, None, :]
    place = jnp.arange(BLOCK)
    causal = place[:, None] >= place[None, :]

    def mask_of(order, alive):
        tail = jnp.broadcast_to(alive[:, :, None], (blocks, BLOCK, poles))
        return jnp.concatenate([same & order[None], tail], axis=2).astype(BF16)

    def spread(flags):
        return jnp.broadcast_to(flags.astype(F32)[:, None], (blocks, LANES))

    forward = (
        mirrored,
        gain.reshape(-1, poles).astype(BF16),
        mask_of(causal, ids == before[:blocks, None]),
        leave,
        (ids == lasts[:, None]).astype(F32),
        across,
        spread(before[:blocks] == lasts),
    )
    backward = (
        response,
        gain_rev.reshape(-1, poles).astype(BF16),
        mask_of(causal.T, ids == after[:, None]),
        leave_rev,
        (ids == firsts[:, None]).astype(F32),
        across,
        spread(after == firsts),
    )
    steps = jnp.arange(rows, dtype=F32)
    whole_leave = jnp.exp(-(rows - 1.0 - steps)[None, :] * rate.reshape(-1, 1))
    whole_leave = (whole_leave * (flat_ids == flat_ids[-1])[None, :]).astype(BF16)
    whole_leave_rev = jnp.exp(-steps[None, :] * rate.reshape(-1, 1))
    whole_leave_rev = (whole_leave_rev * (flat_ids == flat_ids[0])[None, :]).astype(BF16)

    def incoming(state, distance, alive):
        everything = lax.all_gather(state, "ctx").astype(F32)
        gap = jnp.maximum(distance, 0).astype(F32) * rows
        weight = jnp.exp(-gap[:, None, None] * rate_chan[None])
        kept = (alive & (distance >= 0))[:, None, None]
        return jnp.sum(jnp.where(kept, weight * everything, 0.0), axis=0)

    devices = jnp.arange(size, dtype=jnp.int32)
    skip = skip_gain[None, :]
    state = summarize(key_in, value_in, whole_leave, poles, members)
    enter = incoming(state, me - 1 - devices, ends == before[0])
    filtered, gated = run_conv(
        forward_kernel, (query_in, key_in, value_in), skip, forward, enter, (F32, BF16), poles, members
    )
    partial_value = lax.dot_general(
        gated, gathered, (((1,), (1,)), ((), ())), preferred_element_type=F32
    ).astype(BF16)
    mixed_out = lax.psum_scatter(partial_value, "grp", scatter_dimension=1, tiled=True)
    terms, finish = scatter_terms(grad_full, gated, size, me)
    terms, grad_full, gathered = lax.optimization_barrier((terms, grad_full, gathered))
    grad_proj = finish(terms)
    grad_gated = jnp.dot(grad_full, gathered, preferred_element_type=F32)
    state = summarize(grad_gated, query_in, whole_leave_rev, poles, members)
    leaving = incoming(state, devices - 1 - me, opens == after[-1])
    grad_query, grad_key, grad_value = run_conv(
        backward_kernel, (query_in, key_in, value_in, grad_gated, filtered), skip, backward,
        leaving, (BF16, BF16, BF16), poles, members
    )
    return (mixed_out, grad_query, grad_key, grad_value, grad_proj)


def solution(mesh):
    return jax.shard_map(
        local,
        mesh=mesh,
        in_specs=(
            P("ctx", "grp"),
            P("ctx", "grp"),
            P("ctx", "grp"),
            P("grp", None),
            P("grp", None),
            P("grp"),
            P("ctx", "grp"),
            P(),
            P("ctx", "grp"),
        ),
        out_specs=(
            P("ctx", "grp"),
            P("ctx", "grp"),
            P("ctx", "grp"),
            P("ctx", "grp"),
            P("ctx", "grp"),
        ),
        check_vma=False,
    )
```

```python
import functools

import jax
import jax.numpy as jnp
from jax import lax
from jax.experimental import pallas as pl
from jax.experimental.pallas import tpu as pltpu
from jax.sharding import PartitionSpec as P

LANES = 128
BLOCK = 128
F32 = jnp.float32
BF16 = jnp.bfloat16


def doc_index(starts, where_now):
    return jnp.sum((starts[None, :] <= where_now[:, None]).astype(jnp.int32), axis=1) - 1


def pick(stacked, count, rows, members):
    lane_filter = lax.broadcasted_iota(jnp.int32, (rows, LANES), 1) // members
    out = stacked[:rows]
    for g in range(1, count):
        out = jnp.where(lane_filter == g, stacked[g * rows:(g + 1) * rows], out)
    return out


def summary_kernel(count, poles, members, a_ref, b_ref, leave_ref, out_ref):
    line = (a_ref[...].astype(F32) * b_ref[...].astype(F32)).astype(BF16)
    stacked = jnp.dot(leave_ref[...], line, preferred_element_type=F32)
    out_ref[...] = pick(stacked, count, poles, members).astype(out_ref.dtype)


def summarize(a, b, leave, poles, members):
    rows, channels = a.shape
    count = LANES // members
    return pl.pallas_call(
        functools.partial(summary_kernel, count, poles, members),
        grid=(channels // LANES,),
        in_specs=[
            pl.BlockSpec((rows, LANES), lambda j: (0, j)),
            pl.BlockSpec((rows, LANES), lambda j: (0, j)),
            pl.BlockSpec((count * poles, rows), lambda j: (j, 0)),
        ],
        out_specs=pl.BlockSpec((poles, LANES), lambda j: (0, j)),
        out_shape=jax.ShapeDtypeStruct((poles, channels), BF16),
        cost_estimate=pl.CostEstimate(flops=0, bytes_accessed=1 << 20, transcendentals=0),
    )(a, b, leave)


def convolve(reverse, count, poles, members, blocks, line_of, emit, lag_ref, gain_ref, mask_ref,
             leave_ref, alive_ref, across_ref, alive_across_ref, enter_ref, base):
    for g in range(count):
        row = jnp.broadcast_to(lag_ref[g:g + 1, :], (BLOCK, LANES))
        matrix = pltpu.roll(row, 0, 1, stride=1, stride_axis=0)
        base[g * BLOCK:(g + 1) * BLOCK, :LANES] = matrix.astype(BF16)
    base[:, LANES:] = gain_ref[...]
    state = enter_ref[...]
    for step in range(blocks):
        b = blocks - 1 - step if reverse else step
        line = line_of(b)
        low = line.astype(BF16)
        mask = mask_ref[b]
        left = (base[...].reshape(count, BLOCK, LANES + poles) * mask[None]).reshape(
            count * BLOCK, LANES + poles
        )
        right = jnp.concatenate([low, state.astype(BF16)], axis=0)
        result = pick(
            jnp.dot(left, right, preferred_element_type=F32), count, BLOCK, members
        )
        emit(b, line, result)
        if step < blocks - 1:
            gone = leave_ref[...] * alive_ref[b:b + 1, :]
            fresh = pick(
                jnp.dot(gone.astype(BF16), low, preferred_element_type=F32), count, poles, members
            )
            state = across_ref[...] * alive_across_ref[b:b + 1, :] * state + fresh


def forward_kernel(count, poles, members, blocks, query, key, value, skip, lag, gain, mask, leave,
                   alive, across, alive_across, enter, filtered, gated, base):
    def rows(b):
        return pl.ds(b * BLOCK, BLOCK)

    def line_of(b):
        return (key[rows(b), :].astype(F32) * value[rows(b), :].astype(F32)).astype(BF16).astype(F32)

    def emit(b, line, result):
        result = result + skip[...] * line
        filtered[rows(b), :] = result
        gated[rows(b), :] = (query[rows(b), :].astype(F32) * result).astype(BF16)

    convolve(False, count, poles, members, blocks, line_of, emit, lag, gain, mask, leave, alive,
             across, alive_across, enter, base)


def backward_kernel(count, poles, members, blocks, query, key, value, grad_gated, filtered, skip,
                    lag, gain, mask, leave, alive, across, alive_across, enter, grad_query,
                    grad_key, grad_value, base):
    def rows(b):
        return pl.ds(b * BLOCK, BLOCK)

    def line_of(b):
        grad = grad_gated[rows(b), :]
        grad_query[rows(b), :] = (grad * filtered[rows(b), :]).astype(BF16)
        return grad * query[rows(b), :].astype(F32)

    def emit(b, line, result):
        result = result + skip[...] * line
        grad_key[rows(b), :] = (result * value[rows(b), :].astype(F32)).astype(BF16)
        grad_value[rows(b), :] = (result * key[rows(b), :].astype(F32)).astype(BF16)

    convolve(True, count, poles, members, blocks, line_of, emit, lag, gain, mask, leave, alive,
             across, alive_across, enter, base)


def run_conv(kernel, wide, skip, tables, enter, out_types, poles, members):
    rows, channels = wide[0].shape
    count = LANES // members
    blocks = rows // BLOCK
    column = pl.BlockSpec((rows, LANES), lambda j: (0, j))
    lag, gain, mask, leave, alive, across, alive_across = tables
    return pl.pallas_call(
        functools.partial(kernel, count, poles, members, blocks),
        grid=(channels // LANES,),
        in_specs=[column] * len(wide) + [
            pl.BlockSpec((1, LANES), lambda j: (0, j)),
            pl.BlockSpec((count, BLOCK), lambda j: (j, 0)),
            pl.BlockSpec((count * BLOCK, poles), lambda j: (j, 0)),
            pl.BlockSpec((blocks, BLOCK, BLOCK + poles), lambda j: (0, 0, 0)),
            pl.BlockSpec((count * poles, BLOCK), lambda j: (j, 0)),
            pl.BlockSpec((blocks, BLOCK), lambda j: (0, 0)),
            pl.BlockSpec((poles, LANES), lambda j: (0, j)),
            pl.BlockSpec((blocks, LANES), lambda j: (0, 0)),
            pl.BlockSpec((poles, LANES), lambda j: (0, j)),
        ],
        out_specs=[column] * len(out_types),
        out_shape=[jax.ShapeDtypeStruct((rows, channels), kind) for kind in out_types],
        scratch_shapes=[pltpu.VMEM((count * BLOCK, BLOCK + poles), BF16)],
        cost_estimate=pl.CostEstimate(flops=0, bytes_accessed=1 << 20, transcendentals=0),
    )(*wide, skip, lag, gain, mask, leave, alive, across, alive_across, enter)


def swap(value, flip, size):
    return lax.ppermute(value, "ctx", [(i, i ^ flip) for i in range(size)])


def partial_kernel(order_ref, gated_ref, weight_ref, out_ref):
    out_ref[...] = lax.dot_general(
        gated_ref[...], weight_ref[...], (((1,), (1,)), ((), ())), preferred_element_type=F32
    ).astype(BF16)


def partials(order, gated, weights, wide):
    rows, channels = gated.shape
    count = order.shape[0]
    split = 2
    return pl.pallas_call(
        partial_kernel,
        grid_spec=pltpu.PrefetchScalarGridSpec(
            num_scalar_prefetch=1,
            grid=(count, split),
            in_specs=[
                pl.BlockSpec((rows, channels), lambda i, j, order: (0, 0)),
                pl.BlockSpec((wide // split, channels), lambda i, j, order: (order[i] * split + j, 0)),
            ],
            out_specs=pl.BlockSpec((rows, wide // split), lambda i, j, order: (i, j)),
        ),
        out_shape=jax.ShapeDtypeStruct((count * rows, wide), BF16),
        cost_estimate=pl.CostEstimate(flops=0, bytes_accessed=1 << 20, transcendentals=0),
        compiler_params=pltpu.CompilerParams(vmem_limit_bytes=40 << 20),
    )(order, gated, weights)


def tie(value, *earlier):
    return lax.optimization_barrier((value,) + earlier)[0]


MESH = pl.DeviceIdType.MESH


def flipped(me, flip):
    core, x, y = me % 2, me // 2 % 2, me // 4
    core = 1 - core if flip % 2 else core
    x = 1 - x if flip // 2 % 2 else x
    y = 1 - y if flip // 4 else y
    return (y * 2 + x) * 2 + core


def greet(me, z, count):
    barrier = pltpu.get_barrier_semaphore()
    for flip in range(1, 8):
        pl.semaphore_signal(barrier, inc=1, device_id={"ctx": flipped(me, flip)}, device_id_type=MESH)

    @pl.when(z > 0)
    def _():
        pl.semaphore_signal(barrier, inc=1, device_id={"grp": z - 1}, device_id_type=MESH)

    @pl.when(z < count - 1)
    def _():
        pl.semaphore_signal(barrier, inc=1, device_id={"grp": z + 1}, device_id_type=MESH)

    pl.semaphore_wait(barrier, 9 - jnp.where(z == 0, 1, 0) - jnp.where(z == count - 1, 1, 0))


def docs_of(lengths, where):
    start, out = 0, -1
    for i in range(lengths.shape[0]):
        out = out + jnp.where(start <= where, 1, 0)
        start = start + lengths[i]
    return out


def doc_tables(reverse, lengths, me, rows, mask, alive):
    first = me * rows
    shape = (BLOCK, BLOCK)
    down, across = lax.broadcasted_iota(jnp.int32, shape, 0), lax.broadcasted_iota(jnp.int32, shape, 1)
    ordered = down <= across if reverse else down >= across
    crosses = []
    for b in range(rows // BLOCK):
        at = first + b * BLOCK
        entry, left = (at + BLOCK, at) if reverse else (at - 1, at + BLOCK - 1)
        entry, left = docs_of(lengths, entry), docs_of(lengths, left)
        by_row, by_column = docs_of(lengths, at + down), docs_of(lengths, at + across)
        mask[b, :, :LANES] = jnp.where((by_row == by_column) & ordered, 1.0, 0.0).astype(BF16)
        mask[b, :, LANES:] = jnp.where(by_row == entry, 1.0, 0.0).astype(BF16)[:, :mask.shape[2] - LANES]
        alive[b:b + 1, :] = jnp.where(by_column == left, 1.0, 0.0)[:1]
        crosses.append(jnp.where(entry == left, 1.0, 0.0))
    return crosses


def tile_tables(reverse, count, poles, j, rate_col, beta_col, rate, beta, base):
    at = pl.ds(pl.multiple_of(j * LANES, LANES), LANES)
    rates, betas = rate_col[at, :], beta_col[at, :]
    lane = lax.broadcasted_iota(jnp.int32, (LANES, BLOCK), 1)
    lag = lane if reverse else jnp.where(lane == 0, 0, BLOCK - lane)
    response = betas * jnp.exp(-lag.astype(F32) * rates)
    filters = pl.ds(pl.multiple_of(j * count, count), count)
    rate_rows, beta_rows = rate[filters, :], beta[filters, :]
    step = lax.broadcasted_iota(jnp.int32, (BLOCK, poles), 0)
    step = (BLOCK - step if reverse else step + 1).astype(F32)
    for g in range(count):
        row = jnp.sum(response[g * poles:(g + 1) * poles], axis=0, keepdims=True)
        matrix = pltpu.roll(jnp.broadcast_to(row, (BLOCK, LANES)), 0, 1, stride=1, stride_axis=0)
        base[g * BLOCK:(g + 1) * BLOCK, :LANES] = matrix.astype(BF16)
        gain = beta_rows[g:g + 1] * jnp.exp(-step * rate_rows[g:g + 1])
        base[g * BLOCK:(g + 1) * BLOCK, LANES:] = gain.astype(BF16)
    away = lane if reverse else BLOCK - 1 - lane
    return jnp.exp(-away.astype(F32) * rates)


def tile_convolve(reverse, count, poles, members, leave, across, enter, crosses, line_of, emit, mask, alive, base):
    blocks = len(crosses)
    state = enter
    for at in range(blocks):
        b = blocks - 1 - at if reverse else at
        line = line_of(b)
        low = line.astype(BF16)
        left = (base[...].reshape(count, BLOCK, LANES + poles) * mask[b][None]).reshape(
            count * BLOCK, LANES + poles
        )
        right = jnp.concatenate([low, state.astype(BF16)], axis=0)
        emit(b, line, pick(jnp.dot(left, right, preferred_element_type=F32), count, BLOCK, members))
        if at < blocks - 1:
            gone = (leave * alive[b:b + 1, :]).astype(BF16)
            fresh = pick(jnp.dot(gone, low, preferred_element_type=F32), count, poles, members)
            state = across * crosses[b] * state + fresh


def tile_summary(reverse, count, poles, members, lengths, me, rows, rates, line):
    t = lax.broadcasted_iota(jnp.int32, (1, rows), 1)
    edge = me * rows if reverse else me * rows + rows - 1
    kept = jnp.where(docs_of(lengths, me * rows + t) == docs_of(lengths, edge), 1.0, 0.0)
    away = (t if reverse else rows - 1 - t).astype(F32)
    table = (jnp.exp(-away * rates) * kept).astype(BF16)
    return pick(jnp.dot(table, line, preferred_element_type=F32), count, poles, members)


def swap_states(me, states, send, recv):
    copies = [
        pltpu.make_async_remote_copy(
            states.at[0], states.at[flip], send.at[flip], recv.at[flip],
            device_id={"ctx": flipped(me, flip)}, device_id_type=MESH,
        )
        for flip in range(1, 8)
    ]
    for copy in copies:
        copy.start()
    return copies


def entering(reverse, lengths, me, rows, rate_chan, states):
    edge = docs_of(lengths, me * rows + rows if reverse else me * rows - 1)
    total = jnp.zeros(rate_chan.shape, F32)
    for flip in range(1, 8):
        other = flipped(me, flip)
        gap = other - 1 - me if reverse else me - 1 - other
        theirs = docs_of(lengths, other * rows if reverse else other * rows + rows - 1)
        kept = jnp.where((gap >= 0) & (theirs == edge), 1.0, 0.0)
        decay = jnp.exp(-(jnp.maximum(gap, 0) * rows).astype(F32) * rate_chan[...])
        total = total + kept * decay * states[flip].astype(F32)
    return total


def opening_kernel(count, zs, members, lengths, query, key, value, rate_col, beta_col, rate, beta, rate_chan, skip,
                   grad_out, own, lower, upper, whole, filtered, gated, first, base, mask, alive, enter, states,
                   weight, z_send, z_recv, s_send, s_recv, w_send, w_recv, local_sem):
    me, z = lax.axis_index("ctx"), lax.axis_index("grp")
    rows, channels = query.shape
    poles = rate.shape[1]
    tiles = channels // LANES
    height = own.shape[0]
    half = height // 2
    greet(me, z, zs)
    go_up = pltpu.make_async_remote_copy(
        grad_out, lower, z_send.at[0], z_recv.at[0], device_id={"grp": (z + 1) % zs}, device_id_type=MESH
    )
    go_down = pltpu.make_async_remote_copy(
        grad_out, upper, z_send.at[1], z_recv.at[1], device_id={"grp": (z + zs - 1) % zs}, device_id_type=MESH
    )

    @pl.when(z < zs - 1)
    def _():
        go_up.start()

    @pl.when(z > 0)
    def _():
        go_down.start()

    def tile(j):
        return pl.ds(pl.multiple_of(j * LANES, LANES), LANES)

    def product(at, lanes):
        return (key[at, lanes].astype(F32) * value[at, lanes].astype(F32)).astype(BF16)

    def summarize_tile(j, carry):
        states[0, :, tile(j)] = tile_summary(
            False, count, poles, members, lengths, me, rows, rate_col[tile(j), :], product(slice(None), tile(j))
        ).astype(BF16)
        return carry

    lax.fori_loop(0, tiles, summarize_tile, 0)
    state_copies = swap_states(me, states, s_send, s_recv)

    def rows_of(flip, first=0, size=height):
        return pl.ds(pl.multiple_of(flipped(me, flip) * height + first, 16), size)

    def send(number, src, at, flip):
        return pltpu.make_async_remote_copy(
            src, whole.at[at, :], w_send.at[number], w_recv.at[number],
            device_id={"ctx": flipped(me, flip)}, device_id_type=MESH,
        )

    def pass_on(number, at, flip):
        return send(number, whole.at[at, :], at, flip)

    crosses = doc_tables(False, lengths, me, rows, mask, alive)
    for copy in state_copies:
        copy.wait_recv()
    enter[...] = entering(False, lengths, me, rows, rate_chan, states)
    keep_own = pltpu.make_async_copy(own, whole.at[rows_of(0), :], local_sem.at[0])
    keep_own.start()
    by_x, by_y, by_core = send(0, own, rows_of(0), 2), send(1, own, rows_of(0), 4), send(2, own, rows_of(0), 1)
    for copy in (by_x, by_y, by_core):
        copy.start()

    def convolve_tile(j, carry):
        lanes = tile(j)

        def line_of(b):
            return product(pl.ds(b * BLOCK, BLOCK), lanes).astype(F32)

        def emit(b, line, result):
            at = pl.ds(b * BLOCK, BLOCK)
            result = result + skip[:, lanes] * line
            filtered[at, lanes] = result
            gated[at, lanes] = (query[at, lanes].astype(F32) * result).astype(BF16)

        leave = tile_tables(False, count, poles, j, rate_col, beta_col, rate, beta, base)
        across = jnp.exp(-BLOCK * rate_chan[:, lanes])
        tile_convolve(False, count, poles, members, leave, across, enter[:, lanes], crosses, line_of, emit, mask,
                      alive, base)
        return carry

    lax.fori_loop(0, tiles, convolve_tile, 0)
    by_x.wait_recv()
    far_low = pass_on(5, rows_of(2, 0, half), 4)
    far_low.start()
    x_core = pass_on(3, rows_of(2), 1)
    x_core.start()
    by_y.wait_recv()
    far_high = pass_on(6, rows_of(4, half, half), 2)
    far_high.start()
    y_core = pass_on(4, rows_of(4), 1)
    y_core.start()
    far_low.wait_recv()
    low_core = pass_on(7, rows_of(6, 0, half), 1)
    low_core.start()
    far_high.wait_recv()
    high_core = pass_on(8, rows_of(6, half, half), 1)
    high_core.start()
    for copy in (by_core, x_core, y_core, low_core, high_core):
        copy.wait_recv()
    keep_own.wait()
    outermost = jnp.where(z < 2, zs - 1, 0) * (2 * height)
    fetch = pltpu.make_async_copy(
        whole.at[pl.ds(pl.multiple_of(outermost, 16), 2 * height), :], weight, local_sem.at[1]
    )
    fetch.start()
    fetch.wait()
    quarter = rows // 4

    def partial_rows(i, carry):
        at = pl.ds(pl.multiple_of(i * quarter, quarter), quarter)
        first[at, :] = lax.dot_general(
            gated[at, :], weight[...], (((1,), (1,)), ((), ())), preferred_element_type=F32
        ).astype(BF16)
        return carry

    lax.fori_loop(0, 4, partial_rows, 0)
    for copy in state_copies + [by_x, by_y, by_core, far_low, far_high, x_core, y_core, low_core, high_core]:
        copy.wait_send()

    @pl.when(z < zs - 1)
    def _():
        go_up.wait_send()
        go_down.wait_recv()

    @pl.when(z > 0)
    def _():
        go_down.wait_send()
        go_up.wait_recv()


def opening(zs, lengths, query, key, value, rate, beta, skip, grad_out, own, wide):
    rows, channels = query.shape
    filters, poles = rate.shape
    members = channels // filters
    count = LANES // members
    rate_chan = jnp.repeat(rate.T, members, axis=1)
    vmem, anywhere = pl.BlockSpec(memory_space=pltpu.VMEM), pl.BlockSpec(memory_space=pl.ANY)
    moved = jax.ShapeDtypeStruct((rows, channels), BF16)
    dma = pltpu.SemaphoreType.DMA
    return pl.pallas_call(
        functools.partial(opening_kernel, count, zs, members),
        in_specs=[pl.BlockSpec(memory_space=pltpu.SMEM)] + [vmem] * 9 + [anywhere] * 2,
        out_specs=[anywhere] * 3 + [vmem] * 3,
        out_shape=[
            moved, moved, jax.ShapeDtypeStruct((own.shape[0] * 8, channels), BF16),
            jax.ShapeDtypeStruct((rows, channels), F32), moved, jax.ShapeDtypeStruct((rows, wide), BF16),
        ],
        scratch_shapes=[
            pltpu.VMEM((count * BLOCK, BLOCK + poles), BF16),
            pltpu.VMEM((rows // BLOCK, BLOCK, BLOCK + poles), BF16),
            pltpu.VMEM((rows // BLOCK, LANES), F32),
            pltpu.VMEM((poles, channels), F32),
            pltpu.VMEM((8, poles, channels), BF16),
            pltpu.VMEM((wide, channels), BF16),
            dma((2,)), dma((2,)), dma((8,)), dma((8,)), dma((9,)), dma((9,)), dma((2,)),
        ],
        compiler_params=pltpu.CompilerParams(collective_id=1, has_side_effects=True, vmem_limit_bytes=50 << 20),
        cost_estimate=pl.CostEstimate(flops=1 << 34, bytes_accessed=24 << 20, transcendentals=0),
    )(lengths, query, key, value, rate.reshape(-1, 1), beta.reshape(-1, 1), rate, beta, rate_chan, skip, grad_out, own)


SENT = ((3, 3, 0, 0), (2, 2, 1, 1), (1, 0, 3, 2), (0, 1, 2, 3))
GOT = ((0, 1, 2, 3), (1, 0, 3, 2), (2, 2, 1, 1), (3, 3, 0, 0))


def by_place(table, where):
    out = jnp.int32(table[0])
    for i, value in enumerate(table[1:], 1):
        out = jnp.where(where == i, jnp.int32(value), out)
    return out


def closing_kernel(count, zs, members, lengths, query, key, value, rate_col, beta_col, rate, beta, rate_chan, skip,
                   block, gated, slope, filtered, mine0, mine1, mine2, theirs0, theirs1, theirs2, sent_up, sent_down,
                   whole, lower, upper, grad_query, grad_key, grad_value, grad_proj, grad, base, mask, alive, enter,
                   states, weight, theirs3, sums, from_core, near, far, z_send, z_recv, s_send, s_recv, c_send,
                   c_recv, n_send, n_recv, f_send, f_recv, local_sem):
    me, z = lax.axis_index("ctx"), lax.axis_index("grp")
    rows, channels = query.shape
    poles = rate.shape[1]
    tiles = channels // LANES
    height = mine0.shape[0]
    half = channels // 2
    greet(me, z, zs)
    go_up = pltpu.make_async_remote_copy(
        sent_up, lower, z_send.at[0], z_recv.at[0], device_id={"grp": (z + 1) % zs}, device_id_type=MESH
    )
    go_down = pltpu.make_async_remote_copy(
        sent_down, upper, z_send.at[1], z_recv.at[1], device_id={"grp": (z + zs - 1) % zs}, device_id_type=MESH
    )

    @pl.when(z < zs - 1)
    def _():
        go_up.start()

    @pl.when(z > 0)
    def _():
        go_down.start()

    def across_core(number, src):
        copy = pltpu.make_async_remote_copy(
            src, from_core.at[number], c_send.at[number], c_recv.at[number],
            device_id={"ctx": flipped(me, 1)}, device_id_type=MESH,
        )
        copy.start()
        return copy

    core_copies = [across_core(number, src) for number, src in enumerate((theirs0, theirs1, theirs2))]
    newest = by_place(GOT[3], z)
    fetch = pltpu.make_async_copy(
        whole.at[pl.ds(pl.multiple_of(newest * (2 * height), 16), 2 * height), :], weight, local_sem.at[0]
    )
    fetch.start()
    fetch.wait()

    def tile(j):
        return pl.ds(pl.multiple_of(j * LANES, LANES), LANES)

    quarter = rows // 4

    def slope_rows(i, carry):
        at = pl.ds(pl.multiple_of(i * quarter, quarter), quarter)
        grad[at, :] = slope[at, :] + jnp.dot(block[at, :], weight[...], preferred_element_type=F32)
        return carry

    lax.fori_loop(0, 4, slope_rows, 0)

    def summarize_tile(j, carry):
        line = (grad[:, tile(j)] * query[:, tile(j)].astype(F32)).astype(BF16)
        states[0, :, tile(j)] = tile_summary(
            True, count, poles, members, lengths, me, rows, rate_col[tile(j), :], line
        ).astype(BF16)
        return carry

    lax.fori_loop(0, tiles, summarize_tile, 0)
    state_copies = swap_states(me, states, s_send, s_recv)
    span = channels // 4

    def term(core, out):
        features = pl.ds(pl.multiple_of(core * height, height), height)

        def columns(i, carry):
            at = pl.ds(pl.multiple_of(i * span, span), span)
            out[:, at] = lax.dot_general(
                block[:, features], gated[:, at], (((0,), (0,)), ((), ())), preferred_element_type=F32
            ).astype(BF16)
            return carry

        lax.fori_loop(0, 4, columns, 0)

    term(1 - me % 2, theirs3)
    core_copies.append(across_core(3, theirs3))
    term(me % 2, sums.at[3])
    crosses = doc_tables(True, lengths, me, rows, mask, alive)
    x, y = me // 2 % 2, me // 4
    low, high = pl.ds(0, half), pl.ds(half, half)

    def hop_copy(stage, number, columns, flip, sems, into):
        return pltpu.make_async_remote_copy(
            sums.at[number, :, columns], into.at[number, :, columns], sems[0].at[stage, number],
            sems[1].at[stage, number], device_id={"ctx": flipped(me, flip)}, device_id_type=MESH,
        )

    routes = []
    for number, mine in enumerate((mine0, mine1, mine2, None)):
        owner = by_place(GOT[number], z)
        off_x, off_y = owner % 2 != x, owner // 2 != y
        core_copies[number].wait_recv()
        own = sums[number] if mine is None else mine[...]
        sums[number] = (own.astype(F32) + from_core[number].astype(F32)).astype(BF16)
        near_low = hop_copy(0, number, low, 2, (n_send, n_recv), near)
        near_high = hop_copy(1, number, high, 4, (n_send, n_recv), near)
        far_low = hop_copy(0, number, low, 4, (f_send, f_recv), far)
        far_high = hop_copy(1, number, high, 2, (f_send, f_recv), far)
        pl.when(off_x)(near_low.start)
        pl.when(off_y)(near_high.start)
        routes.append((number, off_x, off_y, near_low, near_high, far_low, far_high))

    for copy in state_copies:
        copy.wait_recv()
    enter[...] = entering(True, lengths, me, rows, rate_chan, states)

    def convolve_tile(j, carry):
        lanes = tile(j)

        def line_of(b):
            at = pl.ds(b * BLOCK, BLOCK)
            line = grad[at, lanes]
            grad_query[at, lanes] = (line * filtered[at, lanes]).astype(BF16)
            return line * query[at, lanes].astype(F32)

        def emit(b, line, result):
            at = pl.ds(b * BLOCK, BLOCK)
            result = result + skip[:, lanes] * line
            grad_key[at, lanes] = (result * value[at, lanes].astype(F32)).astype(BF16)
            grad_value[at, lanes] = (result * key[at, lanes].astype(F32)).astype(BF16)

        leave = tile_tables(True, count, poles, j, rate_col, beta_col, rate, beta, base)
        across = jnp.exp(-BLOCK * rate_chan[:, lanes])
        tile_convolve(True, count, poles, members, leave, across, enter[:, lanes], crosses, line_of, emit, mask,
                      alive, base)
        return carry

    early = tiles * 3 // 4
    lax.fori_loop(0, early, convolve_tile, 0)

    def add_near(number, columns, copy):
        def run():
            copy.wait_recv()
            total = sums[number, :, columns].astype(F32) + near[number, :, columns].astype(F32)
            sums[number, :, columns] = total.astype(BF16)
        return run

    for number, off_x, off_y, near_low, near_high, far_low, far_high in routes:
        pl.when(jnp.logical_not(off_x))(add_near(number, low, near_low))
        pl.when(jnp.logical_not(off_y))(add_near(number, high, near_high))
        pl.when(jnp.logical_not(off_x) & off_y)(far_low.start)
        pl.when(jnp.logical_not(off_y) & off_x)(far_high.start)
    lax.fori_loop(early, tiles, convolve_tile, 0)

    def finish(number, far_low, far_high):
        def run():
            far_low.wait_recv()
            far_high.wait_recv()
            grad_proj[...] = sums[number].astype(F32) + far[number].astype(F32)
        return run

    for number, off_x, off_y, near_low, near_high, far_low, far_high in routes:
        on_x, on_y = jnp.logical_not(off_x), jnp.logical_not(off_y)
        pl.when(on_x & on_y)(finish(number, far_low, far_high))
        pl.when(off_x)(near_low.wait_send)
        pl.when(off_y)(near_high.wait_send)
        pl.when(on_x & off_y)(far_low.wait_send)
        pl.when(on_y & off_x)(far_high.wait_send)
    for copy in state_copies + core_copies:
        copy.wait_send()

    @pl.when(z < zs - 1)
    def _():
        go_up.wait_send()
        go_down.wait_recv()

    @pl.when(z > 0)
    def _():
        go_down.wait_send()
        go_up.wait_recv()


def closing(zs, lengths, query, key, value, rate, beta, skip, block, gated, slope, filtered, mine, theirs, sent, whole):
    rows, channels = query.shape
    filters, poles = rate.shape
    members = channels // filters
    count = LANES // members
    height = mine[0].shape[0]
    rate_chan = jnp.repeat(rate.T, members, axis=1)
    vmem, anywhere = pl.BlockSpec(memory_space=pltpu.VMEM), pl.BlockSpec(memory_space=pl.ANY)
    moved = jax.ShapeDtypeStruct((rows, channels), BF16)
    dma = pltpu.SemaphoreType.DMA
    return pl.pallas_call(
        functools.partial(closing_kernel, count, zs, members),
        in_specs=[pl.BlockSpec(memory_space=pltpu.SMEM)] + [vmem] * 16 + [anywhere] * 6,
        out_specs=[anywhere] * 2 + [vmem] * 4,
        out_shape=[moved] * 5 + [jax.ShapeDtypeStruct((height, channels), F32)],
        scratch_shapes=[
            pltpu.VMEM((rows, channels), F32),
            pltpu.VMEM((count * BLOCK, BLOCK + poles), BF16),
            pltpu.VMEM((rows // BLOCK, BLOCK, BLOCK + poles), BF16),
            pltpu.VMEM((rows // BLOCK, LANES), F32),
            pltpu.VMEM((poles, channels), F32),
            pltpu.VMEM((8, poles, channels), BF16),
            pltpu.VMEM((2 * height, channels), BF16),
            pltpu.VMEM((height, channels), BF16),
        ] + [pltpu.VMEM((4, height, channels), BF16)] * 4 + [
            dma((2,)), dma((2,)), dma((8,)), dma((8,)), dma((4,)), dma((4,)), dma((2, 4)), dma((2, 4)), dma((2, 4)),
            dma((2, 4)), dma((1,)),
        ],
        compiler_params=pltpu.CompilerParams(collective_id=2, has_side_effects=True, vmem_limit_bytes=60 << 20),
        cost_estimate=pl.CostEstimate(flops=1 << 34, bytes_accessed=24 << 20, transcendentals=0),
    )(
        lengths, query, key, value, rate.reshape(-1, 1), beta.reshape(-1, 1), rate, beta, rate_chan, skip, block, gated,
        slope, filtered, *mine, *theirs, *sent, whole,
    )


def local(
    query_in, key_in, value_in, residues, decay_time, skip_gain, out_proj, doc_lengths, grad_out
):
    rows, channels = query_in.shape
    filters, poles = residues.shape
    members = channels // filters
    blocks = rows // BLOCK
    size, me = lax.axis_size("ctx"), lax.axis_index("ctx")
    count, z = lax.axis_size("grp"), lax.axis_index("grp")
    assert count == 4
    up = [(i, i + 1) for i in range(count - 1)]
    down = [(i + 1, i) for i in range(count - 1)]

    def exchange(up_value, down_value):
        return lax.ppermute(up_value, "grp", up), lax.ppermute(down_value, "grp", down)

    halves = (slice(0, rows),)
    lower = [[None] * count for _ in halves]
    upper = [[None] * count for _ in halves]
    docs = jnp.arange(doc_lengths.shape[0])
    starts = jnp.sum(jnp.where(docs[None, :] < docs[:, None], doc_lengths[None, :], 0), axis=1)
    flat_ids = doc_index(starts, me * rows + jnp.arange(rows, dtype=jnp.int32))
    ids = flat_ids.reshape(blocks, BLOCK)
    firsts, lasts = ids[:, 0], ids[:, -1]
    before = doc_index(starts, me * rows - 1 + BLOCK * jnp.arange(blocks + 1, dtype=jnp.int32))
    after = doc_index(starts, me * rows + BLOCK * jnp.arange(1, blocks + 1, dtype=jnp.int32))
    ends = doc_index(starts, rows * jnp.arange(1, size + 1, dtype=jnp.int32) - 1)
    opens = doc_index(starts, rows * jnp.arange(size, dtype=jnp.int32))
    rate = 1.0 / decay_time
    beta = residues * jnp.sqrt(-jnp.expm1(-2.0 * rate))
    lags = jnp.arange(BLOCK, dtype=F32)
    rate_chan = jnp.repeat(rate.T, members, axis=1)
    across = jnp.exp(-BLOCK * rate_chan)
    place = jnp.arange(BLOCK)
    causal = place[:, None] >= place[None, :]
    steps = jnp.arange(rows, dtype=F32)

    def mask_of(ids, order, alive):
        same = ids[:, :, None] == ids[:, None, :]
        tail = jnp.broadcast_to(alive[:, :, None], (blocks, BLOCK, poles))
        return jnp.concatenate([same & order[None], tail], axis=2).astype(BF16)

    def spread(flags):
        return jnp.broadcast_to(flags.astype(F32)[:, None], (blocks, LANES))

    def response_of(rate, beta):
        return jnp.sum(beta[:, :, None] * jnp.exp(-lags[None, None, :] * rate[:, :, None]), axis=1)

    def summary_table(rate, distance, kept):
        table = jnp.exp(-distance[None, :] * rate.reshape(-1, 1))
        return (table * kept[None, :]).astype(BF16)

    def gain_of(rate, beta, distance):
        table = beta[:, None, :] * jnp.exp(-distance[None, :, None] * rate[:, None, :])
        return table.reshape(-1, poles).astype(BF16)

    def forward_tables(rate, beta, ids):
        response = response_of(rate, beta)
        mirrored = jnp.concatenate([response[:, :1], response[:, :0:-1]], axis=1)
        return (
            mirrored,
            gain_of(rate, beta, lags + 1.0),
            mask_of(ids, causal, ids == before[:blocks, None]),
            jnp.exp(-(BLOCK - 1.0 - lags)[None, :] * rate.reshape(-1, 1)),
            (ids == lasts[:, None]).astype(F32),
            across,
            spread(before[:blocks] == lasts),
        )

    def backward_tables(rate, beta, ids):
        return (
            response_of(rate, beta),
            gain_of(rate, beta, BLOCK - lags),
            mask_of(ids, causal.T, ids == after[:, None]),
            jnp.exp(-lags[None, :] * rate.reshape(-1, 1)),
            (ids == firsts[:, None]).astype(F32),
            across,
            spread(after == firsts),
        )

    def incoming(state, distance, alive):
        everything = lax.all_gather(state, "ctx").astype(F32)
        gap = jnp.maximum(distance, 0).astype(F32) * rows
        weight = jnp.exp(-gap[:, None, None] * rate_chan[None])
        kept = (alive & (distance >= 0))[:, None, None]
        return jnp.sum(jnp.where(kept, weight * everything, 0.0), axis=0)

    devices = jnp.arange(size, dtype=jnp.int32)
    skip = skip_gain[None, :]
    wide = out_proj.shape[0] * size // count
    order = jnp.stack([by_place(table, z) for table in SENT])

    def forward(query_in, key_in, value_in, out_proj, rate, beta, ids, skip):
        whole_leave = summary_table(rate, rows - 1.0 - steps, flat_ids == flat_ids[-1])
        state = summarize(key_in, value_in, whole_leave, poles, members)
        enter = incoming(state, me - 1 - devices, ends == before[0])
        filtered, gated = run_conv(
            forward_kernel, (query_in, key_in, value_in), skip, forward_tables(rate, beta, ids), enter,
            (F32, BF16), poles, members
        )
        gathered = lax.all_gather(out_proj, "ctx", axis=0, tiled=True)
        return filtered, gated, gathered, partials(order[:1], gated, gathered, wide)

    if size == 8:
        lower[0][0], upper[0][0], gathered, filtered, gated, first = opening(
            count, doc_lengths, query_in, key_in, value_in, rate, beta, skip, grad_out, out_proj, wide
        )
    else:
        lower[0][0], upper[0][0] = exchange(grad_out, grad_out)
        filtered, gated, gathered, first = forward(query_in, key_in, value_in, out_proj, rate, beta, ids, skip)
    odd = z % 2 == 1
    outer = (z == 0) | (z == 3)
    none = jnp.zeros((), BF16)

    def weights(which):
        return lax.dynamic_slice_in_dim(gathered, which * wide, wide, axis=0)

    def add(came, mine):
        return (came.astype(F32) + mine.astype(F32)).astype(BF16)

    def advance(r, mine_up, mine_down, *earlier):
        out = ()
        for h, part in enumerate(halves):
            *came, _ = lax.optimization_barrier((lower[h][r - 1], upper[h][r - 1], earlier))
            came = jnp.where(z == 0, none, came[0]), jnp.where(z == count - 1, none, came[1])
            sent = lax.optimization_barrier((add(came[0], mine_up(part)), add(came[1], mine_down(part))))
            lower[h][r], upper[h][r] = exchange(*sent)
            out += sent
        return out

    sent = advance(
        1,
        lambda part: jnp.where(z == 0, first[part], none),
        lambda part: jnp.where(z == 3, first[part], none),
        first,
    )
    more = partials(tie(order, *sent)[1:], gated, gathered, wide)
    second, third, last = more[:rows], more[rows:2 * rows], more[2 * rows:]

    def join(sources, r):
        return jnp.concatenate([source[r] for source in sources], axis=0)

    contract = (((0,), (0,)), ((), ()))
    terms = []

    def terms_of(block, owners):
        which = by_place(owners, z)
        if size == 8:
            rows_of = wide // 2

            def term(core):
                part = lax.dynamic_slice_in_dim(block, core * rows_of, rows_of, axis=1)
                return lax.dot_general(part, gated, contract, preferred_element_type=F32).astype(BF16)

            terms.append((term(me % 2), term(1 - me % 2)))
            return terms[-1]
        terms.append((which, lax.dot_general(block, gated, contract, preferred_element_type=F32).astype(BF16)))
        return terms[-1][1:]

    def slope(block, owners):
        return jnp.dot(block, weights(by_place(owners, z)), preferred_element_type=F32)

    rate_b, beta_b, ids_b, _ = lax.optimization_barrier((rate, beta, ids, more))
    tables_b = backward_tables(rate_b, beta_b, ids_b)
    whole_leave_rev = summary_table(rate_b, steps, flat_ids == flat_ids[0])

    own = tie(grad_out, more, *sent)
    done0 = terms_of(own, GOT[0])
    grad_gated = slope(own, GOT[0])
    came = lax.optimization_barrier((join(lower, 0), join(upper, 0), grad_gated))
    block = jnp.where(odd, came[0], came[1])
    done1 = terms_of(block, GOT[1])
    grad_gated = grad_gated + slope(block, GOT[1])
    sent = advance(
        2,
        lambda part: jnp.where(z == 0, second[part], jnp.where(z == 1, first[part], none)),
        lambda part: jnp.where(z == 3, second[part], jnp.where(z == 2, first[part], none)),
        more, grad_gated, *done0, *done1,
    )
    up0, up1, low0, low1, *_ = lax.optimization_barrier(
        (join(upper, 0), join(upper, 1), join(lower, 0), join(lower, 1), grad_gated, sent)
    )
    block = jnp.where(z < 2, jnp.where(outer, up1, up0), jnp.where(outer, low1, low0))
    done2 = terms_of(block, GOT[2])
    grad_gated = grad_gated + slope(block, GOT[2])
    for_up = jnp.where(z == 1, second, jnp.where(z == 3, none, third))
    for_down = jnp.where(z == 2, second, jnp.where(z == 0, none, third))
    if size == 8:
        came_up, came_down, up1, low1, _ = lax.optimization_barrier(
            (lower[0][2], upper[0][2], upper[0][1], lower[0][1], (grad_gated, done2))
        )
        sent = add(came_up, for_up), add(came_down, for_down)
        block = jnp.where(z < 2, jnp.where(outer, came_down, up1), jnp.where(outer, came_up, low1))
        lower[0][3], upper[0][3], grad_query, grad_key, grad_value, grad_proj = closing(
            count, doc_lengths, query_in, key_in, value_in, rate, beta, skip, block, gated, grad_gated, filtered,
            [mine for mine, _ in terms], [theirs for _, theirs in terms], sent, gathered
        )
        came_up, came_down = jnp.where(z == 0, none, lower[0][3]), jnp.where(z == count - 1, none, upper[0][3])
        mixed_out = (last.astype(F32) + came_up.astype(F32) + came_down.astype(F32)).astype(BF16)
    else:
        sent = advance(
            3,
            lambda part: jnp.where(z == 1, second[part], jnp.where(z == 3, none, third[part])),
            lambda part: jnp.where(z == 2, second[part], jnp.where(z == 0, none, third[part])),
            grad_gated, terms[0][1], terms[1][1], *done2,
        )
        up1, up2, low1, low2, *_ = lax.optimization_barrier(
            (join(upper, 1), join(upper, 2), join(lower, 1), join(lower, 2), grad_gated, done2, sent)
        )
        block = jnp.where(z < 2, jnp.where(outer, up2, up1), jnp.where(outer, low2, low1))
        done3 = terms_of(block, GOT[3])
        grad_gated = grad_gated + slope(tie(block, *done3), GOT[3])
        term = jnp.zeros((wide * count, channels), BF16)
        for which, value in terms:
            term = lax.dynamic_update_slice(term, value, (which * wide, 0))
        grad_proj = lax.psum_scatter(term, "ctx", scatter_dimension=0, tiled=True).astype(F32)
        state = summarize(grad_gated, query_in, whole_leave_rev, poles, members)
        leaving = incoming(state, devices - 1 - me, opens == after[-1])
        grad_query, grad_key, grad_value = run_conv(
            backward_kernel, (query_in, key_in, value_in, grad_gated, filtered), skip, tables_b,
            leaving, (BF16, BF16, BF16), poles, members
        )
        mixed_out = (last.astype(F32) + join(lower, 3).astype(F32) + join(upper, 3).astype(F32)).astype(BF16)
    return (mixed_out, grad_query, grad_key, grad_value, grad_proj)


def solution(mesh):
    return jax.shard_map(
        local,
        mesh=mesh,
        in_specs=(
            P("ctx", "grp"),
            P("ctx", "grp"),
            P("ctx", "grp"),
            P("grp", None),
            P("grp", None),
            P("grp"),
            P("ctx", "grp"),
            P(),
            P("ctx", "grp"),
        ),
        out_specs=(
            P("ctx", "grp"),
            P("ctx", "grp"),
            P("ctx", "grp"),
            P("ctx", "grp"),
            P("ctx", "grp"),
        ),
        check_vma=False,
    )
```

```python
import functools

import jax
import jax.numpy as jnp
from jax import lax
from jax.experimental import pallas as pl
from jax.experimental.pallas import tpu as pltpu
from jax.sharding import PartitionSpec as P

LANES = 128
BLOCK = 128
F32 = jnp.float32
BF16 = jnp.bfloat16


def doc_index(starts, where_now):
    return jnp.sum((starts[None, :] <= where_now[:, None]).astype(jnp.int32), axis=1) - 1


def pick(stacked, count, rows, members):
    lane_filter = lax.broadcasted_iota(jnp.int32, (rows, LANES), 1) // members
    out = stacked[:rows]
    for g in range(1, count):
        out = jnp.where(lane_filter == g, stacked[g * rows:(g + 1) * rows], out)
    return out


def summary_kernel(count, poles, members, a_ref, b_ref, leave_ref, out_ref):
    line = (a_ref[...].astype(F32) * b_ref[...].astype(F32)).astype(BF16)
    stacked = jnp.dot(leave_ref[...], line, preferred_element_type=F32)
    out_ref[...] = pick(stacked, count, poles, members).astype(out_ref.dtype)


def summarize(a, b, leave, poles, members):
    rows, channels = a.shape
    count = LANES // members
    return pl.pallas_call(
        functools.partial(summary_kernel, count, poles, members),
        grid=(channels // LANES,),
        in_specs=[
            pl.BlockSpec((rows, LANES), lambda j: (0, j)),
            pl.BlockSpec((rows, LANES), lambda j: (0, j)),
            pl.BlockSpec((count * poles, rows), lambda j: (j, 0)),
        ],
        out_specs=pl.BlockSpec((poles, LANES), lambda j: (0, j)),
        out_shape=jax.ShapeDtypeStruct((poles, channels), BF16),
        cost_estimate=pl.CostEstimate(flops=0, bytes_accessed=1 << 20, transcendentals=0),
    )(a, b, leave)


def convolve(reverse, count, poles, members, blocks, line_of, emit, lag_ref, gain_ref, mask_ref,
             leave_ref, alive_ref, across_ref, alive_across_ref, enter_ref, base):
    for g in range(count):
        row = jnp.broadcast_to(lag_ref[g:g + 1, :], (BLOCK, LANES))
        matrix = pltpu.roll(row, 0, 1, stride=1, stride_axis=0)
        base[g * BLOCK:(g + 1) * BLOCK, :LANES] = matrix.astype(BF16)
    base[:, LANES:] = gain_ref[...]
    state = enter_ref[...]
    for step in range(blocks):
        b = blocks - 1 - step if reverse else step
        line = line_of(b)
        low = line.astype(BF16)
        mask = mask_ref[b]
        left = (base[...].reshape(count, BLOCK, LANES + poles) * mask[None]).reshape(
            count * BLOCK, LANES + poles
        )
        right = jnp.concatenate([low, state.astype(BF16)], axis=0)
        result = pick(
            jnp.dot(left, right, preferred_element_type=F32), count, BLOCK, members
        )
        emit(b, line, result)
        if step < blocks - 1:
            gone = leave_ref[...] * alive_ref[b:b + 1, :]
            fresh = pick(
                jnp.dot(gone.astype(BF16), low, preferred_element_type=F32), count, poles, members
            )
            state = across_ref[...] * alive_across_ref[b:b + 1, :] * state + fresh


def forward_kernel(count, poles, members, blocks, query, key, value, skip, lag, gain, mask, leave,
                   alive, across, alive_across, enter, filtered, gated, base):
    def rows(b):
        return pl.ds(b * BLOCK, BLOCK)

    def line_of(b):
        return (key[rows(b), :].astype(F32) * value[rows(b), :].astype(F32)).astype(BF16).astype(F32)

    def emit(b, line, result):
        result = result + skip[...] * line
        filtered[rows(b), :] = result
        gated[rows(b), :] = (query[rows(b), :].astype(F32) * result).astype(BF16)

    convolve(False, count, poles, members, blocks, line_of, emit, lag, gain, mask, leave, alive,
             across, alive_across, enter, base)


def backward_kernel(count, poles, members, blocks, query, key, value, grad_gated, filtered, skip,
                    lag, gain, mask, leave, alive, across, alive_across, enter, grad_query,
                    grad_key, grad_value, base):
    def rows(b):
        return pl.ds(b * BLOCK, BLOCK)

    def line_of(b):
        grad = grad_gated[rows(b), :]
        grad_query[rows(b), :] = (grad * filtered[rows(b), :]).astype(BF16)
        return grad * query[rows(b), :].astype(F32)

    def emit(b, line, result):
        result = result + skip[...] * line
        grad_key[rows(b), :] = (result * value[rows(b), :].astype(F32)).astype(BF16)
        grad_value[rows(b), :] = (result * key[rows(b), :].astype(F32)).astype(BF16)

    convolve(True, count, poles, members, blocks, line_of, emit, lag, gain, mask, leave, alive,
             across, alive_across, enter, base)


def run_conv(kernel, wide, skip, tables, enter, out_types, poles, members):
    rows, channels = wide[0].shape
    count = LANES // members
    blocks = rows // BLOCK
    column = pl.BlockSpec((rows, LANES), lambda j: (0, j))
    lag, gain, mask, leave, alive, across, alive_across = tables
    return pl.pallas_call(
        functools.partial(kernel, count, poles, members, blocks),
        grid=(channels // LANES,),
        in_specs=[column] * len(wide) + [
            pl.BlockSpec((1, LANES), lambda j: (0, j)),
            pl.BlockSpec((count, BLOCK), lambda j: (j, 0)),
            pl.BlockSpec((count * BLOCK, poles), lambda j: (j, 0)),
            pl.BlockSpec((blocks, BLOCK, BLOCK + poles), lambda j: (0, 0, 0)),
            pl.BlockSpec((count * poles, BLOCK), lambda j: (j, 0)),
            pl.BlockSpec((blocks, BLOCK), lambda j: (0, 0)),
            pl.BlockSpec((poles, LANES), lambda j: (0, j)),
            pl.BlockSpec((blocks, LANES), lambda j: (0, 0)),
            pl.BlockSpec((poles, LANES), lambda j: (0, j)),
        ],
        out_specs=[column] * len(out_types),
        out_shape=[jax.ShapeDtypeStruct((rows, channels), kind) for kind in out_types],
        scratch_shapes=[pltpu.VMEM((count * BLOCK, BLOCK + poles), BF16)],
        cost_estimate=pl.CostEstimate(flops=0, bytes_accessed=1 << 20, transcendentals=0),
    )(*wide, skip, lag, gain, mask, leave, alive, across, alive_across, enter)


def swap(value, flip, size):
    return lax.ppermute(value, "ctx", [(i, i ^ flip) for i in range(size)])


def partial_kernel(order_ref, gated_ref, weight_ref, out_ref):
    out_ref[...] = lax.dot_general(
        gated_ref[...], weight_ref[...], (((1,), (1,)), ((), ())), preferred_element_type=F32
    ).astype(BF16)


def partials(order, gated, weights, wide):
    rows, channels = gated.shape
    count = order.shape[0]
    split = 2
    return pl.pallas_call(
        partial_kernel,
        grid_spec=pltpu.PrefetchScalarGridSpec(
            num_scalar_prefetch=1,
            grid=(count, split),
            in_specs=[
                pl.BlockSpec((rows, channels), lambda i, j, order: (0, 0)),
                pl.BlockSpec((wide // split, channels), lambda i, j, order: (order[i] * split + j, 0)),
            ],
            out_specs=pl.BlockSpec((rows, wide // split), lambda i, j, order: (i, j)),
        ),
        out_shape=jax.ShapeDtypeStruct((count * rows, wide), BF16),
        cost_estimate=pl.CostEstimate(flops=0, bytes_accessed=1 << 20, transcendentals=0),
        compiler_params=pltpu.CompilerParams(vmem_limit_bytes=40 << 20),
    )(order, gated, weights)


def tie(value, *earlier):
    return lax.optimization_barrier((value,) + earlier)[0]


MESH = pl.DeviceIdType.MESH


def flipped(me, flip):
    core, x, y = me % 2, me // 2 % 2, me // 4
    core = 1 - core if flip % 2 else core
    x = 1 - x if flip // 2 % 2 else x
    y = 1 - y if flip // 4 else y
    return (y * 2 + x) * 2 + core


def greet(me, z, count):
    barrier = pltpu.get_barrier_semaphore()
    for flip in range(1, 8):
        pl.semaphore_signal(barrier, inc=1, device_id={"ctx": flipped(me, flip)}, device_id_type=MESH)

    @pl.when(z > 0)
    def _():
        pl.semaphore_signal(barrier, inc=1, device_id={"grp": z - 1}, device_id_type=MESH)

    @pl.when(z < count - 1)
    def _():
        pl.semaphore_signal(barrier, inc=1, device_id={"grp": z + 1}, device_id_type=MESH)

    pl.semaphore_wait(barrier, 9 - jnp.where(z == 0, 1, 0) - jnp.where(z == count - 1, 1, 0))


def docs_of(lengths, where):
    start, out = 0, -1
    for i in range(lengths.shape[0]):
        out = out + jnp.where(start <= where, 1, 0)
        start = start + lengths[i]
    return out


def doc_tables(reverse, lengths, me, rows, mask, alive):
    first = me * rows
    shape = (BLOCK, BLOCK)
    down, across = lax.broadcasted_iota(jnp.int32, shape, 0), lax.broadcasted_iota(jnp.int32, shape, 1)
    ordered = down <= across if reverse else down >= across
    crosses = []
    for b in range(rows // BLOCK):
        at = first + b * BLOCK
        entry, left = (at + BLOCK, at) if reverse else (at - 1, at + BLOCK - 1)
        entry, left = docs_of(lengths, entry), docs_of(lengths, left)
        by_row, by_column = docs_of(lengths, at + down), docs_of(lengths, at + across)
        mask[b, :, :LANES] = jnp.where((by_row == by_column) & ordered, 1.0, 0.0).astype(BF16)
        mask[b, :, LANES:] = jnp.where(by_row == entry, 1.0, 0.0).astype(BF16)[:, :mask.shape[2] - LANES]
        alive[b:b + 1, :] = jnp.where(by_column == left, 1.0, 0.0)[:1]
        crosses.append(jnp.where(entry == left, 1.0, 0.0))
    return crosses


def tile_tables(reverse, count, poles, j, rate_col, beta_col, rate, beta, base):
    at = pl.ds(pl.multiple_of(j * LANES, LANES), LANES)
    rates, betas = rate_col[at, :], beta_col[at, :]
    lane = lax.broadcasted_iota(jnp.int32, (LANES, BLOCK), 1)
    lag = lane if reverse else jnp.where(lane == 0, 0, BLOCK - lane)
    response = betas * jnp.exp(-lag.astype(F32) * rates)
    filters = pl.ds(pl.multiple_of(j * count, count), count)
    rate_rows, beta_rows = rate[filters, :], beta[filters, :]
    step = lax.broadcasted_iota(jnp.int32, (BLOCK, poles), 0)
    step = (BLOCK - step if reverse else step + 1).astype(F32)
    for g in range(count):
        row = jnp.sum(response[g * poles:(g + 1) * poles], axis=0, keepdims=True)
        matrix = pltpu.roll(jnp.broadcast_to(row, (BLOCK, LANES)), 0, 1, stride=1, stride_axis=0)
        base[g * BLOCK:(g + 1) * BLOCK, :LANES] = matrix.astype(BF16)
        gain = beta_rows[g:g + 1] * jnp.exp(-step * rate_rows[g:g + 1])
        base[g * BLOCK:(g + 1) * BLOCK, LANES:] = gain.astype(BF16)
    away = lane if reverse else BLOCK - 1 - lane
    return jnp.exp(-away.astype(F32) * rates)


def tile_convolve(reverse, count, poles, members, leave, across, enter, crosses, line_of, emit, mask, alive, base):
    blocks = len(crosses)
    state = enter
    for at in range(blocks):
        b = blocks - 1 - at if reverse else at
        line = line_of(b)
        low = line.astype(BF16)
        left = (base[...].reshape(count, BLOCK, LANES + poles) * mask[b][None]).reshape(
            count * BLOCK, LANES + poles
        )
        right = jnp.concatenate([low, state.astype(BF16)], axis=0)
        emit(b, line, pick(jnp.dot(left, right, preferred_element_type=F32), count, BLOCK, members))
        if at < blocks - 1:
            gone = (leave * alive[b:b + 1, :]).astype(BF16)
            fresh = pick(jnp.dot(gone, low, preferred_element_type=F32), count, poles, members)
            state = across * crosses[b] * state + fresh


def tile_summary(reverse, count, poles, members, lengths, me, rows, rates, line):
    t = lax.broadcasted_iota(jnp.int32, (1, rows), 1)
    edge = me * rows if reverse else me * rows + rows - 1
    kept = jnp.where(docs_of(lengths, me * rows + t) == docs_of(lengths, edge), 1.0, 0.0)
    away = (t if reverse else rows - 1 - t).astype(F32)
    table = (jnp.exp(-away * rates) * kept).astype(BF16)
    return pick(jnp.dot(table, line, preferred_element_type=F32), count, poles, members)


def swap_states(me, states, send, recv):
    copies = [
        pltpu.make_async_remote_copy(
            states.at[0], states.at[flip], send.at[flip], recv.at[flip],
            device_id={"ctx": flipped(me, flip)}, device_id_type=MESH,
        )
        for flip in range(1, 8)
    ]
    for copy in copies:
        copy.start()
    return copies


def entering(reverse, lengths, me, rows, rate_chan, states):
    edge = docs_of(lengths, me * rows + rows if reverse else me * rows - 1)
    total = jnp.zeros(rate_chan.shape, F32)
    for flip in range(1, 8):
        other = flipped(me, flip)
        gap = other - 1 - me if reverse else me - 1 - other
        theirs = docs_of(lengths, other * rows if reverse else other * rows + rows - 1)
        kept = jnp.where((gap >= 0) & (theirs == edge), 1.0, 0.0)
        decay = jnp.exp(-(jnp.maximum(gap, 0) * rows).astype(F32) * rate_chan[...])
        total = total + kept * decay * states[flip].astype(F32)
    return total


def opening_kernel(count, zs, members, lengths, query, key, value, rate_col, beta_col, rate, beta, rate_chan, skip,
                   grad_out, own, lower, upper, whole, filtered, gated, first, base, mask, alive, enter, states,
                   weight, z_send, z_recv, s_send, s_recv, w_send, w_recv, local_sem):
    me, z = lax.axis_index("ctx"), lax.axis_index("grp")
    rows, channels = query.shape
    poles = rate.shape[1]
    tiles = channels // LANES
    height = own.shape[0]
    half = height // 2
    greet(me, z, zs)
    go_up = pltpu.make_async_remote_copy(
        grad_out, lower, z_send.at[0], z_recv.at[0], device_id={"grp": (z + 1) % zs}, device_id_type=MESH
    )
    go_down = pltpu.make_async_remote_copy(
        grad_out, upper, z_send.at[1], z_recv.at[1], device_id={"grp": (z + zs - 1) % zs}, device_id_type=MESH
    )

    @pl.when(z < zs - 1)
    def _():
        go_up.start()

    @pl.when(z > 0)
    def _():
        go_down.start()

    def tile(j):
        return pl.ds(pl.multiple_of(j * LANES, LANES), LANES)

    def product(at, lanes):
        return (key[at, lanes].astype(F32) * value[at, lanes].astype(F32)).astype(BF16)

    def summarize_tile(j, carry):
        states[0, :, tile(j)] = tile_summary(
            False, count, poles, members, lengths, me, rows, rate_col[tile(j), :], product(slice(None), tile(j))
        ).astype(BF16)
        return carry

    lax.fori_loop(0, tiles, summarize_tile, 0)
    state_copies = swap_states(me, states, s_send, s_recv)

    def rows_of(flip, first=0, size=height):
        return pl.ds(pl.multiple_of(flipped(me, flip) * height + first, 16), size)

    def send(number, src, at, flip):
        return pltpu.make_async_remote_copy(
            src, whole.at[at, :], w_send.at[number], w_recv.at[number],
            device_id={"ctx": flipped(me, flip)}, device_id_type=MESH,
        )

    def pass_on(number, at, flip):
        return send(number, whole.at[at, :], at, flip)

    crosses = doc_tables(False, lengths, me, rows, mask, alive)
    for copy in state_copies:
        copy.wait_recv()
    enter[...] = entering(False, lengths, me, rows, rate_chan, states)
    keep_own = pltpu.make_async_copy(own, whole.at[rows_of(0), :], local_sem.at[0])
    keep_own.start()
    by_x, by_y, by_core = send(0, own, rows_of(0), 2), send(1, own, rows_of(0), 4), send(2, own, rows_of(0), 1)
    for copy in (by_x, by_y, by_core):
        copy.start()

    def convolve_tile(j, carry):
        lanes = tile(j)

        def line_of(b):
            return product(pl.ds(b * BLOCK, BLOCK), lanes).astype(F32)

        def emit(b, line, result):
            at = pl.ds(b * BLOCK, BLOCK)
            result = result + skip[:, lanes] * line
            filtered[at, lanes] = result
            gated[at, lanes] = (query[at, lanes].astype(F32) * result).astype(BF16)

        leave = tile_tables(False, count, poles, j, rate_col, beta_col, rate, beta, base)
        across = jnp.exp(-BLOCK * rate_chan[:, lanes])
        tile_convolve(False, count, poles, members, leave, across, enter[:, lanes], crosses, line_of, emit, mask,
                      alive, base)
        return carry

    lax.fori_loop(0, tiles, convolve_tile, 0)
    by_x.wait_recv()
    far_low = pass_on(5, rows_of(2, 0, half), 4)
    far_low.start()
    x_core = pass_on(3, rows_of(2), 1)
    x_core.start()
    by_y.wait_recv()
    far_high = pass_on(6, rows_of(4, half, half), 2)
    far_high.start()
    y_core = pass_on(4, rows_of(4), 1)
    y_core.start()
    far_low.wait_recv()
    low_core = pass_on(7, rows_of(6, 0, half), 1)
    low_core.start()
    far_high.wait_recv()
    high_core = pass_on(8, rows_of(6, half, half), 1)
    high_core.start()
    for copy in (by_core, x_core, y_core, low_core, high_core):
        copy.wait_recv()
    keep_own.wait()
    outermost = jnp.where(z < 2, zs - 1, 0) * (2 * height)
    fetch = pltpu.make_async_copy(
        whole.at[pl.ds(pl.multiple_of(outermost, 16), 2 * height), :], weight, local_sem.at[1]
    )
    fetch.start()
    fetch.wait()
    quarter = rows // 4

    def partial_rows(i, carry):
        at = pl.ds(pl.multiple_of(i * quarter, quarter), quarter)
        first[at, :] = lax.dot_general(
            gated[at, :], weight[...], (((1,), (1,)), ((), ())), preferred_element_type=F32
        ).astype(BF16)
        return carry

    lax.fori_loop(0, 4, partial_rows, 0)
    for copy in state_copies + [by_x, by_y, by_core, far_low, far_high, x_core, y_core, low_core, high_core]:
        copy.wait_send()

    @pl.when(z < zs - 1)
    def _():
        go_up.wait_send()
        go_down.wait_recv()

    @pl.when(z > 0)
    def _():
        go_down.wait_send()
        go_up.wait_recv()


def opening(zs, lengths, query, key, value, rate, beta, skip, grad_out, own, wide):
    rows, channels = query.shape
    filters, poles = rate.shape
    members = channels // filters
    count = LANES // members
    rate_chan = jnp.repeat(rate.T, members, axis=1)
    vmem, anywhere = pl.BlockSpec(memory_space=pltpu.VMEM), pl.BlockSpec(memory_space=pl.ANY)
    moved = jax.ShapeDtypeStruct((rows, channels), BF16)
    dma = pltpu.SemaphoreType.DMA
    return pl.pallas_call(
        functools.partial(opening_kernel, count, zs, members),
        in_specs=[pl.BlockSpec(memory_space=pltpu.SMEM)] + [vmem] * 9 + [anywhere] * 2,
        out_specs=[anywhere] * 3 + [vmem] * 3,
        out_shape=[
            moved, moved, jax.ShapeDtypeStruct((own.shape[0] * 8, channels), BF16),
            jax.ShapeDtypeStruct((rows, channels), F32), moved, jax.ShapeDtypeStruct((rows, wide), BF16),
        ],
        scratch_shapes=[
            pltpu.VMEM((count * BLOCK, BLOCK + poles), BF16),
            pltpu.VMEM((rows // BLOCK, BLOCK, BLOCK + poles), BF16),
            pltpu.VMEM((rows // BLOCK, LANES), F32),
            pltpu.VMEM((poles, channels), F32),
            pltpu.VMEM((8, poles, channels), BF16),
            pltpu.VMEM((wide, channels), BF16),
            dma((2,)), dma((2,)), dma((8,)), dma((8,)), dma((9,)), dma((9,)), dma((2,)),
        ],
        compiler_params=pltpu.CompilerParams(collective_id=1, has_side_effects=True, vmem_limit_bytes=50 << 20),
        cost_estimate=pl.CostEstimate(flops=1 << 34, bytes_accessed=24 << 20, transcendentals=0),
    )(lengths, query, key, value, rate.reshape(-1, 1), beta.reshape(-1, 1), rate, beta, rate_chan, skip, grad_out, own)


SENT = ((3, 3, 0, 0), (2, 2, 1, 1), (1, 0, 3, 2), (0, 1, 2, 3))
GOT = ((0, 1, 2, 3), (1, 0, 3, 2), (2, 2, 1, 1), (3, 3, 0, 0))


def by_place(table, where):
    out = jnp.int32(table[0])
    for i, value in enumerate(table[1:], 1):
        out = jnp.where(where == i, jnp.int32(value), out)
    return out


def middle_kernel(zs, own, gated, lower, upper, first, whole, last, sent_up, sent_down, newest, slope, mine0, mine1,
                  mine2, theirs0, theirs1, theirs2, weights, block, came, second, parts, terms, total, z_send, z_recv,
                  fetch_sem, block_sem, out_sem):
    me, z = lax.axis_index("ctx"), lax.axis_index("grp")
    rows, channels = gated.shape
    wide = weights.shape[1]
    height = wide // 2
    low1, up1, low2, up2 = (came.at[i] for i in range(4))
    greet(me, z, zs)

    def leave_for(way, r, src):
        up = way == 0
        return pltpu.make_async_remote_copy(
            src, came.at[2 * r + way], z_send.at[r, way], z_recv.at[r, way],
            device_id={"grp": (z + 1) % zs if up else (z + zs - 1) % zs}, device_id_type=MESH,
        )

    inner_up, inner_down = (z > 0) & (z < zs - 1), (z > 0) & (z < zs - 1)
    pl.when(z == 0)(leave_for(0, 0, first).start)
    pl.when(inner_up)(leave_for(0, 0, lower).start)
    pl.when(z == zs - 1)(leave_for(1, 0, first).start)
    pl.when(inner_down)(leave_for(1, 0, upper).start)

    fetches = []
    for i, table in enumerate((SENT[1], SENT[2], SENT[3])):
        at = pl.multiple_of(by_place(table, z) * wide, 16)
        fetches.append(pltpu.make_async_copy(whole.at[pl.ds(at, wide), :], weights.at[i], fetch_sem.at[i]))
        fetches[-1].start()

    def take(slot, src):
        return pltpu.make_async_copy(src, block.at[slot], block_sem.at[slot])

    odd = z % 2 == 1
    pl.when(odd)(take(0, lower).start)
    pl.when(jnp.logical_not(odd))(take(0, upper).start)
    pl.when(z == 1)(take(1, upper).start)
    pl.when(z == 2)(take(1, lower).start)
    quarter = rows // 4

    def each_quarter(work):
        def run(i, carry):
            work(pl.ds(pl.multiple_of(i * quarter, quarter), quarter))
            return carry

        lax.fori_loop(0, 4, run, 0)

    def partial(weight, out):
        def work(at):
            out[at, :] = lax.dot_general(
                gated[at, :], weight[...], (((1,), (1,)), ((), ())), preferred_element_type=F32
            ).astype(BF16)
        each_quarter(work)

    copies = []

    def write_out(src, dst):
        copies.append(pltpu.make_async_copy(src, dst, out_sem.at[len(copies)]))
        copies[-1].start()

    def use(number, grads, weight, mine, theirs):
        for side, core, out in ((0, 1 - me % 2, theirs), (1, me % 2, mine)):
            features = pl.ds(pl.multiple_of(core * height, height), height)
            held = terms.at[2 * number + side]

            def columns(i, carry, features=features, held=held):
                at = pl.ds(pl.multiple_of(i * quarter, quarter), quarter)
                held[:, at] = lax.dot_general(
                    grads[:, features], gated[:, at], (((0,), (0,)), ((), ())), preferred_element_type=F32
                ).astype(BF16)
                return carry

            lax.fori_loop(0, channels // quarter, columns, 0)
            write_out(held, out)

        def work(at):
            part = jnp.dot(grads[at, :], weight[...], preferred_element_type=F32)
            total[at, :] = part if number == 0 else total[at, :] + part
        each_quarter(work)

    fetches[0].wait()
    partial(weights.at[0], second)
    fetches[1].wait()
    partial(weights.at[1], parts.at[0])
    fetches[2].wait()
    partial(weights.at[2], parts.at[1])
    write_out(parts.at[1], last)
    use(0, own, weights.at[2], mine0, theirs0)
    take(0, lower).wait()
    use(1, block.at[0], weights.at[1], mine1, theirs1)

    def arrive(r):
        pl.when(z > 0)(leave_for(0, r, lower).wait_recv)
        pl.when(z < zs - 1)(leave_for(1, r, upper).wait_recv)

    def left(r):
        pl.when(z < zs - 1)(leave_for(0, r, lower).wait_send)
        pl.when(z > 0)(leave_for(1, r, upper).wait_send)

    def add_to(arrived, mine):
        def work(at):
            arrived[at, :] = (arrived[at, :].astype(F32) + mine[at, :].astype(F32)).astype(BF16)
        return lambda: each_quarter(work)

    arrive(0)
    left(0)
    load_first = pltpu.make_async_copy(first, parts.at[2], fetch_sem.at[3])
    load_first.start()
    load_first.wait()
    pl.when(z == 1)(add_to(low1, parts.at[2]))
    pl.when(z == 2)(add_to(up1, parts.at[2]))
    pl.when(z == 0)(leave_for(0, 1, second).start)
    pl.when(inner_up)(leave_for(0, 1, low1).start)
    pl.when(z == zs - 1)(leave_for(1, 1, second).start)
    pl.when(inner_down)(leave_for(1, 1, up1).start)
    pl.when(z == 0)(take(1, up1).start)
    pl.when(z == zs - 1)(take(1, low1).start)
    take(1, lower).wait()
    use(2, block.at[1], weights.at[0], mine2, theirs2)
    write_out(total, slope)
    arrive(1)
    left(1)
    third = parts.at[0]
    pl.when(z == 1)(add_to(low2, second))
    pl.when(z == 2)(add_to(low2, third))
    pl.when(z == 1)(add_to(up2, third))
    pl.when(z == 2)(add_to(up2, second))

    def to_next(src, dst, sem):
        return pltpu.make_async_copy(src, dst, block_sem.at[sem])

    pl.when(z == 0)(to_next(third, sent_up, 2).start)
    pl.when(z > 0)(to_next(low2, sent_up, 2).start)
    pl.when(z == zs - 1)(to_next(third, sent_down, 3).start)
    pl.when(z < zs - 1)(to_next(up2, sent_down, 3).start)
    for place, src in enumerate((up2, up1, low1, low2)):
        pl.when(z == place)(to_next(src, newest, 4).start)
    to_next(third, sent_up, 2).wait()
    to_next(third, sent_down, 3).wait()
    to_next(third, newest, 4).wait()
    for copy in copies:
        copy.wait()


def middle(zs, own, gated, lower, upper, first, whole, wide):
    rows, channels = gated.shape
    vmem, anywhere = pl.BlockSpec(memory_space=pltpu.VMEM), pl.BlockSpec(memory_space=pl.ANY)
    moved = jax.ShapeDtypeStruct((rows, channels), BF16)
    half = jax.ShapeDtypeStruct((wide // 2, channels), BF16)
    dma = pltpu.SemaphoreType.DMA
    return pl.pallas_call(
        functools.partial(middle_kernel, zs),
        in_specs=[vmem] * 2 + [anywhere] * 4,
        out_specs=[anywhere] * 11,
        out_shape=[moved] * 4 + [jax.ShapeDtypeStruct((rows, channels), F32)] + [half] * 6,
        scratch_shapes=[
            pltpu.VMEM((3, wide, channels), BF16),
            pltpu.VMEM((2, rows, wide), BF16),
            pltpu.VMEM((4, rows, wide), BF16),
            pltpu.VMEM((rows, wide), BF16),
            pltpu.VMEM((3, rows, wide), BF16),
            pltpu.VMEM((6, wide // 2, channels), BF16),
            pltpu.VMEM((rows, channels), F32),
            dma((2, 2)), dma((2, 2)), dma((4,)), dma((5,)), dma((8,)),
        ],
        compiler_params=pltpu.CompilerParams(collective_id=3, has_side_effects=True, vmem_limit_bytes=56 << 20),
        cost_estimate=pl.CostEstimate(flops=1 << 34, bytes_accessed=24 << 20, transcendentals=0),
    )(own, gated, lower, upper, first, whole)


def closing_kernel(count, zs, members, lengths, query, key, value, rate_col, beta_col, rate, beta, rate_chan, skip,
                   block, gated, slope, filtered, mine0, mine1, mine2, theirs0, theirs1, theirs2, sent_up, sent_down,
                   whole, lower, upper, grad_query, grad_key, grad_value, grad_proj, grad, base, mask, alive, enter,
                   states, weight, theirs3, sums, from_core, near, far, z_send, z_recv, s_send, s_recv, c_send,
                   c_recv, n_send, n_recv, f_send, f_recv, local_sem):
    me, z = lax.axis_index("ctx"), lax.axis_index("grp")
    rows, channels = query.shape
    poles = rate.shape[1]
    tiles = channels // LANES
    height = mine0.shape[0]
    half = channels // 2
    greet(me, z, zs)
    go_up = pltpu.make_async_remote_copy(
        sent_up, lower, z_send.at[0], z_recv.at[0], device_id={"grp": (z + 1) % zs}, device_id_type=MESH
    )
    go_down = pltpu.make_async_remote_copy(
        sent_down, upper, z_send.at[1], z_recv.at[1], device_id={"grp": (z + zs - 1) % zs}, device_id_type=MESH
    )

    @pl.when(z < zs - 1)
    def _():
        go_up.start()

    @pl.when(z > 0)
    def _():
        go_down.start()

    def across_core(number, src):
        copy = pltpu.make_async_remote_copy(
            src, from_core.at[number], c_send.at[number], c_recv.at[number],
            device_id={"ctx": flipped(me, 1)}, device_id_type=MESH,
        )
        copy.start()
        return copy

    core_copies = [across_core(number, src) for number, src in enumerate((theirs0, theirs1, theirs2))]
    newest = by_place(GOT[3], z)
    fetch = pltpu.make_async_copy(
        whole.at[pl.ds(pl.multiple_of(newest * (2 * height), 16), 2 * height), :], weight, local_sem.at[0]
    )
    fetch.start()
    fetch.wait()

    def tile(j):
        return pl.ds(pl.multiple_of(j * LANES, LANES), LANES)

    quarter = rows // 4

    def slope_rows(i, carry):
        at = pl.ds(pl.multiple_of(i * quarter, quarter), quarter)
        grad[at, :] = slope[at, :] + jnp.dot(block[at, :], weight[...], preferred_element_type=F32)
        return carry

    lax.fori_loop(0, 4, slope_rows, 0)

    def summarize_tile(j, carry):
        line = (grad[:, tile(j)] * query[:, tile(j)].astype(F32)).astype(BF16)
        states[0, :, tile(j)] = tile_summary(
            True, count, poles, members, lengths, me, rows, rate_col[tile(j), :], line
        ).astype(BF16)
        return carry

    lax.fori_loop(0, tiles, summarize_tile, 0)
    state_copies = swap_states(me, states, s_send, s_recv)
    span = channels // 4

    def term(core, out):
        features = pl.ds(pl.multiple_of(core * height, height), height)

        def columns(i, carry):
            at = pl.ds(pl.multiple_of(i * span, span), span)
            out[:, at] = lax.dot_general(
                block[:, features], gated[:, at], (((0,), (0,)), ((), ())), preferred_element_type=F32
            ).astype(BF16)
            return carry

        lax.fori_loop(0, 4, columns, 0)

    term(1 - me % 2, theirs3)
    core_copies.append(across_core(3, theirs3))
    term(me % 2, sums.at[3])
    crosses = doc_tables(True, lengths, me, rows, mask, alive)
    x, y = me // 2 % 2, me // 4
    low, high = pl.ds(0, half), pl.ds(half, half)

    def hop_copy(stage, number, columns, flip, sems, into):
        return pltpu.make_async_remote_copy(
            sums.at[number, :, columns], into.at[number, :, columns], sems[0].at[stage, number],
            sems[1].at[stage, number], device_id={"ctx": flipped(me, flip)}, device_id_type=MESH,
        )

    routes = []
    for number, mine in enumerate((mine0, mine1, mine2, None)):
        owner = by_place(GOT[number], z)
        off_x, off_y = owner % 2 != x, owner // 2 != y
        core_copies[number].wait_recv()
        own = sums[number] if mine is None else mine[...]
        sums[number] = (own.astype(F32) + from_core[number].astype(F32)).astype(BF16)
        near_low = hop_copy(0, number, low, 2, (n_send, n_recv), near)
        near_high = hop_copy(1, number, high, 4, (n_send, n_recv), near)
        far_low = hop_copy(0, number, low, 4, (f_send, f_recv), far)
        far_high = hop_copy(1, number, high, 2, (f_send, f_recv), far)
        pl.when(off_x)(near_low.start)
        pl.when(off_y)(near_high.start)
        routes.append((number, off_x, off_y, near_low, near_high, far_low, far_high))

    for copy in state_copies:
        copy.wait_recv()
    enter[...] = entering(True, lengths, me, rows, rate_chan, states)

    def convolve_tile(j, carry):
        lanes = tile(j)

        def line_of(b):
            at = pl.ds(b * BLOCK, BLOCK)
            line = grad[at, lanes]
            grad_query[at, lanes] = (line * filtered[at, lanes]).astype(BF16)
            return line * query[at, lanes].astype(F32)

        def emit(b, line, result):
            at = pl.ds(b * BLOCK, BLOCK)
            result = result + skip[:, lanes] * line
            grad_key[at, lanes] = (result * value[at, lanes].astype(F32)).astype(BF16)
            grad_value[at, lanes] = (result * key[at, lanes].astype(F32)).astype(BF16)

        leave = tile_tables(True, count, poles, j, rate_col, beta_col, rate, beta, base)
        across = jnp.exp(-BLOCK * rate_chan[:, lanes])
        tile_convolve(True, count, poles, members, leave, across, enter[:, lanes], crosses, line_of, emit, mask,
                      alive, base)
        return carry

    early = tiles * 3 // 4
    lax.fori_loop(0, early, convolve_tile, 0)

    def add_near(number, columns, copy):
        def run():
            copy.wait_recv()
            total = sums[number, :, columns].astype(F32) + near[number, :, columns].astype(F32)
            sums[number, :, columns] = total.astype(BF16)
        return run

    for number, off_x, off_y, near_low, near_high, far_low, far_high in routes:
        pl.when(jnp.logical_not(off_x))(add_near(number, low, near_low))
        pl.when(jnp.logical_not(off_y))(add_near(number, high, near_high))
        pl.when(jnp.logical_not(off_x) & off_y)(far_low.start)
        pl.when(jnp.logical_not(off_y) & off_x)(far_high.start)
    lax.fori_loop(early, tiles, convolve_tile, 0)

    def finish(number, far_low, far_high):
        def run():
            far_low.wait_recv()
            far_high.wait_recv()
            grad_proj[...] = sums[number].astype(F32) + far[number].astype(F32)
        return run

    for number, off_x, off_y, near_low, near_high, far_low, far_high in routes:
        on_x, on_y = jnp.logical_not(off_x), jnp.logical_not(off_y)
        pl.when(on_x & on_y)(finish(number, far_low, far_high))
        pl.when(off_x)(near_low.wait_send)
        pl.when(off_y)(near_high.wait_send)
        pl.when(on_x & off_y)(far_low.wait_send)
        pl.when(on_y & off_x)(far_high.wait_send)
    for copy in state_copies + core_copies:
        copy.wait_send()

    @pl.when(z < zs - 1)
    def _():
        go_up.wait_send()
        go_down.wait_recv()

    @pl.when(z > 0)
    def _():
        go_down.wait_send()
        go_up.wait_recv()


def closing(zs, lengths, query, key, value, rate, beta, skip, block, gated, slope, filtered, mine, theirs, sent, whole):
    rows, channels = query.shape
    filters, poles = rate.shape
    members = channels // filters
    count = LANES // members
    height = mine[0].shape[0]
    rate_chan = jnp.repeat(rate.T, members, axis=1)
    vmem, anywhere = pl.BlockSpec(memory_space=pltpu.VMEM), pl.BlockSpec(memory_space=pl.ANY)
    moved = jax.ShapeDtypeStruct((rows, channels), BF16)
    dma = pltpu.SemaphoreType.DMA
    return pl.pallas_call(
        functools.partial(closing_kernel, count, zs, members),
        in_specs=[pl.BlockSpec(memory_space=pltpu.SMEM)] + [vmem] * 16 + [anywhere] * 6,
        out_specs=[anywhere] * 2 + [vmem] * 4,
        out_shape=[moved] * 5 + [jax.ShapeDtypeStruct((height, channels), F32)],
        scratch_shapes=[
            pltpu.VMEM((rows, channels), F32),
            pltpu.VMEM((count * BLOCK, BLOCK + poles), BF16),
            pltpu.VMEM((rows // BLOCK, BLOCK, BLOCK + poles), BF16),
            pltpu.VMEM((rows // BLOCK, LANES), F32),
            pltpu.VMEM((poles, channels), F32),
            pltpu.VMEM((8, poles, channels), BF16),
            pltpu.VMEM((2 * height, channels), BF16),
            pltpu.VMEM((height, channels), BF16),
        ] + [pltpu.VMEM((4, height, channels), BF16)] * 4 + [
            dma((2,)), dma((2,)), dma((8,)), dma((8,)), dma((4,)), dma((4,)), dma((2, 4)), dma((2, 4)), dma((2, 4)),
            dma((2, 4)), dma((1,)),
        ],
        compiler_params=pltpu.CompilerParams(collective_id=2, has_side_effects=True, vmem_limit_bytes=60 << 20),
        cost_estimate=pl.CostEstimate(flops=1 << 34, bytes_accessed=24 << 20, transcendentals=0),
    )(
        lengths, query, key, value, rate.reshape(-1, 1), beta.reshape(-1, 1), rate, beta, rate_chan, skip, block, gated,
        slope, filtered, *mine, *theirs, *sent, whole,
    )


def local(
    query_in, key_in, value_in, residues, decay_time, skip_gain, out_proj, doc_lengths, grad_out
):
    rows, channels = query_in.shape
    filters, poles = residues.shape
    members = channels // filters
    blocks = rows // BLOCK
    size, me = lax.axis_size("ctx"), lax.axis_index("ctx")
    count, z = lax.axis_size("grp"), lax.axis_index("grp")
    assert count == 4
    up = [(i, i + 1) for i in range(count - 1)]
    down = [(i + 1, i) for i in range(count - 1)]

    def exchange(up_value, down_value):
        return lax.ppermute(up_value, "grp", up), lax.ppermute(down_value, "grp", down)

    halves = (slice(0, rows),)
    lower = [[None] * count for _ in halves]
    upper = [[None] * count for _ in halves]
    docs = jnp.arange(doc_lengths.shape[0])
    starts = jnp.sum(jnp.where(docs[None, :] < docs[:, None], doc_lengths[None, :], 0), axis=1)
    flat_ids = doc_index(starts, me * rows + jnp.arange(rows, dtype=jnp.int32))
    ids = flat_ids.reshape(blocks, BLOCK)
    firsts, lasts = ids[:, 0], ids[:, -1]
    before = doc_index(starts, me * rows - 1 + BLOCK * jnp.arange(blocks + 1, dtype=jnp.int32))
    after = doc_index(starts, me * rows + BLOCK * jnp.arange(1, blocks + 1, dtype=jnp.int32))
    ends = doc_index(starts, rows * jnp.arange(1, size + 1, dtype=jnp.int32) - 1)
    opens = doc_index(starts, rows * jnp.arange(size, dtype=jnp.int32))
    rate = 1.0 / decay_time
    beta = residues * jnp.sqrt(-jnp.expm1(-2.0 * rate))
    lags = jnp.arange(BLOCK, dtype=F32)
    rate_chan = jnp.repeat(rate.T, members, axis=1)
    across = jnp.exp(-BLOCK * rate_chan)
    place = jnp.arange(BLOCK)
    causal = place[:, None] >= place[None, :]
    steps = jnp.arange(rows, dtype=F32)

    def mask_of(ids, order, alive):
        same = ids[:, :, None] == ids[:, None, :]
        tail = jnp.broadcast_to(alive[:, :, None], (blocks, BLOCK, poles))
        return jnp.concatenate([same & order[None], tail], axis=2).astype(BF16)

    def spread(flags):
        return jnp.broadcast_to(flags.astype(F32)[:, None], (blocks, LANES))

    def response_of(rate, beta):
        return jnp.sum(beta[:, :, None] * jnp.exp(-lags[None, None, :] * rate[:, :, None]), axis=1)

    def summary_table(rate, distance, kept):
        table = jnp.exp(-distance[None, :] * rate.reshape(-1, 1))
        return (table * kept[None, :]).astype(BF16)

    def gain_of(rate, beta, distance):
        table = beta[:, None, :] * jnp.exp(-distance[None, :, None] * rate[:, None, :])
        return table.reshape(-1, poles).astype(BF16)

    def forward_tables(rate, beta, ids):
        response = response_of(rate, beta)
        mirrored = jnp.concatenate([response[:, :1], response[:, :0:-1]], axis=1)
        return (
            mirrored,
            gain_of(rate, beta, lags + 1.0),
            mask_of(ids, causal, ids == before[:blocks, None]),
            jnp.exp(-(BLOCK - 1.0 - lags)[None, :] * rate.reshape(-1, 1)),
            (ids == lasts[:, None]).astype(F32),
            across,
            spread(before[:blocks] == lasts),
        )

    def backward_tables(rate, beta, ids):
        return (
            response_of(rate, beta),
            gain_of(rate, beta, BLOCK - lags),
            mask_of(ids, causal.T, ids == after[:, None]),
            jnp.exp(-lags[None, :] * rate.reshape(-1, 1)),
            (ids == firsts[:, None]).astype(F32),
            across,
            spread(after == firsts),
        )

    def incoming(state, distance, alive):
        everything = lax.all_gather(state, "ctx").astype(F32)
        gap = jnp.maximum(distance, 0).astype(F32) * rows
        weight = jnp.exp(-gap[:, None, None] * rate_chan[None])
        kept = (alive & (distance >= 0))[:, None, None]
        return jnp.sum(jnp.where(kept, weight * everything, 0.0), axis=0)

    devices = jnp.arange(size, dtype=jnp.int32)
    skip = skip_gain[None, :]
    wide = out_proj.shape[0] * size // count
    order = jnp.stack([by_place(table, z) for table in SENT])

    def forward(query_in, key_in, value_in, out_proj, rate, beta, ids, skip):
        whole_leave = summary_table(rate, rows - 1.0 - steps, flat_ids == flat_ids[-1])
        state = summarize(key_in, value_in, whole_leave, poles, members)
        enter = incoming(state, me - 1 - devices, ends == before[0])
        filtered, gated = run_conv(
            forward_kernel, (query_in, key_in, value_in), skip, forward_tables(rate, beta, ids), enter,
            (F32, BF16), poles, members
        )
        gathered = lax.all_gather(out_proj, "ctx", axis=0, tiled=True)
        return filtered, gated, gathered, partials(order[:1], gated, gathered, wide)

    if size == 8:
        lower[0][0], upper[0][0], gathered, filtered, gated, first = opening(
            count, doc_lengths, query_in, key_in, value_in, rate, beta, skip, grad_out, out_proj, wide
        )
    else:
        lower[0][0], upper[0][0] = exchange(grad_out, grad_out)
        filtered, gated, gathered, first = forward(query_in, key_in, value_in, out_proj, rate, beta, ids, skip)
    odd = z % 2 == 1
    outer = (z == 0) | (z == 3)
    none = jnp.zeros((), BF16)

    if size == 8:
        last, sent_up, sent_down, block, grad_gated, *terms = middle(
            count, grad_out, gated, lower[0][0], upper[0][0], first, gathered, wide
        )
        came_up, came_down, grad_query, grad_key, grad_value, grad_proj = closing(
            count, doc_lengths, query_in, key_in, value_in, rate, beta, skip, block, gated, grad_gated, filtered,
            terms[:3], terms[3:], (sent_up, sent_down), gathered
        )
        came_up, came_down = jnp.where(z == 0, none, came_up), jnp.where(z == count - 1, none, came_down)
        mixed_out = (last.astype(F32) + came_up.astype(F32) + came_down.astype(F32)).astype(BF16)
        return (mixed_out, grad_query, grad_key, grad_value, grad_proj)

    def weights(which):
        return lax.dynamic_slice_in_dim(gathered, which * wide, wide, axis=0)

    def add(came, mine):
        return (came.astype(F32) + mine.astype(F32)).astype(BF16)

    def advance(r, mine_up, mine_down, *earlier):
        out = ()
        for h, part in enumerate(halves):
            *came, _ = lax.optimization_barrier((lower[h][r - 1], upper[h][r - 1], earlier))
            came = jnp.where(z == 0, none, came[0]), jnp.where(z == count - 1, none, came[1])
            sent = lax.optimization_barrier((add(came[0], mine_up(part)), add(came[1], mine_down(part))))
            lower[h][r], upper[h][r] = exchange(*sent)
            out += sent
        return out

    sent = advance(
        1,
        lambda part: jnp.where(z == 0, first[part], none),
        lambda part: jnp.where(z == 3, first[part], none),
        first,
    )
    more = partials(tie(order, *sent)[1:], gated, gathered, wide)
    second, third, last = more[:rows], more[rows:2 * rows], more[2 * rows:]

    def join(sources, r):
        return jnp.concatenate([source[r] for source in sources], axis=0)

    contract = (((0,), (0,)), ((), ()))
    terms = []

    def terms_of(block, owners):
        which = by_place(owners, z)
        terms.append((which, lax.dot_general(block, gated, contract, preferred_element_type=F32).astype(BF16)))
        return terms[-1][1:]

    def slope(block, owners):
        return jnp.dot(block, weights(by_place(owners, z)), preferred_element_type=F32)

    rate_b, beta_b, ids_b, _ = lax.optimization_barrier((rate, beta, ids, more))
    tables_b = backward_tables(rate_b, beta_b, ids_b)
    whole_leave_rev = summary_table(rate_b, steps, flat_ids == flat_ids[0])

    own = tie(grad_out, more, *sent)
    done0 = terms_of(own, GOT[0])
    grad_gated = slope(own, GOT[0])
    came = lax.optimization_barrier((join(lower, 0), join(upper, 0), grad_gated))
    block = jnp.where(odd, came[0], came[1])
    done1 = terms_of(block, GOT[1])
    grad_gated = grad_gated + slope(block, GOT[1])
    sent = advance(
        2,
        lambda part: jnp.where(z == 0, second[part], jnp.where(z == 1, first[part], none)),
        lambda part: jnp.where(z == 3, second[part], jnp.where(z == 2, first[part], none)),
        more, grad_gated, *done0, *done1,
    )
    up0, up1, low0, low1, *_ = lax.optimization_barrier(
        (join(upper, 0), join(upper, 1), join(lower, 0), join(lower, 1), grad_gated, sent)
    )
    block = jnp.where(z < 2, jnp.where(outer, up1, up0), jnp.where(outer, low1, low0))
    done2 = terms_of(block, GOT[2])
    grad_gated = grad_gated + slope(block, GOT[2])
    for_up = jnp.where(z == 1, second, jnp.where(z == 3, none, third))
    for_down = jnp.where(z == 2, second, jnp.where(z == 0, none, third))
    sent = advance(
        3,
        lambda part: jnp.where(z == 1, second[part], jnp.where(z == 3, none, third[part])),
        lambda part: jnp.where(z == 2, second[part], jnp.where(z == 0, none, third[part])),
        grad_gated, terms[0][1], terms[1][1], *done2,
    )
    up1, up2, low1, low2, *_ = lax.optimization_barrier(
        (join(upper, 1), join(upper, 2), join(lower, 1), join(lower, 2), grad_gated, done2, sent)
    )
    block = jnp.where(z < 2, jnp.where(outer, up2, up1), jnp.where(outer, low2, low1))
    done3 = terms_of(block, GOT[3])
    grad_gated = grad_gated + slope(tie(block, *done3), GOT[3])
    term = jnp.zeros((wide * count, channels), BF16)
    for which, value in terms:
        term = lax.dynamic_update_slice(term, value, (which * wide, 0))
    grad_proj = lax.psum_scatter(term, "ctx", scatter_dimension=0, tiled=True).astype(F32)
    state = summarize(grad_gated, query_in, whole_leave_rev, poles, members)
    leaving = incoming(state, devices - 1 - me, opens == after[-1])
    grad_query, grad_key, grad_value = run_conv(
        backward_kernel, (query_in, key_in, value_in, grad_gated, filtered), skip, tables_b,
        leaving, (BF16, BF16, BF16), poles, members
    )
    mixed_out = (last.astype(F32) + join(lower, 3).astype(F32) + join(upper, 3).astype(F32)).astype(BF16)
    return (mixed_out, grad_query, grad_key, grad_value, grad_proj)


def solution(mesh):
    return jax.shard_map(
        local,
        mesh=mesh,
        in_specs=(
            P("ctx", "grp"),
            P("ctx", "grp"),
            P("ctx", "grp"),
            P("grp", None),
            P("grp", None),
            P("grp"),
            P("ctx", "grp"),
            P(),
            P("ctx", "grp"),
        ),
        out_specs=(
            P("ctx", "grp"),
            P("ctx", "grp"),
            P("ctx", "grp"),
            P("ctx", "grp"),
            P("ctx", "grp"),
        ),
        check_vma=False,
    )
```

```python
import functools

import jax
import jax.numpy as jnp
from jax import lax
from jax.experimental import pallas as pl
from jax.experimental.pallas import tpu as pltpu
from jax.sharding import PartitionSpec as P

LANES = 128
BLOCK = 128
F32 = jnp.float32
BF16 = jnp.bfloat16


def doc_index(starts, where_now):
    return jnp.sum((starts[None, :] <= where_now[:, None]).astype(jnp.int32), axis=1) - 1


def pick(stacked, count, rows, members):
    lane_filter = lax.broadcasted_iota(jnp.int32, (rows, LANES), 1) // members
    out = stacked[:rows]
    for g in range(1, count):
        out = jnp.where(lane_filter == g, stacked[g * rows:(g + 1) * rows], out)
    return out


def summary_kernel(count, poles, members, a_ref, b_ref, leave_ref, out_ref):
    line = (a_ref[...].astype(F32) * b_ref[...].astype(F32)).astype(BF16)
    stacked = jnp.dot(leave_ref[...], line, preferred_element_type=F32)
    out_ref[...] = pick(stacked, count, poles, members).astype(out_ref.dtype)


def summarize(a, b, leave, poles, members):
    rows, channels = a.shape
    count = LANES // members
    return pl.pallas_call(
        functools.partial(summary_kernel, count, poles, members),
        grid=(channels // LANES,),
        in_specs=[
            pl.BlockSpec((rows, LANES), lambda j: (0, j)),
            pl.BlockSpec((rows, LANES), lambda j: (0, j)),
            pl.BlockSpec((count * poles, rows), lambda j: (j, 0)),
        ],
        out_specs=pl.BlockSpec((poles, LANES), lambda j: (0, j)),
        out_shape=jax.ShapeDtypeStruct((poles, channels), BF16),
        cost_estimate=pl.CostEstimate(flops=0, bytes_accessed=1 << 20, transcendentals=0),
    )(a, b, leave)


def convolve(reverse, count, poles, members, blocks, line_of, emit, lag_ref, gain_ref, mask_ref,
             leave_ref, alive_ref, across_ref, alive_across_ref, enter_ref, base):
    for g in range(count):
        row = jnp.broadcast_to(lag_ref[g:g + 1, :], (BLOCK, LANES))
        matrix = pltpu.roll(row, 0, 1, stride=1, stride_axis=0)
        base[g * BLOCK:(g + 1) * BLOCK, :LANES] = matrix.astype(BF16)
    base[:, LANES:] = gain_ref[...]
    state = enter_ref[...]
    for step in range(blocks):
        b = blocks - 1 - step if reverse else step
        line = line_of(b)
        low = line.astype(BF16)
        mask = mask_ref[b]
        left = (base[...].reshape(count, BLOCK, LANES + poles) * mask[None]).reshape(
            count * BLOCK, LANES + poles
        )
        right = jnp.concatenate([low, state.astype(BF16)], axis=0)
        result = pick(
            jnp.dot(left, right, preferred_element_type=F32), count, BLOCK, members
        )
        emit(b, line, result)
        if step < blocks - 1:
            gone = leave_ref[...] * alive_ref[b:b + 1, :]
            fresh = pick(
                jnp.dot(gone.astype(BF16), low, preferred_element_type=F32), count, poles, members
            )
            state = across_ref[...] * alive_across_ref[b:b + 1, :] * state + fresh


def forward_kernel(count, poles, members, blocks, query, key, value, skip, lag, gain, mask, leave,
                   alive, across, alive_across, enter, filtered, gated, base):
    def rows(b):
        return pl.ds(b * BLOCK, BLOCK)

    def line_of(b):
        return (key[rows(b), :].astype(F32) * value[rows(b), :].astype(F32)).astype(BF16).astype(F32)

    def emit(b, line, result):
        result = result + skip[...] * line
        filtered[rows(b), :] = result
        gated[rows(b), :] = (query[rows(b), :].astype(F32) * result).astype(BF16)

    convolve(False, count, poles, members, blocks, line_of, emit, lag, gain, mask, leave, alive,
             across, alive_across, enter, base)


def backward_kernel(count, poles, members, blocks, query, key, value, grad_gated, filtered, skip,
                    lag, gain, mask, leave, alive, across, alive_across, enter, grad_query,
                    grad_key, grad_value, base):
    def rows(b):
        return pl.ds(b * BLOCK, BLOCK)

    def line_of(b):
        grad = grad_gated[rows(b), :]
        grad_query[rows(b), :] = (grad * filtered[rows(b), :]).astype(BF16)
        return grad * query[rows(b), :].astype(F32)

    def emit(b, line, result):
        result = result + skip[...] * line
        grad_key[rows(b), :] = (result * value[rows(b), :].astype(F32)).astype(BF16)
        grad_value[rows(b), :] = (result * key[rows(b), :].astype(F32)).astype(BF16)

    convolve(True, count, poles, members, blocks, line_of, emit, lag, gain, mask, leave, alive,
             across, alive_across, enter, base)


def run_conv(kernel, wide, skip, tables, enter, out_types, poles, members):
    rows, channels = wide[0].shape
    count = LANES // members
    blocks = rows // BLOCK
    column = pl.BlockSpec((rows, LANES), lambda j: (0, j))
    lag, gain, mask, leave, alive, across, alive_across = tables
    return pl.pallas_call(
        functools.partial(kernel, count, poles, members, blocks),
        grid=(channels // LANES,),
        in_specs=[column] * len(wide) + [
            pl.BlockSpec((1, LANES), lambda j: (0, j)),
            pl.BlockSpec((count, BLOCK), lambda j: (j, 0)),
            pl.BlockSpec((count * BLOCK, poles), lambda j: (j, 0)),
            pl.BlockSpec((blocks, BLOCK, BLOCK + poles), lambda j: (0, 0, 0)),
            pl.BlockSpec((count * poles, BLOCK), lambda j: (j, 0)),
            pl.BlockSpec((blocks, BLOCK), lambda j: (0, 0)),
            pl.BlockSpec((poles, LANES), lambda j: (0, j)),
            pl.BlockSpec((blocks, LANES), lambda j: (0, 0)),
            pl.BlockSpec((poles, LANES), lambda j: (0, j)),
        ],
        out_specs=[column] * len(out_types),
        out_shape=[jax.ShapeDtypeStruct((rows, channels), kind) for kind in out_types],
        scratch_shapes=[pltpu.VMEM((count * BLOCK, BLOCK + poles), BF16)],
        cost_estimate=pl.CostEstimate(flops=0, bytes_accessed=1 << 20, transcendentals=0),
    )(*wide, skip, lag, gain, mask, leave, alive, across, alive_across, enter)


def swap(value, flip, size):
    return lax.ppermute(value, "ctx", [(i, i ^ flip) for i in range(size)])


def partial_kernel(order_ref, gated_ref, weight_ref, out_ref):
    out_ref[...] = lax.dot_general(
        gated_ref[...], weight_ref[...], (((1,), (1,)), ((), ())), preferred_element_type=F32
    ).astype(BF16)


def partials(order, gated, weights, wide):
    rows, channels = gated.shape
    count = order.shape[0]
    split = 2
    return pl.pallas_call(
        partial_kernel,
        grid_spec=pltpu.PrefetchScalarGridSpec(
            num_scalar_prefetch=1,
            grid=(count, split),
            in_specs=[
                pl.BlockSpec((rows, channels), lambda i, j, order: (0, 0)),
                pl.BlockSpec((wide // split, channels), lambda i, j, order: (order[i] * split + j, 0)),
            ],
            out_specs=pl.BlockSpec((rows, wide // split), lambda i, j, order: (i, j)),
        ),
        out_shape=jax.ShapeDtypeStruct((count * rows, wide), BF16),
        cost_estimate=pl.CostEstimate(flops=0, bytes_accessed=1 << 20, transcendentals=0),
        compiler_params=pltpu.CompilerParams(vmem_limit_bytes=40 << 20),
    )(order, gated, weights)


def tie(value, *earlier):
    return lax.optimization_barrier((value,) + earlier)[0]


MESH = pl.DeviceIdType.MESH


def flipped(me, flip):
    core, x, y = me % 2, me // 2 % 2, me // 4
    core = 1 - core if flip % 2 else core
    x = 1 - x if flip // 2 % 2 else x
    y = 1 - y if flip // 4 else y
    return (y * 2 + x) * 2 + core


def greet(me, z, count):
    barrier = pltpu.get_barrier_semaphore()
    for flip in range(1, 8):
        pl.semaphore_signal(barrier, inc=1, device_id={"ctx": flipped(me, flip)}, device_id_type=MESH)

    @pl.when(z > 0)
    def _():
        pl.semaphore_signal(barrier, inc=1, device_id={"grp": z - 1}, device_id_type=MESH)

    @pl.when(z < count - 1)
    def _():
        pl.semaphore_signal(barrier, inc=1, device_id={"grp": z + 1}, device_id_type=MESH)

    pl.semaphore_wait(barrier, 9 - jnp.where(z == 0, 1, 0) - jnp.where(z == count - 1, 1, 0))


def docs_of(lengths, where):
    start, out = 0, -1
    for i in range(lengths.shape[0]):
        out = out + jnp.where(start <= where, 1, 0)
        start = start + lengths[i]
    return out


def doc_tables(reverse, lengths, me, rows, mask, alive):
    first = me * rows
    shape = (BLOCK, BLOCK)
    down, across = lax.broadcasted_iota(jnp.int32, shape, 0), lax.broadcasted_iota(jnp.int32, shape, 1)
    ordered = down <= across if reverse else down >= across
    crosses = []
    for b in range(rows // BLOCK):
        at = first + b * BLOCK
        entry, left = (at + BLOCK, at) if reverse else (at - 1, at + BLOCK - 1)
        entry, left = docs_of(lengths, entry), docs_of(lengths, left)
        by_row, by_column = docs_of(lengths, at + down), docs_of(lengths, at + across)
        mask[b, :, :LANES] = jnp.where((by_row == by_column) & ordered, 1.0, 0.0).astype(BF16)
        mask[b, :, LANES:] = jnp.where(by_row == entry, 1.0, 0.0).astype(BF16)[:, :mask.shape[2] - LANES]
        alive[b:b + 1, :] = jnp.where(by_column == left, 1.0, 0.0)[:1]
        crosses.append(jnp.where(entry == left, 1.0, 0.0))
    return crosses


def tile_tables(reverse, count, poles, j, rate_col, beta_col, rate, beta, base):
    at = pl.ds(pl.multiple_of(j * LANES, LANES), LANES)
    rates, betas = rate_col[at, :], beta_col[at, :]
    lane = lax.broadcasted_iota(jnp.int32, (LANES, BLOCK), 1)
    lag = lane if reverse else jnp.where(lane == 0, 0, BLOCK - lane)
    response = betas * jnp.exp(-lag.astype(F32) * rates)
    filters = pl.ds(pl.multiple_of(j * count, count), count)
    rate_rows, beta_rows = rate[filters, :], beta[filters, :]
    step = lax.broadcasted_iota(jnp.int32, (BLOCK, poles), 0)
    step = (BLOCK - step if reverse else step + 1).astype(F32)
    for g in range(count):
        row = jnp.sum(response[g * poles:(g + 1) * poles], axis=0, keepdims=True)
        matrix = pltpu.roll(jnp.broadcast_to(row, (BLOCK, LANES)), 0, 1, stride=1, stride_axis=0)
        base[g * BLOCK:(g + 1) * BLOCK, :LANES] = matrix.astype(BF16)
        gain = beta_rows[g:g + 1] * jnp.exp(-step * rate_rows[g:g + 1])
        base[g * BLOCK:(g + 1) * BLOCK, LANES:] = gain.astype(BF16)
    away = lane if reverse else BLOCK - 1 - lane
    return jnp.exp(-away.astype(F32) * rates)


def tile_convolve(reverse, count, poles, members, leave, across, enter, crosses, line_of, emit, mask, alive, base):
    blocks = len(crosses)
    state = enter
    for at in range(blocks):
        b = blocks - 1 - at if reverse else at
        line = line_of(b)
        low = line.astype(BF16)
        left = (base[...].reshape(count, BLOCK, LANES + poles) * mask[b][None]).reshape(
            count * BLOCK, LANES + poles
        )
        right = jnp.concatenate([low, state.astype(BF16)], axis=0)
        emit(b, line, pick(jnp.dot(left, right, preferred_element_type=F32), count, BLOCK, members))
        if at < blocks - 1:
            gone = (leave * alive[b:b + 1, :]).astype(BF16)
            fresh = pick(jnp.dot(gone, low, preferred_element_type=F32), count, poles, members)
            state = across * crosses[b] * state + fresh


def tile_summary(reverse, count, poles, members, lengths, me, rows, rates, line):
    t = lax.broadcasted_iota(jnp.int32, (1, rows), 1)
    edge = me * rows if reverse else me * rows + rows - 1
    kept = jnp.where(docs_of(lengths, me * rows + t) == docs_of(lengths, edge), 1.0, 0.0)
    away = (t if reverse else rows - 1 - t).astype(F32)
    table = (jnp.exp(-away * rates) * kept).astype(BF16)
    return pick(jnp.dot(table, line, preferred_element_type=F32), count, poles, members)


def swap_states(me, states, send, recv):
    copies = [
        pltpu.make_async_remote_copy(
            states.at[0], states.at[flip], send.at[flip], recv.at[flip],
            device_id={"ctx": flipped(me, flip)}, device_id_type=MESH,
        )
        for flip in range(1, 8)
    ]
    for copy in copies:
        copy.start()
    return copies


def entering(reverse, lengths, me, rows, rate_chan, states):
    edge = docs_of(lengths, me * rows + rows if reverse else me * rows - 1)
    total = jnp.zeros(rate_chan.shape, F32)
    for flip in range(1, 8):
        other = flipped(me, flip)
        gap = other - 1 - me if reverse else me - 1 - other
        theirs = docs_of(lengths, other * rows if reverse else other * rows + rows - 1)
        kept = jnp.where((gap >= 0) & (theirs == edge), 1.0, 0.0)
        decay = jnp.exp(-(jnp.maximum(gap, 0) * rows).astype(F32) * rate_chan[...])
        total = total + kept * decay * states[flip].astype(F32)
    return total


def opening_kernel(count, zs, members, lengths, query, key, value, rate_col, beta_col, rate, beta, rate_chan, skip,
                   grad_out, own, lower, upper, whole, filtered, gated, first, base, mask, alive, enter, states,
                   weight, z_send, z_recv, s_send, s_recv, w_send, w_recv, local_sem):
    me, z = lax.axis_index("ctx"), lax.axis_index("grp")
    rows, channels = query.shape
    poles = rate.shape[1]
    tiles = channels // LANES
    height = own.shape[0]
    half = height // 2
    greet(me, z, zs)
    go_up = pltpu.make_async_remote_copy(
        grad_out, lower, z_send.at[0], z_recv.at[0], device_id={"grp": (z + 1) % zs}, device_id_type=MESH
    )
    go_down = pltpu.make_async_remote_copy(
        grad_out, upper, z_send.at[1], z_recv.at[1], device_id={"grp": (z + zs - 1) % zs}, device_id_type=MESH
    )

    @pl.when(z < zs - 1)
    def _():
        go_up.start()

    @pl.when(z > 0)
    def _():
        go_down.start()

    def tile(j):
        return pl.ds(pl.multiple_of(j * LANES, LANES), LANES)

    def product(at, lanes):
        return (key[at, lanes].astype(F32) * value[at, lanes].astype(F32)).astype(BF16)

    def summarize_tile(j, carry):
        states[0, :, tile(j)] = tile_summary(
            False, count, poles, members, lengths, me, rows, rate_col[tile(j), :], product(slice(None), tile(j))
        ).astype(BF16)
        return carry

    lax.fori_loop(0, tiles, summarize_tile, 0)
    state_copies = swap_states(me, states, s_send, s_recv)

    def rows_of(flip, first=0, size=height):
        return pl.ds(pl.multiple_of(flipped(me, flip) * height + first, 16), size)

    def send(number, src, at, flip):
        return pltpu.make_async_remote_copy(
            src, whole.at[at, :], w_send.at[number], w_recv.at[number],
            device_id={"ctx": flipped(me, flip)}, device_id_type=MESH,
        )

    def pass_on(number, at, flip):
        return send(number, whole.at[at, :], at, flip)

    keep_own = pltpu.make_async_copy(own, whole.at[rows_of(0), :], local_sem.at[0])
    keep_own.start()
    by_x, by_y, by_core = send(0, own, rows_of(0), 2), send(1, own, rows_of(0), 4), send(2, own, rows_of(0), 1)
    for copy in (by_x, by_y, by_core):
        copy.start()
    crosses = doc_tables(False, lengths, me, rows, mask, alive)
    for copy in state_copies:
        copy.wait_recv()
    enter[...] = entering(False, lengths, me, rows, rate_chan, states)
    def convolve_tile(j, carry):
        lanes = tile(j)

        def line_of(b):
            return product(pl.ds(b * BLOCK, BLOCK), lanes).astype(F32)

        def emit(b, line, result):
            at = pl.ds(b * BLOCK, BLOCK)
            result = result + skip[:, lanes] * line
            filtered[at, lanes] = result
            gated[at, lanes] = (query[at, lanes].astype(F32) * result).astype(BF16)

        leave = tile_tables(False, count, poles, j, rate_col, beta_col, rate, beta, base)
        across = jnp.exp(-BLOCK * rate_chan[:, lanes])
        tile_convolve(False, count, poles, members, leave, across, enter[:, lanes], crosses, line_of, emit, mask,
                      alive, base)
        return carry

    lax.fori_loop(0, tiles, convolve_tile, 0)
    by_x.wait_recv()
    far_low = pass_on(5, rows_of(2, 0, half), 4)
    far_low.start()
    x_core = pass_on(3, rows_of(2), 1)
    x_core.start()
    by_y.wait_recv()
    far_high = pass_on(6, rows_of(4, half, half), 2)
    far_high.start()
    y_core = pass_on(4, rows_of(4), 1)
    y_core.start()
    far_low.wait_recv()
    low_core = pass_on(7, rows_of(6, 0, half), 1)
    low_core.start()
    far_high.wait_recv()
    high_core = pass_on(8, rows_of(6, half, half), 1)
    high_core.start()
    for copy in (by_core, x_core, y_core, low_core, high_core):
        copy.wait_recv()
    keep_own.wait()
    outermost = jnp.where(z < 2, zs - 1, 0) * (2 * height)
    fetch = pltpu.make_async_copy(
        whole.at[pl.ds(pl.multiple_of(outermost, 16), 2 * height), :], weight, local_sem.at[1]
    )
    fetch.start()
    fetch.wait()
    quarter = rows // 4

    def partial_rows(i, carry):
        at = pl.ds(pl.multiple_of(i * quarter, quarter), quarter)
        first[at, :] = lax.dot_general(
            gated[at, :], weight[...], (((1,), (1,)), ((), ())), preferred_element_type=F32
        ).astype(BF16)
        return carry

    lax.fori_loop(0, 4, partial_rows, 0)
    for copy in state_copies + [by_x, by_y, by_core, far_low, far_high, x_core, y_core, low_core, high_core]:
        copy.wait_send()

    @pl.when(z < zs - 1)
    def _():
        go_up.wait_send()
        go_down.wait_recv()

    @pl.when(z > 0)
    def _():
        go_down.wait_send()
        go_up.wait_recv()


def opening(zs, lengths, query, key, value, rate, beta, skip, grad_out, own, wide):
    rows, channels = query.shape
    filters, poles = rate.shape
    members = channels // filters
    count = LANES // members
    rate_chan = jnp.repeat(rate.T, members, axis=1)
    vmem, anywhere = pl.BlockSpec(memory_space=pltpu.VMEM), pl.BlockSpec(memory_space=pl.ANY)
    moved = jax.ShapeDtypeStruct((rows, channels), BF16)
    dma = pltpu.SemaphoreType.DMA
    return pl.pallas_call(
        functools.partial(opening_kernel, count, zs, members),
        in_specs=[pl.BlockSpec(memory_space=pltpu.SMEM)] + [vmem] * 9 + [anywhere] * 2,
        out_specs=[anywhere] * 3 + [vmem] * 3,
        out_shape=[
            moved, moved, jax.ShapeDtypeStruct((own.shape[0] * 8, channels), BF16),
            jax.ShapeDtypeStruct((rows, channels), F32), moved, jax.ShapeDtypeStruct((rows, wide), BF16),
        ],
        scratch_shapes=[
            pltpu.VMEM((count * BLOCK, BLOCK + poles), BF16),
            pltpu.VMEM((rows // BLOCK, BLOCK, BLOCK + poles), BF16),
            pltpu.VMEM((rows // BLOCK, LANES), F32),
            pltpu.VMEM((poles, channels), F32),
            pltpu.VMEM((8, poles, channels), BF16),
            pltpu.VMEM((wide, channels), BF16),
            dma((2,)), dma((2,)), dma((8,)), dma((8,)), dma((9,)), dma((9,)), dma((2,)),
        ],
        compiler_params=pltpu.CompilerParams(collective_id=1, has_side_effects=True, vmem_limit_bytes=50 << 20),
        cost_estimate=pl.CostEstimate(flops=1 << 34, bytes_accessed=24 << 20, transcendentals=0),
    )(lengths, query, key, value, rate.reshape(-1, 1), beta.reshape(-1, 1), rate, beta, rate_chan, skip, grad_out, own)


SENT = ((3, 3, 0, 0), (2, 2, 1, 1), (1, 0, 3, 2), (0, 1, 2, 3))
GOT = ((0, 1, 2, 3), (1, 0, 3, 2), (2, 2, 1, 1), (3, 3, 0, 0))


def by_place(table, where):
    out = jnp.int32(table[0])
    for i, value in enumerate(table[1:], 1):
        out = jnp.where(where == i, jnp.int32(value), out)
    return out


def middle_kernel(zs, own, gated, lower, upper, first, whole, last, sent_up, sent_down, newest, slope, mine0, mine1,
                  mine2, theirs0, theirs1, theirs2, weights, block, came, second, parts, terms, total, z_send, z_recv,
                  fetch_sem, block_sem, out_sem):
    me, z = lax.axis_index("ctx"), lax.axis_index("grp")
    rows, channels = gated.shape
    wide = weights.shape[1]
    height = wide // 2
    low1, up1, low2, up2 = (came.at[i] for i in range(4))
    greet(me, z, zs)

    def leave_for(way, r, src):
        up = way == 0
        return pltpu.make_async_remote_copy(
            src, came.at[2 * r + way], z_send.at[r, way], z_recv.at[r, way],
            device_id={"grp": (z + 1) % zs if up else (z + zs - 1) % zs}, device_id_type=MESH,
        )

    inner_up, inner_down = (z > 0) & (z < zs - 1), (z > 0) & (z < zs - 1)
    pl.when(z == 0)(leave_for(0, 0, first).start)
    pl.when(inner_up)(leave_for(0, 0, lower).start)
    pl.when(z == zs - 1)(leave_for(1, 0, first).start)
    pl.when(inner_down)(leave_for(1, 0, upper).start)

    fetches = []
    for i, table in enumerate((SENT[1], SENT[2], SENT[3])):
        at = pl.multiple_of(by_place(table, z) * wide, 16)
        fetches.append(pltpu.make_async_copy(whole.at[pl.ds(at, wide), :], weights.at[i], fetch_sem.at[i]))
        fetches[-1].start()

    def take(slot, src):
        return pltpu.make_async_copy(src, block.at[slot], block_sem.at[slot])

    odd = z % 2 == 1
    pl.when(odd)(take(0, lower).start)
    pl.when(jnp.logical_not(odd))(take(0, upper).start)
    pl.when(z == 1)(take(1, upper).start)
    pl.when(z == 2)(take(1, lower).start)
    quarter = rows // 4

    def each_quarter(work):
        def run(i, carry):
            work(pl.ds(pl.multiple_of(i * quarter, quarter), quarter))
            return carry

        lax.fori_loop(0, 4, run, 0)

    def partial(weight, out):
        def work(at):
            out[at, :] = lax.dot_general(
                gated[at, :], weight[...], (((1,), (1,)), ((), ())), preferred_element_type=F32
            ).astype(BF16)
        each_quarter(work)

    copies = []

    def write_out(src, dst):
        copies.append(pltpu.make_async_copy(src, dst, out_sem.at[len(copies)]))
        copies[-1].start()

    def use(number, grads, weight, mine, theirs):
        for side, core, out in ((0, 1 - me % 2, theirs), (1, me % 2, mine)):
            features = pl.ds(pl.multiple_of(core * height, height), height)
            held = terms.at[2 * number + side]

            def columns(i, carry, features=features, held=held):
                at = pl.ds(pl.multiple_of(i * quarter, quarter), quarter)
                held[:, at] = lax.dot_general(
                    grads[:, features], gated[:, at], (((0,), (0,)), ((), ())), preferred_element_type=F32
                ).astype(BF16)
                return carry

            lax.fori_loop(0, channels // quarter, columns, 0)
            write_out(held, out)

        def work(at):
            part = jnp.dot(grads[at, :], weight[...], preferred_element_type=F32)
            total[at, :] = part if number == 0 else total[at, :] + part
        each_quarter(work)

    fetches[0].wait()
    partial(weights.at[0], second)
    fetches[1].wait()
    partial(weights.at[1], parts.at[0])
    fetches[2].wait()
    partial(weights.at[2], parts.at[1])
    write_out(parts.at[1], last)
    use(0, own, weights.at[2], mine0, theirs0)
    take(0, lower).wait()
    use(1, block.at[0], weights.at[1], mine1, theirs1)

    def arrive(r):
        pl.when(z > 0)(leave_for(0, r, lower).wait_recv)
        pl.when(z < zs - 1)(leave_for(1, r, upper).wait_recv)

    def left(r):
        pl.when(z < zs - 1)(leave_for(0, r, lower).wait_send)
        pl.when(z > 0)(leave_for(1, r, upper).wait_send)

    def add_to(arrived, mine):
        def work(at):
            arrived[at, :] = (arrived[at, :].astype(F32) + mine[at, :].astype(F32)).astype(BF16)
        return lambda: each_quarter(work)

    arrive(0)
    left(0)
    load_first = pltpu.make_async_copy(first, parts.at[2], fetch_sem.at[3])
    load_first.start()
    load_first.wait()
    pl.when(z == 1)(add_to(low1, parts.at[2]))
    pl.when(z == 2)(add_to(up1, parts.at[2]))
    pl.when(z == 0)(leave_for(0, 1, second).start)
    pl.when(inner_up)(leave_for(0, 1, low1).start)
    pl.when(z == zs - 1)(leave_for(1, 1, second).start)
    pl.when(inner_down)(leave_for(1, 1, up1).start)
    pl.when(z == 0)(take(1, up1).start)
    pl.when(z == zs - 1)(take(1, low1).start)
    take(1, lower).wait()
    use(2, block.at[1], weights.at[0], mine2, theirs2)
    write_out(total, slope)
    arrive(1)
    left(1)
    third = parts.at[0]
    pl.when(z == 1)(add_to(low2, second))
    pl.when(z == 2)(add_to(low2, third))
    pl.when(z == 1)(add_to(up2, third))
    pl.when(z == 2)(add_to(up2, second))

    def to_next(src, dst, sem):
        return pltpu.make_async_copy(src, dst, block_sem.at[sem])

    pl.when(z == 0)(to_next(third, sent_up, 2).start)
    pl.when(z > 0)(to_next(low2, sent_up, 2).start)
    pl.when(z == zs - 1)(to_next(third, sent_down, 3).start)
    pl.when(z < zs - 1)(to_next(up2, sent_down, 3).start)
    for place, src in enumerate((up2, up1, low1, low2)):
        pl.when(z == place)(to_next(src, newest, 4).start)
    to_next(third, sent_up, 2).wait()
    to_next(third, sent_down, 3).wait()
    to_next(third, newest, 4).wait()
    for copy in copies:
        copy.wait()


def middle(zs, own, gated, lower, upper, first, whole, wide):
    rows, channels = gated.shape
    vmem, anywhere = pl.BlockSpec(memory_space=pltpu.VMEM), pl.BlockSpec(memory_space=pl.ANY)
    moved = jax.ShapeDtypeStruct((rows, channels), BF16)
    half = jax.ShapeDtypeStruct((wide // 2, channels), BF16)
    dma = pltpu.SemaphoreType.DMA
    return pl.pallas_call(
        functools.partial(middle_kernel, zs),
        in_specs=[vmem] * 2 + [anywhere] * 4,
        out_specs=[anywhere] * 11,
        out_shape=[moved] * 4 + [jax.ShapeDtypeStruct((rows, channels), F32)] + [half] * 6,
        scratch_shapes=[
            pltpu.VMEM((3, wide, channels), BF16),
            pltpu.VMEM((2, rows, wide), BF16),
            pltpu.VMEM((4, rows, wide), BF16),
            pltpu.VMEM((rows, wide), BF16),
            pltpu.VMEM((3, rows, wide), BF16),
            pltpu.VMEM((6, wide // 2, channels), BF16),
            pltpu.VMEM((rows, channels), F32),
            dma((2, 2)), dma((2, 2)), dma((4,)), dma((5,)), dma((8,)),
        ],
        compiler_params=pltpu.CompilerParams(collective_id=3, has_side_effects=True, vmem_limit_bytes=56 << 20),
        cost_estimate=pl.CostEstimate(flops=1 << 34, bytes_accessed=24 << 20, transcendentals=0),
    )(own, gated, lower, upper, first, whole)


def closing_kernel(count, zs, members, lengths, query, key, value, rate_col, beta_col, rate, beta, rate_chan, skip,
                   block, gated, slope, filtered, mine0, mine1, mine2, theirs0, theirs1, theirs2, sent_up, sent_down,
                   whole, lower, upper, grad_query, grad_key, grad_value, grad_proj, grad, base, mask, alive, enter,
                   states, weight, theirs3, sums, from_core, near, far, z_send, z_recv, s_send, s_recv, c_send,
                   c_recv, n_send, n_recv, f_send, f_recv, local_sem):
    me, z = lax.axis_index("ctx"), lax.axis_index("grp")
    rows, channels = query.shape
    poles = rate.shape[1]
    tiles = channels // LANES
    height = mine0.shape[0]
    half = channels // 2
    greet(me, z, zs)
    go_up = pltpu.make_async_remote_copy(
        sent_up, lower, z_send.at[0], z_recv.at[0], device_id={"grp": (z + 1) % zs}, device_id_type=MESH
    )
    go_down = pltpu.make_async_remote_copy(
        sent_down, upper, z_send.at[1], z_recv.at[1], device_id={"grp": (z + zs - 1) % zs}, device_id_type=MESH
    )

    @pl.when(z < zs - 1)
    def _():
        go_up.start()

    @pl.when(z > 0)
    def _():
        go_down.start()

    def across_core(number, src):
        copy = pltpu.make_async_remote_copy(
            src, from_core.at[number], c_send.at[number], c_recv.at[number],
            device_id={"ctx": flipped(me, 1)}, device_id_type=MESH,
        )
        copy.start()
        return copy

    core_copies = [across_core(number, src) for number, src in enumerate((theirs0, theirs1, theirs2))]
    newest = by_place(GOT[3], z)
    fetch = pltpu.make_async_copy(
        whole.at[pl.ds(pl.multiple_of(newest * (2 * height), 16), 2 * height), :], weight, local_sem.at[0]
    )
    fetch.start()
    fetch.wait()

    def tile(j):
        return pl.ds(pl.multiple_of(j * LANES, LANES), LANES)

    quarter = rows // 4

    def slope_rows(i, carry):
        at = pl.ds(pl.multiple_of(i * quarter, quarter), quarter)
        grad[at, :] = slope[at, :] + jnp.dot(block[at, :], weight[...], preferred_element_type=F32)
        return carry

    lax.fori_loop(0, 4, slope_rows, 0)

    def summarize_tile(j, carry):
        line = (grad[:, tile(j)] * query[:, tile(j)].astype(F32)).astype(BF16)
        states[0, :, tile(j)] = tile_summary(
            True, count, poles, members, lengths, me, rows, rate_col[tile(j), :], line
        ).astype(BF16)
        return carry

    lax.fori_loop(0, tiles, summarize_tile, 0)
    state_copies = swap_states(me, states, s_send, s_recv)
    span = channels // 4

    def term(core, out):
        features = pl.ds(pl.multiple_of(core * height, height), height)

        def columns(i, carry):
            at = pl.ds(pl.multiple_of(i * span, span), span)
            out[:, at] = lax.dot_general(
                block[:, features], gated[:, at], (((0,), (0,)), ((), ())), preferred_element_type=F32
            ).astype(BF16)
            return carry

        lax.fori_loop(0, 4, columns, 0)

    term(1 - me % 2, theirs3)
    core_copies.append(across_core(3, theirs3))
    term(me % 2, sums.at[3])
    crosses = doc_tables(True, lengths, me, rows, mask, alive)
    x, y = me // 2 % 2, me // 4
    low, high = pl.ds(0, half), pl.ds(half, half)

    def hop_copy(stage, number, columns, flip, sems, into):
        return pltpu.make_async_remote_copy(
            sums.at[number, :, columns], into.at[number, :, columns], sems[0].at[stage, number],
            sems[1].at[stage, number], device_id={"ctx": flipped(me, flip)}, device_id_type=MESH,
        )

    routes = []
    for number, mine in enumerate((mine0, mine1, mine2, None)):
        owner = by_place(GOT[number], z)
        off_x, off_y = owner % 2 != x, owner // 2 != y
        core_copies[number].wait_recv()
        own = sums[number] if mine is None else mine[...]
        sums[number] = (own.astype(F32) + from_core[number].astype(F32)).astype(BF16)
        near_low = hop_copy(0, number, low, 2, (n_send, n_recv), near)
        near_high = hop_copy(1, number, high, 4, (n_send, n_recv), near)
        far_low = hop_copy(0, number, low, 4, (f_send, f_recv), far)
        far_high = hop_copy(1, number, high, 2, (f_send, f_recv), far)
        pl.when(off_x)(near_low.start)
        pl.when(off_y)(near_high.start)
        routes.append((number, off_x, off_y, near_low, near_high, far_low, far_high))

    for copy in state_copies:
        copy.wait_recv()
    enter[...] = entering(True, lengths, me, rows, rate_chan, states)

    def convolve_tile(j, carry):
        lanes = tile(j)

        def line_of(b):
            at = pl.ds(b * BLOCK, BLOCK)
            line = grad[at, lanes]
            grad_query[at, lanes] = (line * filtered[at, lanes]).astype(BF16)
            return line * query[at, lanes].astype(F32)

        def emit(b, line, result):
            at = pl.ds(b * BLOCK, BLOCK)
            result = result + skip[:, lanes] * line
            grad_key[at, lanes] = (result * value[at, lanes].astype(F32)).astype(BF16)
            grad_value[at, lanes] = (result * key[at, lanes].astype(F32)).astype(BF16)

        leave = tile_tables(True, count, poles, j, rate_col, beta_col, rate, beta, base)
        across = jnp.exp(-BLOCK * rate_chan[:, lanes])
        tile_convolve(True, count, poles, members, leave, across, enter[:, lanes], crosses, line_of, emit, mask,
                      alive, base)
        return carry

    early = tiles * 3 // 4
    lax.fori_loop(0, early, convolve_tile, 0)

    def add_near(number, columns, copy):
        def run():
            copy.wait_recv()
            total = sums[number, :, columns].astype(F32) + near[number, :, columns].astype(F32)
            sums[number, :, columns] = total.astype(BF16)
        return run

    for number, off_x, off_y, near_low, near_high, far_low, far_high in routes:
        pl.when(jnp.logical_not(off_x))(add_near(number, low, near_low))
        pl.when(jnp.logical_not(off_y))(add_near(number, high, near_high))
        pl.when(jnp.logical_not(off_x) & off_y)(far_low.start)
        pl.when(jnp.logical_not(off_y) & off_x)(far_high.start)
    lax.fori_loop(early, tiles, convolve_tile, 0)

    def finish(number, far_low, far_high):
        def run():
            far_low.wait_recv()
            far_high.wait_recv()
            grad_proj[...] = sums[number].astype(F32) + far[number].astype(F32)
        return run

    for number, off_x, off_y, near_low, near_high, far_low, far_high in routes:
        on_x, on_y = jnp.logical_not(off_x), jnp.logical_not(off_y)
        pl.when(on_x & on_y)(finish(number, far_low, far_high))
        pl.when(off_x)(near_low.wait_send)
        pl.when(off_y)(near_high.wait_send)
        pl.when(on_x & off_y)(far_low.wait_send)
        pl.when(on_y & off_x)(far_high.wait_send)
    for copy in state_copies + core_copies:
        copy.wait_send()

    @pl.when(z < zs - 1)
    def _():
        go_up.wait_send()
        go_down.wait_recv()

    @pl.when(z > 0)
    def _():
        go_down.wait_send()
        go_up.wait_recv()


def closing(zs, lengths, query, key, value, rate, beta, skip, block, gated, slope, filtered, mine, theirs, sent, whole):
    rows, channels = query.shape
    filters, poles = rate.shape
    members = channels // filters
    count = LANES // members
    height = mine[0].shape[0]
    rate_chan = jnp.repeat(rate.T, members, axis=1)
    vmem, anywhere = pl.BlockSpec(memory_space=pltpu.VMEM), pl.BlockSpec(memory_space=pl.ANY)
    moved = jax.ShapeDtypeStruct((rows, channels), BF16)
    dma = pltpu.SemaphoreType.DMA
    return pl.pallas_call(
        functools.partial(closing_kernel, count, zs, members),
        in_specs=[pl.BlockSpec(memory_space=pltpu.SMEM)] + [vmem] * 16 + [anywhere] * 6,
        out_specs=[anywhere] * 2 + [vmem] * 4,
        out_shape=[moved] * 5 + [jax.ShapeDtypeStruct((height, channels), F32)],
        scratch_shapes=[
            pltpu.VMEM((rows, channels), F32),
            pltpu.VMEM((count * BLOCK, BLOCK + poles), BF16),
            pltpu.VMEM((rows // BLOCK, BLOCK, BLOCK + poles), BF16),
            pltpu.VMEM((rows // BLOCK, LANES), F32),
            pltpu.VMEM((poles, channels), F32),
            pltpu.VMEM((8, poles, channels), BF16),
            pltpu.VMEM((2 * height, channels), BF16),
            pltpu.VMEM((height, channels), BF16),
        ] + [pltpu.VMEM((4, height, channels), BF16)] * 4 + [
            dma((2,)), dma((2,)), dma((8,)), dma((8,)), dma((4,)), dma((4,)), dma((2, 4)), dma((2, 4)), dma((2, 4)),
            dma((2, 4)), dma((1,)),
        ],
        compiler_params=pltpu.CompilerParams(collective_id=2, has_side_effects=True, vmem_limit_bytes=60 << 20),
        cost_estimate=pl.CostEstimate(flops=1 << 34, bytes_accessed=24 << 20, transcendentals=0),
    )(
        lengths, query, key, value, rate.reshape(-1, 1), beta.reshape(-1, 1), rate, beta, rate_chan, skip, block, gated,
        slope, filtered, *mine, *theirs, *sent, whole,
    )


def local(
    query_in, key_in, value_in, residues, decay_time, skip_gain, out_proj, doc_lengths, grad_out
):
    rows, channels = query_in.shape
    filters, poles = residues.shape
    members = channels // filters
    blocks = rows // BLOCK
    size, me = lax.axis_size("ctx"), lax.axis_index("ctx")
    count, z = lax.axis_size("grp"), lax.axis_index("grp")
    assert count == 4
    up = [(i, i + 1) for i in range(count - 1)]
    down = [(i + 1, i) for i in range(count - 1)]

    def exchange(up_value, down_value):
        return lax.ppermute(up_value, "grp", up), lax.ppermute(down_value, "grp", down)

    halves = (slice(0, rows),)
    lower = [[None] * count for _ in halves]
    upper = [[None] * count for _ in halves]
    docs = jnp.arange(doc_lengths.shape[0])
    starts = jnp.sum(jnp.where(docs[None, :] < docs[:, None], doc_lengths[None, :], 0), axis=1)
    flat_ids = doc_index(starts, me * rows + jnp.arange(rows, dtype=jnp.int32))
    ids = flat_ids.reshape(blocks, BLOCK)
    firsts, lasts = ids[:, 0], ids[:, -1]
    before = doc_index(starts, me * rows - 1 + BLOCK * jnp.arange(blocks + 1, dtype=jnp.int32))
    after = doc_index(starts, me * rows + BLOCK * jnp.arange(1, blocks + 1, dtype=jnp.int32))
    ends = doc_index(starts, rows * jnp.arange(1, size + 1, dtype=jnp.int32) - 1)
    opens = doc_index(starts, rows * jnp.arange(size, dtype=jnp.int32))
    rate = 1.0 / decay_time
    beta = residues * jnp.sqrt(-jnp.expm1(-2.0 * rate))
    lags = jnp.arange(BLOCK, dtype=F32)
    rate_chan = jnp.repeat(rate.T, members, axis=1)
    across = jnp.exp(-BLOCK * rate_chan)
    place = jnp.arange(BLOCK)
    causal = place[:, None] >= place[None, :]
    steps = jnp.arange(rows, dtype=F32)

    def mask_of(ids, order, alive):
        same = ids[:, :, None] == ids[:, None, :]
        tail = jnp.broadcast_to(alive[:, :, None], (blocks, BLOCK, poles))
        return jnp.concatenate([same & order[None], tail], axis=2).astype(BF16)

    def spread(flags):
        return jnp.broadcast_to(flags.astype(F32)[:, None], (blocks, LANES))

    def response_of(rate, beta):
        return jnp.sum(beta[:, :, None] * jnp.exp(-lags[None, None, :] * rate[:, :, None]), axis=1)

    def summary_table(rate, distance, kept):
        table = jnp.exp(-distance[None, :] * rate.reshape(-1, 1))
        return (table * kept[None, :]).astype(BF16)

    def gain_of(rate, beta, distance):
        table = beta[:, None, :] * jnp.exp(-distance[None, :, None] * rate[:, None, :])
        return table.reshape(-1, poles).astype(BF16)

    def forward_tables(rate, beta, ids):
        response = response_of(rate, beta)
        mirrored = jnp.concatenate([response[:, :1], response[:, :0:-1]], axis=1)
        return (
            mirrored,
            gain_of(rate, beta, lags + 1.0),
            mask_of(ids, causal, ids == before[:blocks, None]),
            jnp.exp(-(BLOCK - 1.0 - lags)[None, :] * rate.reshape(-1, 1)),
            (ids == lasts[:, None]).astype(F32),
            across,
            spread(before[:blocks] == lasts),
        )

    def backward_tables(rate, beta, ids):
        return (
            response_of(rate, beta),
            gain_of(rate, beta, BLOCK - lags),
            mask_of(ids, causal.T, ids == after[:, None]),
            jnp.exp(-lags[None, :] * rate.reshape(-1, 1)),
            (ids == firsts[:, None]).astype(F32),
            across,
            spread(after == firsts),
        )

    def incoming(state, distance, alive):
        everything = lax.all_gather(state, "ctx").astype(F32)
        gap = jnp.maximum(distance, 0).astype(F32) * rows
        weight = jnp.exp(-gap[:, None, None] * rate_chan[None])
        kept = (alive & (distance >= 0))[:, None, None]
        return jnp.sum(jnp.where(kept, weight * everything, 0.0), axis=0)

    devices = jnp.arange(size, dtype=jnp.int32)
    skip = skip_gain[None, :]
    wide = out_proj.shape[0] * size // count
    order = jnp.stack([by_place(table, z) for table in SENT])

    def forward(query_in, key_in, value_in, out_proj, rate, beta, ids, skip):
        whole_leave = summary_table(rate, rows - 1.0 - steps, flat_ids == flat_ids[-1])
        state = summarize(key_in, value_in, whole_leave, poles, members)
        enter = incoming(state, me - 1 - devices, ends == before[0])
        filtered, gated = run_conv(
            forward_kernel, (query_in, key_in, value_in), skip, forward_tables(rate, beta, ids), enter,
            (F32, BF16), poles, members
        )
        gathered = lax.all_gather(out_proj, "ctx", axis=0, tiled=True)
        return filtered, gated, gathered, partials(order[:1], gated, gathered, wide)

    if size == 8:
        lower[0][0], upper[0][0], gathered, filtered, gated, first = opening(
            count, doc_lengths, query_in, key_in, value_in, rate, beta, skip, grad_out, out_proj, wide
        )
    else:
        lower[0][0], upper[0][0] = exchange(grad_out, grad_out)
        filtered, gated, gathered, first = forward(query_in, key_in, value_in, out_proj, rate, beta, ids, skip)
    odd = z % 2 == 1
    outer = (z == 0) | (z == 3)
    none = jnp.zeros((), BF16)

    if size == 8:
        last, sent_up, sent_down, block, grad_gated, *terms = middle(
            count, grad_out, gated, lower[0][0], upper[0][0], first, gathered, wide
        )
        came_up, came_down, grad_query, grad_key, grad_value, grad_proj = closing(
            count, doc_lengths, query_in, key_in, value_in, rate, beta, skip, block, gated, grad_gated, filtered,
            terms[:3], terms[3:], (sent_up, sent_down), gathered
        )
        came_up, came_down = jnp.where(z == 0, none, came_up), jnp.where(z == count - 1, none, came_down)
        mixed_out = (last.astype(F32) + came_up.astype(F32) + came_down.astype(F32)).astype(BF16)
        return (mixed_out, grad_query, grad_key, grad_value, grad_proj)

    def weights(which):
        return lax.dynamic_slice_in_dim(gathered, which * wide, wide, axis=0)

    def add(came, mine):
        return (came.astype(F32) + mine.astype(F32)).astype(BF16)

    def advance(r, mine_up, mine_down, *earlier):
        out = ()
        for h, part in enumerate(halves):
            *came, _ = lax.optimization_barrier((lower[h][r - 1], upper[h][r - 1], earlier))
            came = jnp.where(z == 0, none, came[0]), jnp.where(z == count - 1, none, came[1])
            sent = lax.optimization_barrier((add(came[0], mine_up(part)), add(came[1], mine_down(part))))
            lower[h][r], upper[h][r] = exchange(*sent)
            out += sent
        return out

    sent = advance(
        1,
        lambda part: jnp.where(z == 0, first[part], none),
        lambda part: jnp.where(z == 3, first[part], none),
        first,
    )
    more = partials(tie(order, *sent)[1:], gated, gathered, wide)
    second, third, last = more[:rows], more[rows:2 * rows], more[2 * rows:]

    def join(sources, r):
        return jnp.concatenate([source[r] for source in sources], axis=0)

    contract = (((0,), (0,)), ((), ()))
    terms = []

    def terms_of(block, owners):
        which = by_place(owners, z)
        terms.append((which, lax.dot_general(block, gated, contract, preferred_element_type=F32).astype(BF16)))
        return terms[-1][1:]

    def slope(block, owners):
        return jnp.dot(block, weights(by_place(owners, z)), preferred_element_type=F32)

    rate_b, beta_b, ids_b, _ = lax.optimization_barrier((rate, beta, ids, more))
    tables_b = backward_tables(rate_b, beta_b, ids_b)
    whole_leave_rev = summary_table(rate_b, steps, flat_ids == flat_ids[0])

    own = tie(grad_out, more, *sent)
    done0 = terms_of(own, GOT[0])
    grad_gated = slope(own, GOT[0])
    came = lax.optimization_barrier((join(lower, 0), join(upper, 0), grad_gated))
    block = jnp.where(odd, came[0], came[1])
    done1 = terms_of(block, GOT[1])
    grad_gated = grad_gated + slope(block, GOT[1])
    sent = advance(
        2,
        lambda part: jnp.where(z == 0, second[part], jnp.where(z == 1, first[part], none)),
        lambda part: jnp.where(z == 3, second[part], jnp.where(z == 2, first[part], none)),
        more, grad_gated, *done0, *done1,
    )
    up0, up1, low0, low1, *_ = lax.optimization_barrier(
        (join(upper, 0), join(upper, 1), join(lower, 0), join(lower, 1), grad_gated, sent)
    )
    block = jnp.where(z < 2, jnp.where(outer, up1, up0), jnp.where(outer, low1, low0))
    done2 = terms_of(block, GOT[2])
    grad_gated = grad_gated + slope(block, GOT[2])
    for_up = jnp.where(z == 1, second, jnp.where(z == 3, none, third))
    for_down = jnp.where(z == 2, second, jnp.where(z == 0, none, third))
    sent = advance(
        3,
        lambda part: jnp.where(z == 1, second[part], jnp.where(z == 3, none, third[part])),
        lambda part: jnp.where(z == 2, second[part], jnp.where(z == 0, none, third[part])),
        grad_gated, terms[0][1], terms[1][1], *done2,
    )
    up1, up2, low1, low2, *_ = lax.optimization_barrier(
        (join(upper, 1), join(upper, 2), join(lower, 1), join(lower, 2), grad_gated, done2, sent)
    )
    block = jnp.where(z < 2, jnp.where(outer, up2, up1), jnp.where(outer, low2, low1))
    done3 = terms_of(block, GOT[3])
    grad_gated = grad_gated + slope(tie(block, *done3), GOT[3])
    term = jnp.zeros((wide * count, channels), BF16)
    for which, value in terms:
        term = lax.dynamic_update_slice(term, value, (which * wide, 0))
    grad_proj = lax.psum_scatter(term, "ctx", scatter_dimension=0, tiled=True).astype(F32)
    state = summarize(grad_gated, query_in, whole_leave_rev, poles, members)
    leaving = incoming(state, devices - 1 - me, opens == after[-1])
    grad_query, grad_key, grad_value = run_conv(
        backward_kernel, (query_in, key_in, value_in, grad_gated, filtered), skip, tables_b,
        leaving, (BF16, BF16, BF16), poles, members
    )
    mixed_out = (last.astype(F32) + join(lower, 3).astype(F32) + join(upper, 3).astype(F32)).astype(BF16)
    return (mixed_out, grad_query, grad_key, grad_value, grad_proj)


def solution(mesh):
    return jax.shard_map(
        local,
        mesh=mesh,
        in_specs=(
            P("ctx", "grp"),
            P("ctx", "grp"),
            P("ctx", "grp"),
            P("grp", None),
            P("grp", None),
            P("grp"),
            P("ctx", "grp"),
            P(),
            P("ctx", "grp"),
        ),
        out_specs=(
            P("ctx", "grp"),
            P("ctx", "grp"),
            P("ctx", "grp"),
            P("ctx", "grp"),
            P("ctx", "grp"),
        ),
        check_vma=False,
    )
```

```python
import functools

import jax
import jax.numpy as jnp
from jax import lax
from jax.experimental import pallas as pl
from jax.experimental.pallas import tpu as pltpu
from jax.sharding import PartitionSpec as P

LANES = 128
BLOCK = 128
F32 = jnp.float32
BF16 = jnp.bfloat16


def doc_index(starts, where_now):
    return jnp.sum((starts[None, :] <= where_now[:, None]).astype(jnp.int32), axis=1) - 1


def pick(stacked, count, rows, members):
    lane_filter = lax.broadcasted_iota(jnp.int32, (rows, LANES), 1) // members
    out = stacked[:rows]
    for g in range(1, count):
        out = jnp.where(lane_filter == g, stacked[g * rows:(g + 1) * rows], out)
    return out


def summary_kernel(count, poles, members, a_ref, b_ref, leave_ref, out_ref):
    line = (a_ref[...].astype(F32) * b_ref[...].astype(F32)).astype(BF16)
    stacked = jnp.dot(leave_ref[...], line, preferred_element_type=F32)
    out_ref[...] = pick(stacked, count, poles, members).astype(out_ref.dtype)


def summarize(a, b, leave, poles, members):
    rows, channels = a.shape
    count = LANES // members
    return pl.pallas_call(
        functools.partial(summary_kernel, count, poles, members),
        grid=(channels // LANES,),
        in_specs=[
            pl.BlockSpec((rows, LANES), lambda j: (0, j)),
            pl.BlockSpec((rows, LANES), lambda j: (0, j)),
            pl.BlockSpec((count * poles, rows), lambda j: (j, 0)),
        ],
        out_specs=pl.BlockSpec((poles, LANES), lambda j: (0, j)),
        out_shape=jax.ShapeDtypeStruct((poles, channels), BF16),
        cost_estimate=pl.CostEstimate(flops=0, bytes_accessed=1 << 20, transcendentals=0),
    )(a, b, leave)


def convolve(reverse, count, poles, members, blocks, line_of, emit, lag_ref, gain_ref, mask_ref,
             leave_ref, alive_ref, across_ref, alive_across_ref, enter_ref, base):
    for g in range(count):
        row = jnp.broadcast_to(lag_ref[g:g + 1, :], (BLOCK, LANES))
        matrix = pltpu.roll(row, 0, 1, stride=1, stride_axis=0)
        base[g * BLOCK:(g + 1) * BLOCK, :LANES] = matrix.astype(BF16)
    base[:, LANES:] = gain_ref[...]
    state = enter_ref[...]
    for step in range(blocks):
        b = blocks - 1 - step if reverse else step
        line = line_of(b)
        low = line.astype(BF16)
        mask = mask_ref[b]
        left = (base[...].reshape(count, BLOCK, LANES + poles) * mask[None]).reshape(
            count * BLOCK, LANES + poles
        )
        right = jnp.concatenate([low, state.astype(BF16)], axis=0)
        result = pick(
            jnp.dot(left, right, preferred_element_type=F32), count, BLOCK, members
        )
        emit(b, line, result)
        if step < blocks - 1:
            gone = leave_ref[...] * alive_ref[b:b + 1, :]
            fresh = pick(
                jnp.dot(gone.astype(BF16), low, preferred_element_type=F32), count, poles, members
            )
            state = across_ref[...] * alive_across_ref[b:b + 1, :] * state + fresh


def forward_kernel(count, poles, members, blocks, query, key, value, skip, lag, gain, mask, leave,
                   alive, across, alive_across, enter, filtered, gated, base):
    def rows(b):
        return pl.ds(b * BLOCK, BLOCK)

    def line_of(b):
        return (key[rows(b), :].astype(F32) * value[rows(b), :].astype(F32)).astype(BF16).astype(F32)

    def emit(b, line, result):
        result = result + skip[...] * line
        filtered[rows(b), :] = result
        gated[rows(b), :] = (query[rows(b), :].astype(F32) * result).astype(BF16)

    convolve(False, count, poles, members, blocks, line_of, emit, lag, gain, mask, leave, alive,
             across, alive_across, enter, base)


def backward_kernel(count, poles, members, blocks, query, key, value, grad_gated, filtered, skip,
                    lag, gain, mask, leave, alive, across, alive_across, enter, grad_query,
                    grad_key, grad_value, base):
    def rows(b):
        return pl.ds(b * BLOCK, BLOCK)

    def line_of(b):
        grad = grad_gated[rows(b), :]
        grad_query[rows(b), :] = (grad * filtered[rows(b), :]).astype(BF16)
        return grad * query[rows(b), :].astype(F32)

    def emit(b, line, result):
        result = result + skip[...] * line
        grad_key[rows(b), :] = (result * value[rows(b), :].astype(F32)).astype(BF16)
        grad_value[rows(b), :] = (result * key[rows(b), :].astype(F32)).astype(BF16)

    convolve(True, count, poles, members, blocks, line_of, emit, lag, gain, mask, leave, alive,
             across, alive_across, enter, base)


def run_conv(kernel, wide, skip, tables, enter, out_types, poles, members):
    rows, channels = wide[0].shape
    count = LANES // members
    blocks = rows // BLOCK
    column = pl.BlockSpec((rows, LANES), lambda j: (0, j))
    lag, gain, mask, leave, alive, across, alive_across = tables
    return pl.pallas_call(
        functools.partial(kernel, count, poles, members, blocks),
        grid=(channels // LANES,),
        in_specs=[column] * len(wide) + [
            pl.BlockSpec((1, LANES), lambda j: (0, j)),
            pl.BlockSpec((count, BLOCK), lambda j: (j, 0)),
            pl.BlockSpec((count * BLOCK, poles), lambda j: (j, 0)),
            pl.BlockSpec((blocks, BLOCK, BLOCK + poles), lambda j: (0, 0, 0)),
            pl.BlockSpec((count * poles, BLOCK), lambda j: (j, 0)),
            pl.BlockSpec((blocks, BLOCK), lambda j: (0, 0)),
            pl.BlockSpec((poles, LANES), lambda j: (0, j)),
            pl.BlockSpec((blocks, LANES), lambda j: (0, 0)),
            pl.BlockSpec((poles, LANES), lambda j: (0, j)),
        ],
        out_specs=[column] * len(out_types),
        out_shape=[jax.ShapeDtypeStruct((rows, channels), kind) for kind in out_types],
        scratch_shapes=[pltpu.VMEM((count * BLOCK, BLOCK + poles), BF16)],
        cost_estimate=pl.CostEstimate(flops=0, bytes_accessed=1 << 20, transcendentals=0),
    )(*wide, skip, lag, gain, mask, leave, alive, across, alive_across, enter)


def swap(value, flip, size):
    return lax.ppermute(value, "ctx", [(i, i ^ flip) for i in range(size)])


def partial_kernel(order_ref, gated_ref, weight_ref, out_ref):
    out_ref[...] = lax.dot_general(
        gated_ref[...], weight_ref[...], (((1,), (1,)), ((), ())), preferred_element_type=F32
    ).astype(BF16)


def partials(order, gated, weights, wide):
    rows, channels = gated.shape
    count = order.shape[0]
    split = 2
    return pl.pallas_call(
        partial_kernel,
        grid_spec=pltpu.PrefetchScalarGridSpec(
            num_scalar_prefetch=1,
            grid=(count, split),
            in_specs=[
                pl.BlockSpec((rows, channels), lambda i, j, order: (0, 0)),
                pl.BlockSpec((wide // split, channels), lambda i, j, order: (order[i] * split + j, 0)),
            ],
            out_specs=pl.BlockSpec((rows, wide // split), lambda i, j, order: (i, j)),
        ),
        out_shape=jax.ShapeDtypeStruct((count * rows, wide), BF16),
        cost_estimate=pl.CostEstimate(flops=0, bytes_accessed=1 << 20, transcendentals=0),
        compiler_params=pltpu.CompilerParams(vmem_limit_bytes=40 << 20),
    )(order, gated, weights)


def tie(value, *earlier):
    return lax.optimization_barrier((value,) + earlier)[0]


MESH = pl.DeviceIdType.MESH


def flipped(me, flip):
    core, x, y = me % 2, me // 2 % 2, me // 4
    core = 1 - core if flip % 2 else core
    x = 1 - x if flip // 2 % 2 else x
    y = 1 - y if flip // 4 else y
    return (y * 2 + x) * 2 + core


def greet(me, z, count):
    barrier = pltpu.get_barrier_semaphore()
    for flip in range(1, 8):
        pl.semaphore_signal(barrier, inc=1, device_id={"ctx": flipped(me, flip)}, device_id_type=MESH)

    @pl.when(z > 0)
    def _():
        pl.semaphore_signal(barrier, inc=1, device_id={"grp": z - 1}, device_id_type=MESH)

    @pl.when(z < count - 1)
    def _():
        pl.semaphore_signal(barrier, inc=1, device_id={"grp": z + 1}, device_id_type=MESH)

    pl.semaphore_wait(barrier, 9 - jnp.where(z == 0, 1, 0) - jnp.where(z == count - 1, 1, 0))


def docs_of(lengths, where):
    start, out = 0, -1
    for i in range(lengths.shape[0]):
        out = out + jnp.where(start <= where, 1, 0)
        start = start + lengths[i]
    return out


def doc_tables(reverse, lengths, me, rows, mask, alive):
    first = me * rows
    shape = (BLOCK, BLOCK)
    down, across = lax.broadcasted_iota(jnp.int32, shape, 0), lax.broadcasted_iota(jnp.int32, shape, 1)
    ordered = down <= across if reverse else down >= across
    crosses = []
    for b in range(rows // BLOCK):
        at = first + b * BLOCK
        entry, left = (at + BLOCK, at) if reverse else (at - 1, at + BLOCK - 1)
        entry, left = docs_of(lengths, entry), docs_of(lengths, left)
        by_row, by_column = docs_of(lengths, at + down), docs_of(lengths, at + across)
        mask[b, :, :LANES] = jnp.where((by_row == by_column) & ordered, 1.0, 0.0).astype(BF16)
        mask[b, :, LANES:] = jnp.where(by_row == entry, 1.0, 0.0).astype(BF16)[:, :mask.shape[2] - LANES]
        alive[b:b + 1, :] = jnp.where(by_column == left, 1.0, 0.0)[:1]
        crosses.append(jnp.where(entry == left, 1.0, 0.0))
    return crosses


def tile_tables(reverse, count, poles, j, rate_col, beta_col, rate, beta, base):
    at = pl.ds(pl.multiple_of(j * LANES, LANES), LANES)
    rates, betas = rate_col[at, :], beta_col[at, :]
    lane = lax.broadcasted_iota(jnp.int32, (LANES, BLOCK), 1)
    lag = lane if reverse else jnp.where(lane == 0, 0, BLOCK - lane)
    response = betas * jnp.exp(-lag.astype(F32) * rates)
    filters = pl.ds(pl.multiple_of(j * count, count), count)
    rate_rows, beta_rows = rate[filters, :], beta[filters, :]
    step = lax.broadcasted_iota(jnp.int32, (BLOCK, poles), 0)
    step = (BLOCK - step if reverse else step + 1).astype(F32)
    for g in range(count):
        row = jnp.sum(response[g * poles:(g + 1) * poles], axis=0, keepdims=True)
        matrix = pltpu.roll(jnp.broadcast_to(row, (BLOCK, LANES)), 0, 1, stride=1, stride_axis=0)
        base[g * BLOCK:(g + 1) * BLOCK, :LANES] = matrix.astype(BF16)
        gain = beta_rows[g:g + 1] * jnp.exp(-step * rate_rows[g:g + 1])
        base[g * BLOCK:(g + 1) * BLOCK, LANES:] = gain.astype(BF16)
    away = lane if reverse else BLOCK - 1 - lane
    return jnp.exp(-away.astype(F32) * rates)


def tile_convolve(reverse, count, poles, members, leave, across, enter, crosses, line_of, emit, mask, alive, base):
    blocks = len(crosses)
    state = enter
    for at in range(blocks):
        b = blocks - 1 - at if reverse else at
        line = line_of(b)
        low = line.astype(BF16)
        left = (base[...].reshape(count, BLOCK, LANES + poles) * mask[b][None]).reshape(
            count * BLOCK, LANES + poles
        )
        right = jnp.concatenate([low, state.astype(BF16)], axis=0)
        emit(b, line, pick(jnp.dot(left, right, preferred_element_type=F32), count, BLOCK, members))
        if at < blocks - 1:
            gone = (leave * alive[b:b + 1, :]).astype(BF16)
            fresh = pick(jnp.dot(gone, low, preferred_element_type=F32), count, poles, members)
            state = across * crosses[b] * state + fresh


def tile_summary(reverse, count, poles, members, lengths, me, rows, rates, line):
    t = lax.broadcasted_iota(jnp.int32, (1, rows), 1)
    edge = me * rows if reverse else me * rows + rows - 1
    kept = jnp.where(docs_of(lengths, me * rows + t) == docs_of(lengths, edge), 1.0, 0.0)
    away = (t if reverse else rows - 1 - t).astype(F32)
    table = (jnp.exp(-away * rates) * kept).astype(BF16)
    return pick(jnp.dot(table, line, preferred_element_type=F32), count, poles, members)


def swap_states(me, states, send, recv):
    copies = [
        pltpu.make_async_remote_copy(
            states.at[0], states.at[flip], send.at[flip], recv.at[flip],
            device_id={"ctx": flipped(me, flip)}, device_id_type=MESH,
        )
        for flip in range(1, 8)
    ]
    for copy in copies:
        copy.start()
    return copies


def entering(reverse, lengths, me, rows, rate_chan, states):
    edge = docs_of(lengths, me * rows + rows if reverse else me * rows - 1)
    total = jnp.zeros(rate_chan.shape, F32)
    for flip in range(1, 8):
        other = flipped(me, flip)
        gap = other - 1 - me if reverse else me - 1 - other
        theirs = docs_of(lengths, other * rows if reverse else other * rows + rows - 1)
        kept = jnp.where((gap >= 0) & (theirs == edge), 1.0, 0.0)
        decay = jnp.exp(-(jnp.maximum(gap, 0) * rows).astype(F32) * rate_chan[...])
        total = total + kept * decay * states[flip].astype(F32)
    return total


def opening_kernel(count, zs, members, lengths, query, key, value, rate_col, beta_col, rate, beta, rate_chan, skip,
                   grad_out, own, lower, upper, whole, filtered, gated, first, base, mask, alive, enter, states,
                   weight, z_send, z_recv, s_send, s_recv, w_send, w_recv, local_sem):
    me, z = lax.axis_index("ctx"), lax.axis_index("grp")
    rows, channels = query.shape
    poles = rate.shape[1]
    tiles = channels // LANES
    height = own.shape[0]
    half = height // 2
    greet(me, z, zs)
    go_up = pltpu.make_async_remote_copy(
        grad_out, lower, z_send.at[0], z_recv.at[0], device_id={"grp": (z + 1) % zs}, device_id_type=MESH
    )
    go_down = pltpu.make_async_remote_copy(
        grad_out, upper, z_send.at[1], z_recv.at[1], device_id={"grp": (z + zs - 1) % zs}, device_id_type=MESH
    )

    @pl.when(z < zs - 1)
    def _():
        go_up.start()

    @pl.when(z > 0)
    def _():
        go_down.start()

    def tile(j):
        return pl.ds(pl.multiple_of(j * LANES, LANES), LANES)

    def product(at, lanes):
        return (key[at, lanes].astype(F32) * value[at, lanes].astype(F32)).astype(BF16)

    def summarize_tile(j, carry):
        states[0, :, tile(j)] = tile_summary(
            False, count, poles, members, lengths, me, rows, rate_col[tile(j), :], product(slice(None), tile(j))
        ).astype(BF16)
        return carry

    lax.fori_loop(0, tiles, summarize_tile, 0)
    state_copies = swap_states(me, states, s_send, s_recv)

    def rows_of(flip, first=0, size=height):
        return pl.ds(pl.multiple_of(flipped(me, flip) * height + first, 16), size)

    def send(number, src, at, flip):
        return pltpu.make_async_remote_copy(
            src, whole.at[at, :], w_send.at[number], w_recv.at[number],
            device_id={"ctx": flipped(me, flip)}, device_id_type=MESH,
        )

    def pass_on(number, at, flip):
        return send(number, whole.at[at, :], at, flip)

    keep_own = pltpu.make_async_copy(own, whole.at[rows_of(0), :], local_sem.at[0])
    keep_own.start()
    by_x, by_y, by_core = send(0, own, rows_of(0), 2), send(1, own, rows_of(0), 4), send(2, own, rows_of(0), 1)
    for copy in (by_x, by_y, by_core):
        copy.start()
    crosses = doc_tables(False, lengths, me, rows, mask, alive)
    for copy in state_copies:
        copy.wait_recv()
    enter[...] = entering(False, lengths, me, rows, rate_chan, states)
    def convolve_tile(j, carry):
        lanes = tile(j)

        def line_of(b):
            return product(pl.ds(b * BLOCK, BLOCK), lanes).astype(F32)

        def emit(b, line, result):
            at = pl.ds(b * BLOCK, BLOCK)
            result = result + skip[:, lanes] * line
            filtered[at, lanes] = result
            gated[at, lanes] = (query[at, lanes].astype(F32) * result).astype(BF16)

        leave = tile_tables(False, count, poles, j, rate_col, beta_col, rate, beta, base)
        across = jnp.exp(-BLOCK * rate_chan[:, lanes])
        tile_convolve(False, count, poles, members, leave, across, enter[:, lanes], crosses, line_of, emit, mask,
                      alive, base)
        return carry

    early = tiles * 3 // 4
    lax.fori_loop(0, early, convolve_tile, 0)
    by_x.wait_recv()
    far_low = pass_on(5, rows_of(2, 0, half), 4)
    far_low.start()
    x_core = pass_on(3, rows_of(2), 1)
    x_core.start()
    by_y.wait_recv()
    far_high = pass_on(6, rows_of(4, half, half), 2)
    far_high.start()
    y_core = pass_on(4, rows_of(4), 1)
    y_core.start()
    lax.fori_loop(early, tiles, convolve_tile, 0)
    far_low.wait_recv()
    low_core = pass_on(7, rows_of(6, 0, half), 1)
    low_core.start()
    far_high.wait_recv()
    high_core = pass_on(8, rows_of(6, half, half), 1)
    high_core.start()
    for copy in (by_core, x_core, y_core, low_core, high_core):
        copy.wait_recv()
    keep_own.wait()
    outermost = jnp.where(z < 2, zs - 1, 0) * (2 * height)
    fetch = pltpu.make_async_copy(
        whole.at[pl.ds(pl.multiple_of(outermost, 16), 2 * height), :], weight, local_sem.at[1]
    )
    fetch.start()
    fetch.wait()
    quarter = rows // 4

    def partial_rows(i, carry):
        at = pl.ds(pl.multiple_of(i * quarter, quarter), quarter)
        first[at, :] = lax.dot_general(
            gated[at, :], weight[...], (((1,), (1,)), ((), ())), preferred_element_type=F32
        ).astype(BF16)
        return carry

    lax.fori_loop(0, 4, partial_rows, 0)
    for copy in state_copies + [by_x, by_y, by_core, far_low, far_high, x_core, y_core, low_core, high_core]:
        copy.wait_send()

    @pl.when(z < zs - 1)
    def _():
        go_up.wait_send()
        go_down.wait_recv()

    @pl.when(z > 0)
    def _():
        go_down.wait_send()
        go_up.wait_recv()


def opening(zs, lengths, query, key, value, rate, beta, skip, grad_out, own, wide):
    rows, channels = query.shape
    filters, poles = rate.shape
    members = channels // filters
    count = LANES // members
    rate_chan = jnp.repeat(rate.T, members, axis=1)
    vmem, anywhere = pl.BlockSpec(memory_space=pltpu.VMEM), pl.BlockSpec(memory_space=pl.ANY)
    moved = jax.ShapeDtypeStruct((rows, channels), BF16)
    dma = pltpu.SemaphoreType.DMA
    return pl.pallas_call(
        functools.partial(opening_kernel, count, zs, members),
        in_specs=[pl.BlockSpec(memory_space=pltpu.SMEM)] + [vmem] * 9 + [anywhere] * 2,
        out_specs=[anywhere] * 3 + [vmem] * 3,
        out_shape=[
            moved, moved, jax.ShapeDtypeStruct((own.shape[0] * 8, channels), BF16),
            jax.ShapeDtypeStruct((rows, channels), F32), moved, jax.ShapeDtypeStruct((rows, wide), BF16),
        ],
        scratch_shapes=[
            pltpu.VMEM((count * BLOCK, BLOCK + poles), BF16),
            pltpu.VMEM((rows // BLOCK, BLOCK, BLOCK + poles), BF16),
            pltpu.VMEM((rows // BLOCK, LANES), F32),
            pltpu.VMEM((poles, channels), F32),
            pltpu.VMEM((8, poles, channels), BF16),
            pltpu.VMEM((wide, channels), BF16),
            dma((2,)), dma((2,)), dma((8,)), dma((8,)), dma((9,)), dma((9,)), dma((2,)),
        ],
        compiler_params=pltpu.CompilerParams(collective_id=1, has_side_effects=True, vmem_limit_bytes=50 << 20),
        cost_estimate=pl.CostEstimate(flops=1 << 34, bytes_accessed=24 << 20, transcendentals=0),
    )(lengths, query, key, value, rate.reshape(-1, 1), beta.reshape(-1, 1), rate, beta, rate_chan, skip, grad_out, own)


SENT = ((3, 3, 0, 0), (2, 2, 1, 1), (1, 0, 3, 2), (0, 1, 2, 3))
GOT = ((0, 1, 2, 3), (1, 0, 3, 2), (2, 2, 1, 1), (3, 3, 0, 0))


def by_place(table, where):
    out = jnp.int32(table[0])
    for i, value in enumerate(table[1:], 1):
        out = jnp.where(where == i, jnp.int32(value), out)
    return out


def middle_kernel(zs, own, gated, lower, upper, first, whole, last, sent_up, sent_down, newest, slope, mine0, mine1,
                  mine2, theirs0, theirs1, theirs2, weights, block, came, second, parts, terms, total, z_send, z_recv,
                  fetch_sem, block_sem, out_sem):
    me, z = lax.axis_index("ctx"), lax.axis_index("grp")
    rows, channels = gated.shape
    wide = weights.shape[1]
    height = wide // 2
    low1, up1, low2, up2 = (came.at[i] for i in range(4))
    greet(me, z, zs)

    def leave_for(way, r, src):
        up = way == 0
        return pltpu.make_async_remote_copy(
            src, came.at[2 * r + way], z_send.at[r, way], z_recv.at[r, way],
            device_id={"grp": (z + 1) % zs if up else (z + zs - 1) % zs}, device_id_type=MESH,
        )

    inner_up, inner_down = (z > 0) & (z < zs - 1), (z > 0) & (z < zs - 1)
    pl.when(z == 0)(leave_for(0, 0, first).start)
    pl.when(inner_up)(leave_for(0, 0, lower).start)
    pl.when(z == zs - 1)(leave_for(1, 0, first).start)
    pl.when(inner_down)(leave_for(1, 0, upper).start)

    fetches = []
    for i, table in enumerate((SENT[1], SENT[2], SENT[3])):
        at = pl.multiple_of(by_place(table, z) * wide, 16)
        fetches.append(pltpu.make_async_copy(whole.at[pl.ds(at, wide), :], weights.at[i], fetch_sem.at[i]))
        fetches[-1].start()

    def take(slot, src):
        return pltpu.make_async_copy(src, block.at[slot], block_sem.at[slot])

    odd = z % 2 == 1
    pl.when(odd)(take(0, lower).start)
    pl.when(jnp.logical_not(odd))(take(0, upper).start)
    pl.when(z == 1)(take(1, upper).start)
    pl.when(z == 2)(take(1, lower).start)
    quarter = rows // 4

    def each_quarter(work):
        def run(i, carry):
            work(pl.ds(pl.multiple_of(i * quarter, quarter), quarter))
            return carry

        lax.fori_loop(0, 4, run, 0)

    def partial(weight, out):
        def work(at):
            out[at, :] = lax.dot_general(
                gated[at, :], weight[...], (((1,), (1,)), ((), ())), preferred_element_type=F32
            ).astype(BF16)
        each_quarter(work)

    copies = []

    def write_out(src, dst):
        copies.append(pltpu.make_async_copy(src, dst, out_sem.at[len(copies)]))
        copies[-1].start()

    def use(number, grads, weight, mine, theirs):
        for side, core, out in ((0, 1 - me % 2, theirs), (1, me % 2, mine)):
            features = pl.ds(pl.multiple_of(core * height, height), height)
            held = terms.at[2 * number + side]

            def columns(i, carry, features=features, held=held):
                at = pl.ds(pl.multiple_of(i * quarter, quarter), quarter)
                held[:, at] = lax.dot_general(
                    grads[:, features], gated[:, at], (((0,), (0,)), ((), ())), preferred_element_type=F32
                ).astype(BF16)
                return carry

            lax.fori_loop(0, channels // quarter, columns, 0)
            write_out(held, out)

        def work(at):
            part = jnp.dot(grads[at, :], weight[...], preferred_element_type=F32)
            total[at, :] = part if number == 0 else total[at, :] + part
        each_quarter(work)

    fetches[0].wait()
    partial(weights.at[0], second)
    fetches[1].wait()
    partial(weights.at[1], parts.at[0])
    fetches[2].wait()
    partial(weights.at[2], parts.at[1])
    write_out(parts.at[1], last)
    use(0, own, weights.at[2], mine0, theirs0)
    take(0, lower).wait()
    use(1, block.at[0], weights.at[1], mine1, theirs1)

    def arrive(r):
        pl.when(z > 0)(leave_for(0, r, lower).wait_recv)
        pl.when(z < zs - 1)(leave_for(1, r, upper).wait_recv)

    def left(r):
        pl.when(z < zs - 1)(leave_for(0, r, lower).wait_send)
        pl.when(z > 0)(leave_for(1, r, upper).wait_send)

    def add_to(arrived, mine):
        def work(at):
            arrived[at, :] = (arrived[at, :].astype(F32) + mine[at, :].astype(F32)).astype(BF16)
        return lambda: each_quarter(work)

    arrive(0)
    left(0)
    load_first = pltpu.make_async_copy(first, parts.at[2], fetch_sem.at[3])
    load_first.start()
    load_first.wait()
    pl.when(z == 1)(add_to(low1, parts.at[2]))
    pl.when(z == 2)(add_to(up1, parts.at[2]))
    pl.when(z == 0)(leave_for(0, 1, second).start)
    pl.when(inner_up)(leave_for(0, 1, low1).start)
    pl.when(z == zs - 1)(leave_for(1, 1, second).start)
    pl.when(inner_down)(leave_for(1, 1, up1).start)
    pl.when(z == 0)(take(1, up1).start)
    pl.when(z == zs - 1)(take(1, low1).start)
    take(1, lower).wait()
    use(2, block.at[1], weights.at[0], mine2, theirs2)
    write_out(total, slope)
    arrive(1)
    left(1)
    third = parts.at[0]
    pl.when(z == 1)(add_to(low2, second))
    pl.when(z == 2)(add_to(low2, third))
    pl.when(z == 1)(add_to(up2, third))
    pl.when(z == 2)(add_to(up2, second))

    def to_next(src, dst, sem):
        return pltpu.make_async_copy(src, dst, block_sem.at[sem])

    pl.when(z == 0)(to_next(third, sent_up, 2).start)
    pl.when(z > 0)(to_next(low2, sent_up, 2).start)
    pl.when(z == zs - 1)(to_next(third, sent_down, 3).start)
    pl.when(z < zs - 1)(to_next(up2, sent_down, 3).start)
    for place, src in enumerate((up2, up1, low1, low2)):
        pl.when(z == place)(to_next(src, newest, 4).start)
    to_next(third, sent_up, 2).wait()
    to_next(third, sent_down, 3).wait()
    to_next(third, newest, 4).wait()
    for copy in copies:
        copy.wait()


def middle(zs, own, gated, lower, upper, first, whole, wide):
    rows, channels = gated.shape
    vmem, anywhere = pl.BlockSpec(memory_space=pltpu.VMEM), pl.BlockSpec(memory_space=pl.ANY)
    moved = jax.ShapeDtypeStruct((rows, channels), BF16)
    half = jax.ShapeDtypeStruct((wide // 2, channels), BF16)
    dma = pltpu.SemaphoreType.DMA
    return pl.pallas_call(
        functools.partial(middle_kernel, zs),
        in_specs=[vmem] * 2 + [anywhere] * 4,
        out_specs=[anywhere] * 11,
        out_shape=[moved] * 4 + [jax.ShapeDtypeStruct((rows, channels), F32)] + [half] * 6,
        scratch_shapes=[
            pltpu.VMEM((3, wide, channels), BF16),
            pltpu.VMEM((2, rows, wide), BF16),
            pltpu.VMEM((4, rows, wide), BF16),
            pltpu.VMEM((rows, wide), BF16),
            pltpu.VMEM((3, rows, wide), BF16),
            pltpu.VMEM((6, wide // 2, channels), BF16),
            pltpu.VMEM((rows, channels), F32),
            dma((2, 2)), dma((2, 2)), dma((4,)), dma((5,)), dma((8,)),
        ],
        compiler_params=pltpu.CompilerParams(collective_id=3, has_side_effects=True, vmem_limit_bytes=56 << 20),
        cost_estimate=pl.CostEstimate(flops=1 << 34, bytes_accessed=24 << 20, transcendentals=0),
    )(own, gated, lower, upper, first, whole)


def closing_kernel(count, zs, members, lengths, query, key, value, rate_col, beta_col, rate, beta, rate_chan, skip,
                   block, gated, slope, filtered, mine0, mine1, mine2, theirs0, theirs1, theirs2, sent_up, sent_down,
                   whole, lower, upper, grad_query, grad_key, grad_value, grad_proj, grad, base, mask, alive, enter,
                   states, weight, theirs3, sums, from_core, near, far, z_send, z_recv, s_send, s_recv, c_send,
                   c_recv, n_send, n_recv, f_send, f_recv, local_sem):
    me, z = lax.axis_index("ctx"), lax.axis_index("grp")
    rows, channels = query.shape
    poles = rate.shape[1]
    tiles = channels // LANES
    height = mine0.shape[0]
    half = channels // 2
    greet(me, z, zs)
    go_up = pltpu.make_async_remote_copy(
        sent_up, lower, z_send.at[0], z_recv.at[0], device_id={"grp": (z + 1) % zs}, device_id_type=MESH
    )
    go_down = pltpu.make_async_remote_copy(
        sent_down, upper, z_send.at[1], z_recv.at[1], device_id={"grp": (z + zs - 1) % zs}, device_id_type=MESH
    )

    @pl.when(z < zs - 1)
    def _():
        go_up.start()

    @pl.when(z > 0)
    def _():
        go_down.start()

    def across_core(number, src):
        copy = pltpu.make_async_remote_copy(
            src, from_core.at[number], c_send.at[number], c_recv.at[number],
            device_id={"ctx": flipped(me, 1)}, device_id_type=MESH,
        )
        copy.start()
        return copy

    core_copies = [across_core(number, src) for number, src in enumerate((theirs0, theirs1, theirs2))]
    newest = by_place(GOT[3], z)
    fetch = pltpu.make_async_copy(
        whole.at[pl.ds(pl.multiple_of(newest * (2 * height), 16), 2 * height), :], weight, local_sem.at[0]
    )
    fetch.start()
    fetch.wait()

    def tile(j):
        return pl.ds(pl.multiple_of(j * LANES, LANES), LANES)

    quarter = rows // 4

    def slope_rows(i, carry):
        at = pl.ds(pl.multiple_of(i * quarter, quarter), quarter)
        grad[at, :] = slope[at, :] + jnp.dot(block[at, :], weight[...], preferred_element_type=F32)
        return carry

    lax.fori_loop(0, 4, slope_rows, 0)

    def summarize_tile(j, carry):
        line = (grad[:, tile(j)] * query[:, tile(j)].astype(F32)).astype(BF16)
        states[0, :, tile(j)] = tile_summary(
            True, count, poles, members, lengths, me, rows, rate_col[tile(j), :], line
        ).astype(BF16)
        return carry

    lax.fori_loop(0, tiles, summarize_tile, 0)
    state_copies = swap_states(me, states, s_send, s_recv)
    span = channels // 4

    def term(core, out):
        features = pl.ds(pl.multiple_of(core * height, height), height)

        def columns(i, carry):
            at = pl.ds(pl.multiple_of(i * span, span), span)
            out[:, at] = lax.dot_general(
                block[:, features], gated[:, at], (((0,), (0,)), ((), ())), preferred_element_type=F32
            ).astype(BF16)
            return carry

        lax.fori_loop(0, 4, columns, 0)

    term(1 - me % 2, theirs3)
    core_copies.append(across_core(3, theirs3))
    term(me % 2, sums.at[3])
    crosses = doc_tables(True, lengths, me, rows, mask, alive)
    x, y = me // 2 % 2, me // 4
    low, high = pl.ds(0, half), pl.ds(half, half)

    def hop_copy(stage, number, columns, flip, sems, into):
        return pltpu.make_async_remote_copy(
            sums.at[number, :, columns], into.at[number, :, columns], sems[0].at[stage, number],
            sems[1].at[stage, number], device_id={"ctx": flipped(me, flip)}, device_id_type=MESH,
        )

    routes = []
    for number, mine in enumerate((mine0, mine1, mine2, None)):
        owner = by_place(GOT[number], z)
        off_x, off_y = owner % 2 != x, owner // 2 != y
        core_copies[number].wait_recv()
        own = sums[number] if mine is None else mine[...]
        sums[number] = (own.astype(F32) + from_core[number].astype(F32)).astype(BF16)
        near_low = hop_copy(0, number, low, 2, (n_send, n_recv), near)
        near_high = hop_copy(1, number, high, 4, (n_send, n_recv), near)
        far_low = hop_copy(0, number, low, 4, (f_send, f_recv), far)
        far_high = hop_copy(1, number, high, 2, (f_send, f_recv), far)
        pl.when(off_x)(near_low.start)
        pl.when(off_y)(near_high.start)
        routes.append((number, off_x, off_y, near_low, near_high, far_low, far_high))

    for copy in state_copies:
        copy.wait_recv()
    enter[...] = entering(True, lengths, me, rows, rate_chan, states)

    def convolve_tile(j, carry):
        lanes = tile(j)

        def line_of(b):
            at = pl.ds(b * BLOCK, BLOCK)
            line = grad[at, lanes]
            grad_query[at, lanes] = (line * filtered[at, lanes]).astype(BF16)
            return line * query[at, lanes].astype(F32)

        def emit(b, line, result):
            at = pl.ds(b * BLOCK, BLOCK)
            result = result + skip[:, lanes] * line
            grad_key[at, lanes] = (result * value[at, lanes].astype(F32)).astype(BF16)
            grad_value[at, lanes] = (result * key[at, lanes].astype(F32)).astype(BF16)

        leave = tile_tables(True, count, poles, j, rate_col, beta_col, rate, beta, base)
        across = jnp.exp(-BLOCK * rate_chan[:, lanes])
        tile_convolve(True, count, poles, members, leave, across, enter[:, lanes], crosses, line_of, emit, mask,
                      alive, base)
        return carry

    early = tiles * 3 // 4
    lax.fori_loop(0, early, convolve_tile, 0)

    def add_near(number, columns, copy):
        def run():
            copy.wait_recv()
            total = sums[number, :, columns].astype(F32) + near[number, :, columns].astype(F32)
            sums[number, :, columns] = total.astype(BF16)
        return run

    for number, off_x, off_y, near_low, near_high, far_low, far_high in routes:
        pl.when(jnp.logical_not(off_x))(add_near(number, low, near_low))
        pl.when(jnp.logical_not(off_y))(add_near(number, high, near_high))
        pl.when(jnp.logical_not(off_x) & off_y)(far_low.start)
        pl.when(jnp.logical_not(off_y) & off_x)(far_high.start)
    lax.fori_loop(early, tiles, convolve_tile, 0)

    def finish(number, far_low, far_high):
        def run():
            far_low.wait_recv()
            far_high.wait_recv()
            grad_proj[...] = sums[number].astype(F32) + far[number].astype(F32)
        return run

    for number, off_x, off_y, near_low, near_high, far_low, far_high in routes:
        on_x, on_y = jnp.logical_not(off_x), jnp.logical_not(off_y)
        pl.when(on_x & on_y)(finish(number, far_low, far_high))
        pl.when(off_x)(near_low.wait_send)
        pl.when(off_y)(near_high.wait_send)
        pl.when(on_x & off_y)(far_low.wait_send)
        pl.when(on_y & off_x)(far_high.wait_send)
    for copy in state_copies + core_copies:
        copy.wait_send()

    @pl.when(z < zs - 1)
    def _():
        go_up.wait_send()
        go_down.wait_recv()

    @pl.when(z > 0)
    def _():
        go_down.wait_send()
        go_up.wait_recv()


def closing(zs, lengths, query, key, value, rate, beta, skip, block, gated, slope, filtered, mine, theirs, sent, whole):
    rows, channels = query.shape
    filters, poles = rate.shape
    members = channels // filters
    count = LANES // members
    height = mine[0].shape[0]
    rate_chan = jnp.repeat(rate.T, members, axis=1)
    vmem, anywhere = pl.BlockSpec(memory_space=pltpu.VMEM), pl.BlockSpec(memory_space=pl.ANY)
    moved = jax.ShapeDtypeStruct((rows, channels), BF16)
    dma = pltpu.SemaphoreType.DMA
    return pl.pallas_call(
        functools.partial(closing_kernel, count, zs, members),
        in_specs=[pl.BlockSpec(memory_space=pltpu.SMEM)] + [vmem] * 16 + [anywhere] * 6,
        out_specs=[anywhere] * 2 + [vmem] * 4,
        out_shape=[moved] * 5 + [jax.ShapeDtypeStruct((height, channels), F32)],
        scratch_shapes=[
            pltpu.VMEM((rows, channels), F32),
            pltpu.VMEM((count * BLOCK, BLOCK + poles), BF16),
            pltpu.VMEM((rows // BLOCK, BLOCK, BLOCK + poles), BF16),
            pltpu.VMEM((rows // BLOCK, LANES), F32),
            pltpu.VMEM((poles, channels), F32),
            pltpu.VMEM((8, poles, channels), BF16),
            pltpu.VMEM((2 * height, channels), BF16),
            pltpu.VMEM((height, channels), BF16),
        ] + [pltpu.VMEM((4, height, channels), BF16)] * 4 + [
            dma((2,)), dma((2,)), dma((8,)), dma((8,)), dma((4,)), dma((4,)), dma((2, 4)), dma((2, 4)), dma((2, 4)),
            dma((2, 4)), dma((1,)),
        ],
        compiler_params=pltpu.CompilerParams(collective_id=2, has_side_effects=True, vmem_limit_bytes=60 << 20),
        cost_estimate=pl.CostEstimate(flops=1 << 34, bytes_accessed=24 << 20, transcendentals=0),
    )(
        lengths, query, key, value, rate.reshape(-1, 1), beta.reshape(-1, 1), rate, beta, rate_chan, skip, block, gated,
        slope, filtered, *mine, *theirs, *sent, whole,
    )


def local(
    query_in, key_in, value_in, residues, decay_time, skip_gain, out_proj, doc_lengths, grad_out
):
    rows, channels = query_in.shape
    filters, poles = residues.shape
    members = channels // filters
    blocks = rows // BLOCK
    size, me = lax.axis_size("ctx"), lax.axis_index("ctx")
    count, z = lax.axis_size("grp"), lax.axis_index("grp")
    assert count == 4
    up = [(i, i + 1) for i in range(count - 1)]
    down = [(i + 1, i) for i in range(count - 1)]

    def exchange(up_value, down_value):
        return lax.ppermute(up_value, "grp", up), lax.ppermute(down_value, "grp", down)

    halves = (slice(0, rows),)
    lower = [[None] * count for _ in halves]
    upper = [[None] * count for _ in halves]
    docs = jnp.arange(doc_lengths.shape[0])
    starts = jnp.sum(jnp.where(docs[None, :] < docs[:, None], doc_lengths[None, :], 0), axis=1)
    flat_ids = doc_index(starts, me * rows + jnp.arange(rows, dtype=jnp.int32))
    ids = flat_ids.reshape(blocks, BLOCK)
    firsts, lasts = ids[:, 0], ids[:, -1]
    before = doc_index(starts, me * rows - 1 + BLOCK * jnp.arange(blocks + 1, dtype=jnp.int32))
    after = doc_index(starts, me * rows + BLOCK * jnp.arange(1, blocks + 1, dtype=jnp.int32))
    ends = doc_index(starts, rows * jnp.arange(1, size + 1, dtype=jnp.int32) - 1)
    opens = doc_index(starts, rows * jnp.arange(size, dtype=jnp.int32))
    rate = 1.0 / decay_time
    beta = residues * jnp.sqrt(-jnp.expm1(-2.0 * rate))
    lags = jnp.arange(BLOCK, dtype=F32)
    rate_chan = jnp.repeat(rate.T, members, axis=1)
    across = jnp.exp(-BLOCK * rate_chan)
    place = jnp.arange(BLOCK)
    causal = place[:, None] >= place[None, :]
    steps = jnp.arange(rows, dtype=F32)

    def mask_of(ids, order, alive):
        same = ids[:, :, None] == ids[:, None, :]
        tail = jnp.broadcast_to(alive[:, :, None], (blocks, BLOCK, poles))
        return jnp.concatenate([same & order[None], tail], axis=2).astype(BF16)

    def spread(flags):
        return jnp.broadcast_to(flags.astype(F32)[:, None], (blocks, LANES))

    def response_of(rate, beta):
        return jnp.sum(beta[:, :, None] * jnp.exp(-lags[None, None, :] * rate[:, :, None]), axis=1)

    def summary_table(rate, distance, kept):
        table = jnp.exp(-distance[None, :] * rate.reshape(-1, 1))
        return (table * kept[None, :]).astype(BF16)

    def gain_of(rate, beta, distance):
        table = beta[:, None, :] * jnp.exp(-distance[None, :, None] * rate[:, None, :])
        return table.reshape(-1, poles).astype(BF16)

    def forward_tables(rate, beta, ids):
        response = response_of(rate, beta)
        mirrored = jnp.concatenate([response[:, :1], response[:, :0:-1]], axis=1)
        return (
            mirrored,
            gain_of(rate, beta, lags + 1.0),
            mask_of(ids, causal, ids == before[:blocks, None]),
            jnp.exp(-(BLOCK - 1.0 - lags)[None, :] * rate.reshape(-1, 1)),
            (ids == lasts[:, None]).astype(F32),
            across,
            spread(before[:blocks] == lasts),
        )

    def backward_tables(rate, beta, ids):
        return (
            response_of(rate, beta),
            gain_of(rate, beta, BLOCK - lags),
            mask_of(ids, causal.T, ids == after[:, None]),
            jnp.exp(-lags[None, :] * rate.reshape(-1, 1)),
            (ids == firsts[:, None]).astype(F32),
            across,
            spread(after == firsts),
        )

    def incoming(state, distance, alive):
        everything = lax.all_gather(state, "ctx").astype(F32)
        gap = jnp.maximum(distance, 0).astype(F32) * rows
        weight = jnp.exp(-gap[:, None, None] * rate_chan[None])
        kept = (alive & (distance >= 0))[:, None, None]
        return jnp.sum(jnp.where(kept, weight * everything, 0.0), axis=0)

    devices = jnp.arange(size, dtype=jnp.int32)
    skip = skip_gain[None, :]
    wide = out_proj.shape[0] * size // count
    order = jnp.stack([by_place(table, z) for table in SENT])

    def forward(query_in, key_in, value_in, out_proj, rate, beta, ids, skip):
        whole_leave = summary_table(rate, rows - 1.0 - steps, flat_ids == flat_ids[-1])
        state = summarize(key_in, value_in, whole_leave, poles, members)
        enter = incoming(state, me - 1 - devices, ends == before[0])
        filtered, gated = run_conv(
            forward_kernel, (query_in, key_in, value_in), skip, forward_tables(rate, beta, ids), enter,
            (F32, BF16), poles, members
        )
        gathered = lax.all_gather(out_proj, "ctx", axis=0, tiled=True)
        return filtered, gated, gathered, partials(order[:1], gated, gathered, wide)

    if size == 8:
        lower[0][0], upper[0][0], gathered, filtered, gated, first = opening(
            count, doc_lengths, query_in, key_in, value_in, rate, beta, skip, grad_out, out_proj, wide
        )
    else:
        lower[0][0], upper[0][0] = exchange(grad_out, grad_out)
        filtered, gated, gathered, first = forward(query_in, key_in, value_in, out_proj, rate, beta, ids, skip)
    odd = z % 2 == 1
    outer = (z == 0) | (z == 3)
    none = jnp.zeros((), BF16)

    if size == 8:
        last, sent_up, sent_down, block, grad_gated, *terms = middle(
            count, grad_out, gated, lower[0][0], upper[0][0], first, gathered, wide
        )
        came_up, came_down, grad_query, grad_key, grad_value, grad_proj = closing(
            count, doc_lengths, query_in, key_in, value_in, rate, beta, skip, block, gated, grad_gated, filtered,
            terms[:3], terms[3:], (sent_up, sent_down), gathered
        )
        came_up, came_down = jnp.where(z == 0, none, came_up), jnp.where(z == count - 1, none, came_down)
        mixed_out = (last.astype(F32) + came_up.astype(F32) + came_down.astype(F32)).astype(BF16)
        return (mixed_out, grad_query, grad_key, grad_value, grad_proj)

    def weights(which):
        return lax.dynamic_slice_in_dim(gathered, which * wide, wide, axis=0)

    def add(came, mine):
        return (came.astype(F32) + mine.astype(F32)).astype(BF16)

    def advance(r, mine_up, mine_down, *earlier):
        out = ()
        for h, part in enumerate(halves):
            *came, _ = lax.optimization_barrier((lower[h][r - 1], upper[h][r - 1], earlier))
            came = jnp.where(z == 0, none, came[0]), jnp.where(z == count - 1, none, came[1])
            sent = lax.optimization_barrier((add(came[0], mine_up(part)), add(came[1], mine_down(part))))
            lower[h][r], upper[h][r] = exchange(*sent)
            out += sent
        return out

    sent = advance(
        1,
        lambda part: jnp.where(z == 0, first[part], none),
        lambda part: jnp.where(z == 3, first[part], none),
        first,
    )
    more = partials(tie(order, *sent)[1:], gated, gathered, wide)
    second, third, last = more[:rows], more[rows:2 * rows], more[2 * rows:]

    def join(sources, r):
        return jnp.concatenate([source[r] for source in sources], axis=0)

    contract = (((0,), (0,)), ((), ()))
    terms = []

    def terms_of(block, owners):
        which = by_place(owners, z)
        terms.append((which, lax.dot_general(block, gated, contract, preferred_element_type=F32).astype(BF16)))
        return terms[-1][1:]

    def slope(block, owners):
        return jnp.dot(block, weights(by_place(owners, z)), preferred_element_type=F32)

    rate_b, beta_b, ids_b, _ = lax.optimization_barrier((rate, beta, ids, more))
    tables_b = backward_tables(rate_b, beta_b, ids_b)
    whole_leave_rev = summary_table(rate_b, steps, flat_ids == flat_ids[0])

    own = tie(grad_out, more, *sent)
    done0 = terms_of(own, GOT[0])
    grad_gated = slope(own, GOT[0])
    came = lax.optimization_barrier((join(lower, 0), join(upper, 0), grad_gated))
    block = jnp.where(odd, came[0], came[1])
    done1 = terms_of(block, GOT[1])
    grad_gated = grad_gated + slope(block, GOT[1])
    sent = advance(
        2,
        lambda part: jnp.where(z == 0, second[part], jnp.where(z == 1, first[part], none)),
        lambda part: jnp.where(z == 3, second[part], jnp.where(z == 2, first[part], none)),
        more, grad_gated, *done0, *done1,
    )
    up0, up1, low0, low1, *_ = lax.optimization_barrier(
        (join(upper, 0), join(upper, 1), join(lower, 0), join(lower, 1), grad_gated, sent)
    )
    block = jnp.where(z < 2, jnp.where(outer, up1, up0), jnp.where(outer, low1, low0))
    done2 = terms_of(block, GOT[2])
    grad_gated = grad_gated + slope(block, GOT[2])
    for_up = jnp.where(z == 1, second, jnp.where(z == 3, none, third))
    for_down = jnp.where(z == 2, second, jnp.where(z == 0, none, third))
    sent = advance(
        3,
        lambda part: jnp.where(z == 1, second[part], jnp.where(z == 3, none, third[part])),
        lambda part: jnp.where(z == 2, second[part], jnp.where(z == 0, none, third[part])),
        grad_gated, terms[0][1], terms[1][1], *done2,
    )
    up1, up2, low1, low2, *_ = lax.optimization_barrier(
        (join(upper, 1), join(upper, 2), join(lower, 1), join(lower, 2), grad_gated, done2, sent)
    )
    block = jnp.where(z < 2, jnp.where(outer, up2, up1), jnp.where(outer, low2, low1))
    done3 = terms_of(block, GOT[3])
    grad_gated = grad_gated + slope(tie(block, *done3), GOT[3])
    term = jnp.zeros((wide * count, channels), BF16)
    for which, value in terms:
        term = lax.dynamic_update_slice(term, value, (which * wide, 0))
    grad_proj = lax.psum_scatter(term, "ctx", scatter_dimension=0, tiled=True).astype(F32)
    state = summarize(grad_gated, query_in, whole_leave_rev, poles, members)
    leaving = incoming(state, devices - 1 - me, opens == after[-1])
    grad_query, grad_key, grad_value = run_conv(
        backward_kernel, (query_in, key_in, value_in, grad_gated, filtered), skip, tables_b,
        leaving, (BF16, BF16, BF16), poles, members
    )
    mixed_out = (last.astype(F32) + join(lower, 3).astype(F32) + join(upper, 3).astype(F32)).astype(BF16)
    return (mixed_out, grad_query, grad_key, grad_value, grad_proj)


def solution(mesh):
    return jax.shard_map(
        local,
        mesh=mesh,
        in_specs=(
            P("ctx", "grp"),
            P("ctx", "grp"),
            P("ctx", "grp"),
            P("grp", None),
            P("grp", None),
            P("grp"),
            P("ctx", "grp"),
            P(),
            P("ctx", "grp"),
        ),
        out_specs=(
            P("ctx", "grp"),
            P("ctx", "grp"),
            P("ctx", "grp"),
            P("ctx", "grp"),
            P("ctx", "grp"),
        ),
        check_vma=False,
    )
```
